512 devices in a mesh: clip: 4 (over y), row: 8 (over x, core), tm: 16 (over z).
Axes of the slice: x: 4, y: 4, z: 16, core: 2. Of those that a mesh axis runs over, the one named last changes fastest.
Arguments:
- clip_input: bfloat16 [4, 32, 16, 48, 192], P('clip', 'tm', 'row'), may hold values from -6 to 6
- out_grad: bfloat16 [4, 64, 16, 48, 192], P('clip', 'tm', 'row'), may hold values from -6 to 6
- weight_one: bfloat16 [3, 3, 3, 192, 192], replicated, may hold values from -0.078125 to 0.078125
- weight_two: bfloat16 [3, 3, 3, 192, 192], replicated, may hold values from -0.078125 to 0.078125
- lengths: int32 [4], P('clip'), may hold values from 2 to 32, as said below
Outputs:
- input_grad: float32 [4, 32, 16, 48, 192], P('clip', 'tm', 'row')
- kernel_grad: float32 [5184, 192], P(('clip', 'tm'), 'row')
The draws below stay inside these ranges and needn't reach their ends.
Inputs may be any that keep to these rules, and one draw needn't show every extreme that they name: `lengths`: every clip has at least 2 frames; one clip has all 32 frames in every draw.
All inputs are finite; a program needn't handle non-finite values.
Results may differ from the reference program's by a relative error of at most 0.0065.
Values may be sent and summed in bfloat16 or wider, within the bound.
No kernel may reach another device: no remote copies, remote signals or barrier semaphores. Data moves between devices by JAX's collectives and lax.ppermute only.
A program may use at most 64 MiB of HBM per device.

```python
import math
import jax
import jax.numpy as jnp
from jax import lax

C = 192
TAPS = 27
FC = 2
WD = 48
CLIPS = 4
FRAMES = 32
ROWS = 16


def draw_lengths(key, part):
    base = jax.random.randint(key, (CLIPS,), FC, FRAMES + 1)
    chosen = jax.random.randint(jax.random.fold_in(key, 17), (), 0, CLIPS)
    return jnp.where(jnp.arange(CLIPS) == chosen, FRAMES, base).astype(jnp.int32)


def shard_levels(key, dims, pieces, least, top_value):
    def one(dim, shards_of):
        draws = jax.random.uniform(jax.random.fold_in(jax.random.fold_in(key, 6), dim), (shards_of,), jnp.float32, least / len(pieces), top_value / len(pieces))
        return jnp.repeat(jnp.exp(draws), dims[dim] // shards_of).reshape((-1,) + (1,) * (len(dims) - dim - 1))

    level = one(*pieces[0])
    for cut in pieces[1:]:
        level = level * one(*cut)
    return level


def normal_values(key, dims, scale, most, cuts=(), kind=jnp.bfloat16):
    array = scale * jax.random.normal(key, dims, jnp.float32)
    if cuts:
        array = array * shard_levels(key, dims, cuts, -0.22, 0.18)
    return jnp.clip(array, -most, most).astype(kind)


def setup_inputs(seed: int = 0) -> dict:
    splits = jax.random.split(jax.random.key(seed), 6)
    return {
        "clip_input": normal_values(splits[0], (CLIPS, FRAMES, ROWS, WD, C), 1.0, 6.0, ((0, 4), (1, 16), (2, 8))),
        "out_grad": normal_values(splits[1], (CLIPS, 2 * FRAMES, ROWS, WD, C), 1.0, 6.0, ((0, 4), (1, 16), (2, 8))),
        "weight_one": normal_values(splits[2], (3, 3, 3, C, C), (TAPS * C) ** -0.5, 0.078125),
        "weight_two": normal_values(splits[3], (3, 3, 3, C, C), (TAPS * C) ** -0.5, 0.078125),
        "lengths": draw_lengths(jax.random.fold_in(splits[5], 71), 0),
    }


def causal_conv(field, kernel, pad_time):
    return lax.conv_general_dilated(field, kernel, (1, 1, 1), [pad_time, (1, 1), (1, 1)], dimension_numbers=('NDHWC', 'DHWIO', 'NDHWC'), preferred_element_type=jnp.float32)

def flipped(kernel):
    return jnp.swapaxes(kernel[:, ::-1, ::-1], 3, 4)

def reference(clip_input, out_grad, weight_one, weight_two, lengths):
    nclip, nframe, nrow, ncol, chan = clip_input.shape
    hidden = causal_conv(clip_input, weight_one[::-1], (2, 0))
    act = jax.nn.silu(hidden).astype(jnp.bfloat16)
    upsampled = jnp.repeat(act, 2, axis=1)
    steps_out = 2 * nframe
    frame_ids = jnp.arange(steps_out, dtype=jnp.int32)
    keep = frame_ids[None, :] < (2 * lengths)[:, None]
    masked = jnp.where(keep[:, :, None, None, None], out_grad, jnp.zeros_like(out_grad))
    padded = jnp.pad(upsampled, ((0, 0), (2, 0), (1, 1), (1, 1), (0, 0)))
    masked_wide = masked.astype(jnp.float32)
    terms = []
    for i in range(3):
        for j in range(3):
            for k in range(3):
                piece = padded[:, 2 - i:2 - i + steps_out, j:j + nrow, k:k + ncol].astype(jnp.float32)
                terms.append(jnp.einsum('bshwc,bshwd->cd', piece, masked_wide))
    scale = 1.0 / math.sqrt(nclip * steps_out * nrow * ncol)
    kernel_grad = jnp.stack(terms).reshape(-1, chan) * scale
    up_grad = causal_conv(masked, flipped(weight_two), (0, 2))
    pair_sum = up_grad.reshape(nclip, nframe, 2, nrow, ncol, chan).sum(axis=2)
    sigma = jax.nn.sigmoid(hidden)
    hidden_grad = (pair_sum * sigma * (1.0 + hidden * (1.0 - sigma))).astype(jnp.bfloat16)
    input_grad = causal_conv(hidden_grad, flipped(weight_one), (0, 2))
    return (input_grad, kernel_grad)
```

```python
import functools
import math

import jax
import jax.numpy as jnp
from jax import lax
from jax.experimental import pallas as pl
from jax.experimental.pallas import tpu as pltpu
from jax.sharding import PartitionSpec as P

BF = jnp.bfloat16
F32 = jnp.float32
EDGE = 16
PITCH = 64
WIDE = 72
VMEM_LIMIT = 56 * 1024 * 1024


def route(sizes, steps):
    total = math.prod(sizes)
    pairs = []
    for source in range(total):
        index, rest = [], source
        for size in reversed(sizes):
            index.append(rest % size)
            rest //= size
        index = index[::-1]
        there = [a + b for a, b in zip(index, steps)]
        if all(0 <= a < size for a, size in zip(there, sizes)):
            target = 0
            for a, size in zip(there, sizes):
                target = target * size + a
            pairs.append((source, target))
    return pairs


def move(value, axes, steps):
    sizes = [lax.axis_size(axis) for axis in axes]
    return lax.ppermute(value, axes if len(axes) > 1 else axes[0], route(sizes, steps))


def spread(ref, index, cols, value):
    ref[index, EDGE : EDGE + cols, :] = value.astype(F32)


def clear_edges(ref, cols):
    blocks, width, chan = ref.shape
    ref[:, 0:EDGE, :] = jnp.zeros((blocks, EDGE, chan), F32)
    ref[:, EDGE + cols :, :] = jnp.zeros((blocks, width - EDGE - cols, chan), F32)


def transposed_dot(a, b):
    return lax.dot_general(a, b, (((1,), (1,)), ((), ())), preferred_element_type=F32)


def first_kernel(
    lengths, x, g, above, below, xprev, gnext, w1, w2,
    pay, hg, hg_top, hg_bot,
    xs, ps, xk, pk,
):
    frames, rows, cols, chan = x.shape
    cells = frames * rows * cols
    peers = pay.shape[0]
    width = chan // peers
    block = lax.axis_index("tm")
    clear_edges(xs, cols)
    clear_edges(ps, cols)
    for f in range(2):
        for r in range(4):
            spread(xs, f * 4 + r, cols, xprev[f, r])
        for r in range(2):
            spread(xs, (2 + f) * 4 + 1 + r, cols, x[f, r])
        spread(xs, (2 + f) * 4, cols, above[f])
        spread(xs, (2 + f) * 4 + 3, cols, below[f])
    for k in range(3):
        xk[k] = xs[:, EDGE - 1 + k : EDGE - 1 + k + cols, :].astype(BF)
    hidden = jnp.zeros((cells, chan), F32)
    for i in range(3):
        for j in range(3):
            for k in range(3):
                part = [xk[k, (f + 2 - i) * 4 + j : (f + 2 - i) * 4 + j + 2] for f in range(2)]
                patch = jnp.concatenate(part, axis=0).reshape(cells, chan)
                hidden += jnp.dot(patch, w1[i * 9 + j * 3 + k], preferred_element_type=F32)
    sigma = 1.0 / (1.0 + jnp.exp(-hidden))
    act = (hidden * sigma).astype(BF)
    limit = 2 * lengths[0] - 2 * frames * block

    def cotangent(f, r):
        if f >= 2 * frames:
            value = gnext[f - 2 * frames, r]
        elif r == 0:
            value = above[frames + f]
        elif r == 3:
            value = below[frames + f]
        else:
            value = g[f, r - 1]
        value = value.astype(F32)
        return jnp.where(f < limit, value, jnp.zeros_like(value))

    for r in range(4):
        field = [cotangent(f, r) for f in range(6)]
        for a in range(5):
            spread(ps, a * 4 + r, cols, field[a] + field[a + 1])
    for k in range(3):
        pk[k] = ps[:, EDGE + 1 - k : EDGE + 1 - k + cols, :].astype(BF)
    pair = jnp.zeros((cells, chan), F32)
    for i in range(3):
        for j in range(3):
            for k in range(3):
                part = [pk[k, (2 * t + i) * 4 + 2 - j : (2 * t + i) * 4 + 4 - j] for t in range(2)]
                patch = jnp.concatenate(part, axis=0).reshape(cells, chan)
                pair += transposed_dot(patch, w2[i * 9 + j * 3 + k])
    grad = (pair * sigma * (1.0 + hidden * (1.0 - sigma))).astype(BF)
    grad = grad.reshape(frames, rows, cols, chan)
    hg[...] = grad
    hg_top[...] = grad[:, 0]
    hg_bot[...] = grad[:, 1]
    half = cells // 2
    wide = act.astype(F32)
    low = wide[:, :128].astype(BF)
    high = jnp.concatenate([wide[:half, 128:], wide[half:, 128:]], axis=1).astype(BF)
    turned = [
        jnp.transpose(ps[a * 4 + 1 : a * 4 + 3, 0:PITCH, :].reshape(2 * PITCH, chan))
        for a in range(5)
    ]
    for p in range(peers):
        pay[p, 0:cells, :] = low
        pay[p, cells : cells + half, :] = high
        mine = jnp.concatenate([v[p * width : (p + 1) * width] for v in turned], axis=0)
        pay[p, cells + half :, :] = mine.astype(BF)


def second_kernel(got, out, field, left, prod):
    peers = got.shape[0]
    cells = field.shape[0] // peers // (4 * PITCH) * 192
    half = cells // 2
    chan = field.shape[1]
    width = chan // peers
    cols = 48
    blocks, _, lanes = out.shape
    span = 27 * chan // blocks
    field[...] = jnp.zeros(field.shape, BF)
    low_lane = lax.broadcasted_iota(jnp.int32, (width, 128), 1) < PITCH
    for q in range(peers):
        low = got[q, 0:cells, :]
        high = got[q, cells : cells + half, :].astype(F32)
        high = [high[:, 0:64].astype(BF), high[:, 64:128].astype(BF)]
        for t in range(2):
            for r in range(2):
                at = ((t * peers + q) * 2 + r) * PITCH + EDGE
                field[at : at + cols, 0:128] = low[(t * 2 + r) * cols : (t * 2 + r + 1) * cols]
                field[at : at + cols, 128:192] = high[t][r * cols : (r + 1) * cols]
    base = cells + half
    for a in range(5):
        plain = [
            got[q, base + a * width : base + (a + 1) * width, :].astype(F32) for q in range(peers)
        ]
        swapped = [pltpu.roll(v, PITCH, 1) for v in plain]
        zero = jnp.zeros((width, 128), F32)
        ring = [zero] + swapped + [zero]
        for q in range(peers):
            rows_of = [
                jnp.where(low_lane, ring[q + 1], ring[q + 2]),
                plain[q],
                jnp.where(low_lane, ring[q], ring[q + 1]),
            ]
            for j in range(3):
                for k in range(3):
                    value = rows_of[j]
                    if k != 1:
                        value = pltpu.roll(value, 127 if k == 0 else 1, 1)
                    for t in range(2):
                        i = a - 2 * t
                        if 0 <= i < 3:
                            tap = i * 9 + j * 3 + k
                            at = (t * peers + q) * 128
                            left[tap * width : (tap + 1) * width, at : at + 128] = value
    prod[:, 192:256] = jnp.zeros((prod.shape[0], 64), F32)
    for i in range(3):
        rows = slice(i * 9 * width, (i + 1) * 9 * width)
        prod[rows, 0:192] = jnp.dot(
            left[rows, :].astype(BF), field[...], preferred_element_type=F32
        )
    lane = lax.broadcasted_iota(jnp.int32, (width, 256), 1)
    for b in range(blocks):
        pieces = []
        done = 0
        while done < span:
            tap, start = divmod(b * span + done, chan)
            size = min(span - done, chan - start)
            pieces.append((tap, start, size, done))
            done += size
        for chunk in range(0, lanes, 128):
            value = None
            for tap, start, size, at in pieces:
                if at + size <= chunk or at >= chunk + 128:
                    continue
                shift = (at - chunk - start) % 256
                part = prod[tap * width : (tap + 1) * width, :]
                if shift:
                    part = pltpu.roll(part, shift, 1)
                part = part[:, :128]
                if value is None:
                    value = part
                else:
                    value = jnp.where(lane[:, :128] < at - chunk, value, part)
            if value is None:
                value = jnp.zeros((width, 128), F32)
            out[b, :, chunk : chunk + 128] = value.astype(BF)


def clip_kernel(got, out):
    total = got[0].astype(F32)
    for p in range(1, got.shape[0]):
        total += got[p].astype(F32)
    out[...] = total.astype(BF)


def last_kernel(scale, got, out):
    total = got[0].astype(F32)
    for p in range(1, got.shape[0]):
        total += got[p].astype(F32)
    out[...] = jnp.transpose(total * scale)[: out.shape[0], :]


def grad_kernel(hg, top, bot, nxt, nxt_top, nxt_bot, w1, out, hs, hk):
    frames, rows, cols, chan = hg.shape
    cells = frames * rows * cols
    clear_edges(hs, cols)
    for f in range(2):
        spread(hs, f * 4, cols, top[f])
        spread(hs, f * 4 + 3, cols, bot[f])
        spread(hs, (2 + f) * 4, cols, nxt_top[f])
        spread(hs, (2 + f) * 4 + 3, cols, nxt_bot[f])
        for r in range(2):
            spread(hs, f * 4 + 1 + r, cols, hg[f, r])
            spread(hs, (2 + f) * 4 + 1 + r, cols, nxt[f, r])
    for k in range(3):
        hk[k] = hs[:, EDGE + 1 - k : EDGE + 1 - k + cols, :].astype(BF)
    total = jnp.zeros((cells, chan), F32)
    for i in range(3):
        for j in range(3):
            for k in range(3):
                part = [hk[k, (f + i) * 4 + 2 - j : (f + i) * 4 + 4 - j] for f in range(2)]
                patch = jnp.concatenate(part, axis=0).reshape(cells, chan)
                total += transposed_dot(patch, w1[i * 9 + j * 3 + k])
    out[...] = total.reshape(frames, rows, cols, chan)


def in_vmem(count):
    return [pl.BlockSpec(memory_space=pltpu.VMEM)] * count


def call(body, name, shapes, args, scratch, scalars=()):
    specs = [pl.BlockSpec(memory_space=pltpu.SMEM)] * len(scalars) + in_vmem(len(args))
    outs = [jax.ShapeDtypeStruct(shape, kind) for shape, kind in shapes]
    return pl.pallas_call(
        body,
        name=name,
        out_shape=outs,
        in_specs=specs,
        out_specs=in_vmem(len(outs)),
        scratch_shapes=[pltpu.VMEM(shape, kind) for shape, kind in scratch],
        compiler_params=pltpu.CompilerParams(vmem_limit_bytes=VMEM_LIMIT),
    )(*scalars, *args)


def local(clip_input, out_grad, weight_one, weight_two, lengths):
    frames, rows, cols, chan = clip_input.shape[1:]
    cells = frames * rows * cols
    peers = lax.axis_size("row")
    clips = lax.axis_size("clip")
    steps = lax.axis_size("tm")
    width = chan // peers
    x = clip_input[0]
    g = out_grad[0]
    w1 = weight_one.reshape(27, chan, chan)
    w2 = weight_two.reshape(27, chan, chan)

    top = jnp.concatenate([x[:, 0], g[:, 0]], axis=0)
    bot = jnp.concatenate([x[:, 1], g[:, 1]], axis=0)
    above = move(bot, ("row",), (1,))
    below = move(top, ("row",), (-1,))
    x_tall = jnp.stack([above[:2], x[:, 0], x[:, 1], below[:2]], axis=1)
    g_tall = jnp.stack([above[2:4], g[:2, 0], g[:2, 1], below[2:4]], axis=1)
    xprev = move(x_tall, ("tm",), (1,))
    gnext = move(g_tall, ("tm",), (-1,))

    edge = (frames, cols, chan)
    pay, hg, hg_top, hg_bot = call(
        first_kernel,
        "hidden_and_pairs",
        [
            ((peers, cells + cells // 2 + 5 * width, 128), BF),
            ((frames, rows, cols, chan), BF),
            (edge, BF),
            (edge, BF),
        ],
        (x, g, above, below, xprev, gnext, w1, w2),
        [
            ((16, WIDE, chan), F32),
            ((20, WIDE, chan), F32),
            ((3, 16, cols, chan), BF),
            ((3, 20, cols, chan), BF),
        ],
        scalars=(lengths,),
    )
    got = lax.all_to_all(pay, "row", 0, 0)
    above_h = move(hg_bot, ("row",), (1,))
    below_h = move(hg_top, ("row",), (-1,))
    next_h = move(hg, ("tm",), (-1,))
    next_above = move(hg_bot, ("row", "tm"), (1, -1))
    next_below = move(hg_top, ("row", "tm"), (-1, -1))

    blocks = clips * steps
    span = 27 * chan // blocks
    lanes = (span + 127) // 128 * 128
    (part,) = call(
        second_kernel,
        "kernel_grad_part",
        [((blocks, width, lanes), BF)],
        (got,),
        [
            ((2 * peers * 2 * PITCH, chan), BF),
            ((27 * width, 2 * peers * 128), F32),
            ((27 * width, 256), F32),
        ],
    )
    by_clip = lax.all_to_all(part.reshape(clips, steps * width, lanes), "clip", 0, 0)
    (summed,) = call(clip_kernel, "clip_sum", [((steps * width, lanes), BF)], (by_clip,), [])
    by_step = lax.all_to_all(summed.reshape(steps, width, lanes), "tm", 0, 0)
    total = clips * 2 * frames * steps * rows * peers * cols
    (kernel_grad,) = call(
        functools.partial(last_kernel, 1.0 / math.sqrt(total)),
        "kernel_grad_sum",
        [((span, width), F32)],
        (by_step,),
        [],
    )
    (input_grad,) = call(
        grad_kernel,
        "input_grad",
        [((frames, rows, cols, chan), F32)],
        (hg, above_h, below_h, next_h, next_above, next_below, w1),
        [((16, WIDE, chan), F32), ((3, 16, cols, chan), BF)],
    )
    return (input_grad[None], kernel_grad)


def solution(mesh):
    return jax.shard_map(
        local,
        mesh=mesh,
        in_specs=(
            P("clip", "tm", "row", None, None),
            P("clip", "tm", "row", None, None),
            P(),
            P(),
            P("clip"),
        ),
        out_specs=(P("clip", "tm", "row", None, None), P(("clip", "tm"), "row")),
        check_vma=False,
    )
```

```python
import functools
import math

import jax
import jax.numpy as jnp
from jax import lax
from jax.experimental import pallas as pl
from jax.experimental.pallas import tpu as pltpu
from jax.sharding import PartitionSpec as P

BF = jnp.bfloat16
F32 = jnp.float32
EDGE = 16
PITCH = 64
WIDE = 72
MIB = 1024 * 1024


def route(sizes, steps):
    total = math.prod(sizes)
    pairs = []
    for source in range(total):
        index, rest = [], source
        for size in reversed(sizes):
            index.append(rest % size)
            rest //= size
        index = index[::-1]
        there = [a + b for a, b in zip(index, steps)]
        if all(0 <= a < size for a, size in zip(there, sizes)):
            target = 0
            for a, size in zip(there, sizes):
                target = target * size + a
            pairs.append((source, target))
    return pairs


def move(value, axes, steps):
    sizes = [lax.axis_size(axis) for axis in axes]
    return lax.ppermute(value, axes if len(axes) > 1 else axes[0], route(sizes, steps))


def spread(ref, index, cols, value):
    ref[index, EDGE : EDGE + cols, :] = value.astype(F32)


def clear_edges(ref, cols):
    blocks, width, chan = ref.shape
    ref[:, 0:EDGE, :] = jnp.zeros((blocks, EDGE, chan), F32)
    ref[:, EDGE + cols :, :] = jnp.zeros((blocks, width - EDGE - cols, chan), F32)


def transposed_dot(a, b):
    return lax.dot_general(a, b, (((1,), (1,)), ((), ())), preferred_element_type=F32)


def edges_kernel(x, g, xprev, gnext, top, bot, sem):
    nx, ng = x.shape[0], g.shape[0]
    copies = []
    for row, out in ((0, top), (1, bot)):
        for source, at in ((x, 0), (g, 2 * nx)):
            target = out.at[at : at + source.shape[0]]
            copies.append(pltpu.make_async_copy(source.at[:, row], target, sem.at[len(copies)]))
    for copy in copies:
        copy.start()
    for row, out in ((0, top), (1, bot)):
        for f in range(nx):
            out[nx + f] = xprev[f, row]
            out[2 * nx + ng + f] = gnext[f, row]
    for copy in copies:
        copy.wait()


def packed(width, span):
    return (width, span) == (24, 81)


def first_kernel(
    lengths, x_far, g_far, w1_far, w2_far, above, below, xprev, gnext,
    pay, hg, hg_top, hg_bot,
    xs, ps, xk, pk, x, g, w1, w2, sem,
):
    pairs = ((x_far, x), (w1_far, w1), (g_far, g), (w2_far, w2))
    copies = [pltpu.make_async_copy(a, b, sem.at[n]) for n, (a, b) in enumerate(pairs)]
    for copy in copies:
        copy.start()
    frames, rows, cols, chan = x.shape
    cells = frames * rows * cols
    peers = pay.shape[0]
    width = chan // peers
    block = lax.axis_index("tm")
    clear_edges(xs, cols)
    clear_edges(ps, cols)
    copies[0].wait()
    for f in range(2):
        for r in range(2):
            spread(xs, f * 4 + 1 + r, cols, xprev[f, r])
            spread(xs, (2 + f) * 4 + 1 + r, cols, x[f, r])
        spread(xs, f * 4, cols, above[2 + f])
        spread(xs, f * 4 + 3, cols, below[2 + f])
        spread(xs, (2 + f) * 4, cols, above[f])
        spread(xs, (2 + f) * 4 + 3, cols, below[f])
    for k in range(3):
        xk[k] = xs[:, EDGE - 1 + k : EDGE - 1 + k + cols, :].astype(BF)
    copies[1].wait()
    hidden = jnp.zeros((cells, chan), F32)
    for i in range(3):
        for j in range(3):
            for k in range(3):
                part = [xk[k, (f + 2 - i) * 4 + j : (f + 2 - i) * 4 + j + 2] for f in range(2)]
                patch = jnp.concatenate(part, axis=0).reshape(cells, chan)
                hidden += jnp.dot(patch, w1[i * 9 + j * 3 + k], preferred_element_type=F32)
    sigma = 1.0 / (1.0 + jnp.exp(-hidden))
    act = (hidden * sigma).astype(BF)
    limit = 2 * lengths[0] - 2 * frames * block

    def cotangent(f, r):
        if r == 0:
            value = above[2 * frames + f]
        elif r == 3:
            value = below[2 * frames + f]
        elif f >= 2 * frames:
            value = gnext[f - 2 * frames, r - 1]
        else:
            value = g[f, r - 1]
        value = value.astype(F32)
        return jnp.where(f < limit, value, jnp.zeros_like(value))

    copies[2].wait()
    for r in range(4):
        field = [cotangent(f, r) for f in range(6)]
        for a in range(5):
            spread(ps, a * 4 + r, cols, field[a] + field[a + 1])
    for k in range(3):
        pk[k] = ps[:, EDGE + 1 - k : EDGE + 1 - k + cols, :].astype(BF)
    copies[3].wait()
    pair = jnp.zeros((cells, chan), F32)
    for i in range(3):
        for j in range(3):
            for k in range(3):
                part = [pk[k, (2 * t + i) * 4 + 2 - j : (2 * t + i) * 4 + 4 - j] for t in range(2)]
                patch = jnp.concatenate(part, axis=0).reshape(cells, chan)
                pair += transposed_dot(patch, w2[i * 9 + j * 3 + k])
    grad = (pair * sigma * (1.0 + hidden * (1.0 - sigma))).astype(BF)
    grad = grad.reshape(frames, rows, cols, chan)
    hg[...] = grad
    hg_top[...] = grad[:, 0]
    hg_bot[...] = grad[:, 1]
    half = cells // 2
    wide = act.astype(F32)
    low = wide[:, :128].astype(BF)
    high = jnp.concatenate([wide[:half, 128:], wide[half:, 128:]], axis=1).astype(BF)
    turned = [
        jnp.transpose(ps[a * 4 + 1 : a * 4 + 3, 0:PITCH, :].reshape(2 * PITCH, chan))
        for a in range(5)
    ]
    for p in range(peers):
        pay[p, 0:cells, :] = low
        pay[p, cells : cells + half, :] = high
        mine = jnp.concatenate([v[p * width : (p + 1) * width] for v in turned], axis=0)
        pay[p, cells + half :, :] = mine.astype(BF)


def tall_kernel(hg, above, below, tall):
    tall[:, 0] = above[...]
    tall[:, 1] = hg[:, 0]
    tall[:, 2] = hg[:, 1]
    tall[:, 3] = below[...]


def second_kernel(span, got, out, field, left, prod):
    peers = got.shape[0]
    cells = field.shape[0] // peers // (4 * PITCH) * 192
    half = cells // 2
    chan = field.shape[1]
    width = chan // peers
    cols = 48
    blocks, _, lanes = out.shape
    field[...] = jnp.zeros(field.shape, BF)
    low_lane = lax.broadcasted_iota(jnp.int32, (width, 128), 1) < PITCH
    for q in range(peers):
        low = got[q, 0:cells, :]
        high = got[q, cells : cells + half, :].astype(F32)
        high = [high[:, 0:64].astype(BF), high[:, 64:128].astype(BF)]
        for t in range(2):
            for r in range(2):
                at = ((t * peers + q) * 2 + r) * PITCH + EDGE
                field[at : at + cols, 0:128] = low[(t * 2 + r) * cols : (t * 2 + r + 1) * cols]
                field[at : at + cols, 128:192] = high[t][r * cols : (r + 1) * cols]
    base = cells + half
    for a in range(5):
        plain = [
            got[q, base + a * width : base + (a + 1) * width, :].astype(F32) for q in range(peers)
        ]
        swapped = [pltpu.roll(v, PITCH, 1) for v in plain]
        zero = jnp.zeros((width, 128), F32)
        ring = [zero] + swapped + [zero]
        for q in range(peers):
            rows_of = [
                jnp.where(low_lane, ring[q + 1], ring[q + 2]),
                plain[q],
                jnp.where(low_lane, ring[q], ring[q + 1]),
            ]
            for j in range(3):
                for k in range(3):
                    value = rows_of[j]
                    if k != 1:
                        value = pltpu.roll(value, 127 if k == 0 else 1, 1)
                    for t in range(2):
                        i = a - 2 * t
                        if 0 <= i < 3:
                            tap = i * 9 + j * 3 + k
                            at = (t * peers + q) * 128
                            left[tap * width : (tap + 1) * width, at : at + 128] = value
    prod[:, 192:256] = jnp.zeros((prod.shape[0], 64), F32)
    for i in range(3):
        rows = slice(i * 9 * width, (i + 1) * 9 * width)
        prod[rows, 0:192] = jnp.dot(
            left[rows, :].astype(BF), field[...], preferred_element_type=F32
        )
    lane = lax.broadcasted_iota(jnp.int32, (width, 256), 1)
    for b in range(blocks):
        pieces = []
        done = 0
        while done < span:
            tap, start = divmod(b * span + done, chan)
            size = min(span - done, chan - start)
            pieces.append((tap, start, size, done))
            done += size
        for chunk in range(0, lanes, 128):
            value = None
            for tap, start, size, at in pieces:
                if at + size <= chunk or at >= chunk + 128:
                    continue
                shift = (at - chunk - start) % 256
                part = prod[tap * width : (tap + 1) * width, :]
                if shift:
                    part = pltpu.roll(part, shift, 1)
                part = part[:, :128]
                if value is None:
                    value = part
                else:
                    value = jnp.where(lane[:, :128] < at - chunk, value, part)
            if value is None:
                value = jnp.zeros((width, 128), F32)
            if packed(width, span):
                tail = value[16:24]
                tail = jnp.concatenate([pltpu.roll(tail, 81, 1), pltpu.roll(tail, 40, 1)], axis=0)
                value = jnp.where(lane[:16, :128] < span, value[:16], tail)
            out[b, :, chunk : chunk + 128] = value.astype(BF)


def clip_kernel(got, out):
    total = got[0].astype(F32)
    for p in range(1, got.shape[0]):
        total += got[p].astype(F32)
    out[...] = total.astype(BF)


def last_kernel(scale, w1_far, got, tall, after, out, grad, hs, hk, w1, sem):
    copy = pltpu.make_async_copy(w1_far, w1, sem.at[0])
    copy.start()
    width, span = out.shape
    total = got[0].astype(F32)
    for p in range(1, got.shape[0]):
        total += got[p].astype(F32)
    total = total * scale
    if packed(width, span):
        lane = lax.broadcasted_iota(jnp.int32, (8, 128), 1)
        tail = jnp.where(lane < 41, pltpu.roll(total[:8], 47, 1), pltpu.roll(total[8:], 88, 1))
        out[:16] = total[:, :span]
        out[16:] = tail[:, :span]
    else:
        out[...] = total[:, :span]
    frames, rows, cols, chan = grad.shape
    cells = frames * rows * cols
    clear_edges(hs, cols)
    for f in range(2):
        for r in range(4):
            spread(hs, f * 4 + r, cols, tall[f, r])
            spread(hs, (2 + f) * 4 + r, cols, after[f, r])
    for k in range(3):
        hk[k] = hs[:, EDGE + 1 - k : EDGE + 1 - k + cols, :].astype(BF)
    copy.wait()
    acc = jnp.zeros((cells, chan), F32)
    for i in range(3):
        for j in range(3):
            for k in range(3):
                part = [hk[k, (f + i) * 4 + 2 - j : (f + i) * 4 + 4 - j] for f in range(2)]
                patch = jnp.concatenate(part, axis=0).reshape(cells, chan)
                acc += transposed_dot(patch, w1[i * 9 + j * 3 + k])
    grad[...] = acc.reshape(frames, rows, cols, chan)


def call(body, name, limit, shapes, args, scratch, far=(), scalars=(), sems=0):
    spaces = [pltpu.SMEM] * len(scalars) + [pltpu.HBM] * len(far) + [pltpu.VMEM] * len(args)
    far = [pltpu.with_memory_space_constraint(value, pltpu.HBM) for value in far]
    outs = [jax.ShapeDtypeStruct(shape, kind) for shape, kind in shapes]
    buffers = [pltpu.VMEM(shape, kind) for shape, kind in scratch]
    if sems:
        buffers.append(pltpu.SemaphoreType.DMA((sems,)))
    return pl.pallas_call(
        body,
        name=name,
        out_shape=outs,
        in_specs=[pl.BlockSpec(memory_space=space) for space in spaces],
        out_specs=[pl.BlockSpec(memory_space=pltpu.VMEM)] * len(outs),
        scratch_shapes=buffers,
        compiler_params=pltpu.CompilerParams(vmem_limit_bytes=limit * MIB),
    )(*scalars, *far, *args)


def local(clip_input, out_grad, weight_one, weight_two, lengths):
    frames, rows, cols, chan = clip_input.shape[1:]
    cells = frames * rows * cols
    peers = lax.axis_size("row")
    clips = lax.axis_size("clip")
    steps = lax.axis_size("tm")
    width = chan // peers
    x = clip_input[0]
    g = out_grad[0]
    w1 = weight_one.reshape(27, chan, chan)
    w2 = weight_two.reshape(27, chan, chan)

    xprev = move(x, ("tm",), (1,))
    gnext = move(g[:frames], ("tm",), (-1,))
    band = (5 * frames, cols, chan)
    top, bot = call(
        edges_kernel,
        "edge_rows",
        4,
        [(band, BF), (band, BF)],
        (xprev, gnext),
        [],
        far=(x, g),
        sems=4,
    )
    above = move(bot, ("row",), (1,))
    below = move(top, ("row",), (-1,))

    edge = (frames, cols, chan)
    pay, hg, hg_top, hg_bot = call(
        first_kernel,
        "hidden_and_pairs",
        20,
        [
            ((peers, cells + cells // 2 + 5 * width, 128), BF),
            ((frames, rows, cols, chan), BF),
            (edge, BF),
            (edge, BF),
        ],
        (above, below, xprev, gnext),
        [
            ((16, WIDE, chan), F32),
            ((20, WIDE, chan), F32),
            ((3, 16, cols, chan), BF),
            ((3, 20, cols, chan), BF),
            (x.shape, BF),
            (g.shape, BF),
            (w1.shape, BF),
            (w2.shape, BF),
        ],
        far=(x, g, w1, w2),
        scalars=(lengths,),
        sems=4,
    )
    above_h = move(hg_bot, ("row",), (1,))
    below_h = move(hg_top, ("row",), (-1,))
    pay, above_h, below_h = lax.optimization_barrier((pay, above_h, below_h))
    got = lax.all_to_all(pay, "row", 0, 0)
    got, hg, above_h, below_h = lax.optimization_barrier((got, hg, above_h, below_h))
    (tall,) = call(
        tall_kernel,
        "tall_band",
        4,
        [((frames, rows + 2, cols, chan), BF)],
        (hg, above_h, below_h),
        [],
    )
    after = move(tall, ("tm",), (-1,))

    blocks = clips * steps
    span = 27 * chan // blocks
    shape = (16, 128) if packed(width, span) else (width, (span + 127) // 128 * 128)
    (part,) = call(
        functools.partial(second_kernel, span),
        "kernel_grad_part",
        16,
        [((blocks,) + shape, BF)],
        (got,),
        [
            ((2 * peers * 2 * PITCH, chan), BF),
            ((27 * width, 2 * peers * 128), F32),
            ((27 * width, 256), F32),
        ],
    )
    part, after = lax.optimization_barrier((part, after))
    by_clip = lax.all_to_all(part.reshape((clips, steps * shape[0], shape[1])), "clip", 0, 0)
    (summed,) = call(
        clip_kernel,
        "clip_sum",
        4,
        [((steps * shape[0], shape[1]), BF)],
        (by_clip,),
        [],
    )
    by_step = lax.all_to_all(summed.reshape((steps,) + shape), "tm", 0, 0)
    total = clips * 2 * frames * steps * rows * peers * cols
    kernel_grad, input_grad = call(
        functools.partial(last_kernel, 1.0 / math.sqrt(total)),
        "both_grads",
        16,
        [((width, span), F32), ((frames, rows, cols, chan), F32)],
        (by_step, tall, after),
        [((16, WIDE, chan), F32), ((3, 16, cols, chan), BF), (w1.shape, BF)],
        far=(w1,),
        sems=1,
    )
    return (input_grad[None], kernel_grad.T)


def solution(mesh):
    return jax.shard_map(
        local,
        mesh=mesh,
        in_specs=(
            P("clip", "tm", "row", None, None),
            P("clip", "tm", "row", None, None),
            P(),
            P(),
            P("clip"),
        ),
        out_specs=(P("clip", "tm", "row", None, None), P(("clip", "tm"), "row")),
        check_vma=False,
    )
```

```python
import functools
import math

import jax
import jax.numpy as jnp
from jax import lax
from jax.experimental import pallas as pl
from jax.experimental.pallas import tpu as pltpu
from jax.sharding import PartitionSpec as P

BF = jnp.bfloat16
F32 = jnp.float32
EDGE = 16
PITCH = 64
WIDE = 72
MIB = 1024 * 1024


def route(sizes, steps):
    total = math.prod(sizes)
    pairs = []
    for source in range(total):
        index, rest = [], source
        for size in reversed(sizes):
            index.append(rest % size)
            rest //= size
        index = index[::-1]
        there = [a + b for a, b in zip(index, steps)]
        if all(0 <= a < size for a, size in zip(there, sizes)):
            target = 0
            for a, size in zip(there, sizes):
                target = target * size + a
            pairs.append((source, target))
    return pairs


def move(value, axes, steps):
    sizes = [lax.axis_size(axis) for axis in axes]
    return lax.ppermute(value, axes if len(axes) > 1 else axes[0], route(sizes, steps))


def spread(ref, index, cols, value):
    ref[index, EDGE : EDGE + cols, :] = value.astype(F32)


def clear_edges(ref, cols):
    blocks, width, chan = ref.shape
    ref[:, 0:EDGE, :] = jnp.zeros((blocks, EDGE, chan), F32)
    ref[:, EDGE + cols :, :] = jnp.zeros((blocks, width - EDGE - cols, chan), F32)


def transposed_dot(a, b):
    return lax.dot_general(a, b, (((1,), (1,)), ((), ())), preferred_element_type=F32)


def band_kernel(x, g, xprev, gnext, band, sem):
    nx, ng = x.shape[0], g.shape[0]
    copies = [
        pltpu.make_async_copy(x, band.at[0:nx], sem.at[0]),
        pltpu.make_async_copy(g, band.at[2 * nx : 2 * nx + ng], sem.at[1]),
    ]
    for copy in copies:
        copy.start()
    band[nx : 2 * nx] = xprev[...]
    band[2 * nx + ng :] = gnext[...]
    for copy in copies:
        copy.wait()


def packed(width, span):
    return (width, span) == (24, 81)


def first_kernel(
    lengths, x_far, g_far, w1_far, w2_far, above, below, xprev, gnext,
    pay, tall,
    xs, ps, xk, pk, x, g, w1, w2, sem,
):
    pairs = ((x_far, x), (w1_far, w1), (g_far, g), (w2_far, w2))
    copies = [pltpu.make_async_copy(a, b, sem.at[n]) for n, (a, b) in enumerate(pairs)]
    for copy in copies:
        copy.start()
    frames, rows, cols, chan = x.shape
    cells = frames * rows * cols
    reach = 2 * cells
    peers = pay.shape[0]
    width = chan // peers
    block = lax.axis_index("tm")
    clear_edges(xs, cols)
    clear_edges(ps, cols)
    copies[0].wait()
    for f in range(2):
        for r in range(2):
            spread(xs, f * 6 + r, cols, above[2 + f, r])
            spread(xs, f * 6 + 2 + r, cols, xprev[f, r])
            spread(xs, f * 6 + 4 + r, cols, below[2 + f, r])
            spread(xs, (2 + f) * 6 + r, cols, above[f, r])
            spread(xs, (2 + f) * 6 + 2 + r, cols, x[f, r])
            spread(xs, (2 + f) * 6 + 4 + r, cols, below[f, r])
    for k in range(3):
        xk[k] = xs[:, EDGE - 1 + k : EDGE - 1 + k + cols, :].astype(BF)
    copies[1].wait()
    hidden = jnp.zeros((reach, chan), F32)
    for i in range(3):
        for j in range(3):
            for k in range(3):
                part = [xk[k, (f + 2 - i) * 6 + j : (f + 2 - i) * 6 + j + 4] for f in range(2)]
                patch = jnp.concatenate(part, axis=0).reshape(reach, chan)
                hidden += jnp.dot(patch, w1[i * 9 + j * 3 + k], preferred_element_type=F32)
    sigma = 1.0 / (1.0 + jnp.exp(-hidden))
    act = (hidden * sigma).reshape(frames, rows + 2, cols, chan)[:, 1 : 1 + rows]
    act = act.reshape(cells, chan).astype(BF)
    limit = 2 * lengths[0] - 2 * frames * block

    def cotangent(f, r):
        if r < 2:
            value = above[2 * frames + f, r]
        elif r > 3:
            value = below[2 * frames + f, r - 4]
        elif f >= 2 * frames:
            value = gnext[f - 2 * frames, r - 2]
        else:
            value = g[f, r - 2]
        value = value.astype(F32)
        return jnp.where(f < limit, value, jnp.zeros_like(value))

    copies[2].wait()
    for r in range(6):
        field = [cotangent(f, r) for f in range(6)]
        for a in range(5):
            spread(ps, a * 6 + r, cols, field[a] + field[a + 1])
    for k in range(3):
        pk[k] = ps[:, EDGE + 1 - k : EDGE + 1 - k + cols, :].astype(BF)
    copies[3].wait()
    pair = jnp.zeros((reach, chan), F32)
    for i in range(3):
        for j in range(3):
            for k in range(3):
                part = [pk[k, (2 * t + i) * 6 + 2 - j : (2 * t + i) * 6 + 6 - j] for t in range(2)]
                patch = jnp.concatenate(part, axis=0).reshape(reach, chan)
                pair += transposed_dot(patch, w2[i * 9 + j * 3 + k])
    grad = (pair * sigma * (1.0 + hidden * (1.0 - sigma))).reshape(frames, rows + 2, cols, chan)
    band = lax.axis_index("row")
    none = jnp.zeros((frames, cols, chan), F32)
    tall[:, 0] = jnp.where(band > 0, grad[:, 0], none).astype(BF)
    tall[:, 1 : 1 + rows] = grad[:, 1 : 1 + rows].astype(BF)
    tall[:, 1 + rows] = jnp.where(band < peers - 1, grad[:, 1 + rows], none).astype(BF)
    half = cells // 2
    wide = act.astype(F32)
    low = wide[:, :128].astype(BF)
    high = jnp.concatenate([wide[:half, 128:], wide[half:, 128:]], axis=1).astype(BF)
    turned = [
        jnp.transpose(ps[a * 6 + 2 : a * 6 + 4, 0:PITCH, :].reshape(2 * PITCH, chan))
        for a in range(5)
    ]
    for p in range(peers):
        pay[p, 0:cells, :] = low
        pay[p, cells : cells + half, :] = high
        mine = jnp.concatenate([v[p * width : (p + 1) * width] for v in turned], axis=0)
        pay[p, cells + half :, :] = mine.astype(BF)


def second_kernel(span, got, out, field, left, prod):
    peers = got.shape[0]
    cells = field.shape[0] // peers // (4 * PITCH) * 192
    half = cells // 2
    chan = field.shape[1]
    width = chan // peers
    cols = 48
    blocks, _, lanes = out.shape
    field[...] = jnp.zeros(field.shape, BF)
    low_lane = lax.broadcasted_iota(jnp.int32, (width, 128), 1) < PITCH
    for q in range(peers):
        low = got[q, 0:cells, :]
        high = got[q, cells : cells + half, :].astype(F32)
        high = [high[:, 0:64].astype(BF), high[:, 64:128].astype(BF)]
        for t in range(2):
            for r in range(2):
                at = ((t * peers + q) * 2 + r) * PITCH + EDGE
                field[at : at + cols, 0:128] = low[(t * 2 + r) * cols : (t * 2 + r + 1) * cols]
                field[at : at + cols, 128:192] = high[t][r * cols : (r + 1) * cols]
    base = cells + half
    for a in range(5):
        plain = [
            got[q, base + a * width : base + (a + 1) * width, :].astype(F32) for q in range(peers)
        ]
        swapped = [pltpu.roll(v, PITCH, 1) for v in plain]
        zero = jnp.zeros((width, 128), F32)
        ring = [zero] + swapped + [zero]
        for q in range(peers):
            rows_of = [
                jnp.where(low_lane, ring[q + 1], ring[q + 2]),
                plain[q],
                jnp.where(low_lane, ring[q], ring[q + 1]),
            ]
            for j in range(3):
                for k in range(3):
                    value = rows_of[j]
                    if k != 1:
                        value = pltpu.roll(value, 127 if k == 0 else 1, 1)
                    for t in range(2):
                        i = a - 2 * t
                        if 0 <= i < 3:
                            tap = i * 9 + j * 3 + k
                            at = (t * peers + q) * 128
                            left[tap * width : (tap + 1) * width, at : at + 128] = value
    prod[:, 192:256] = jnp.zeros((prod.shape[0], 64), F32)
    for i in range(3):
        rows = slice(i * 9 * width, (i + 1) * 9 * width)
        prod[rows, 0:192] = jnp.dot(
            left[rows, :].astype(BF), field[...], preferred_element_type=F32
        )
    lane = lax.broadcasted_iota(jnp.int32, (width, 256), 1)
    for b in range(blocks):
        pieces = []
        done = 0
        while done < span:
            tap, start = divmod(b * span + done, chan)
            size = min(span - done, chan - start)
            pieces.append((tap, start, size, done))
            done += size
        for chunk in range(0, lanes, 128):
            value = None
            for tap, start, size, at in pieces:
                if at + size <= chunk or at >= chunk + 128:
                    continue
                shift = (at - chunk - start) % 256
                part = prod[tap * width : (tap + 1) * width, :]
                if shift:
                    part = pltpu.roll(part, shift, 1)
                part = part[:, :128]
                if value is None:
                    value = part
                else:
                    value = jnp.where(lane[:, :128] < at - chunk, value, part)
            if value is None:
                value = jnp.zeros((width, 128), F32)
            if packed(width, span):
                tail = value[16:24]
                tail = jnp.concatenate([pltpu.roll(tail, 81, 1), pltpu.roll(tail, 40, 1)], axis=0)
                value = jnp.where(lane[:16, :128] < span, value[:16], tail)
            out[b, :, chunk : chunk + 128] = value.astype(BF)


def clip_kernel(got, out):
    total = got[0].astype(F32)
    for p in range(1, got.shape[0]):
        total += got[p].astype(F32)
    out[...] = total.astype(BF)


def last_kernel(scale, got, out):
    width, span = out.shape
    total = got[0].astype(F32)
    for p in range(1, got.shape[0]):
        total += got[p].astype(F32)
    total = total * scale
    if packed(width, span):
        lane = lax.broadcasted_iota(jnp.int32, (8, 128), 1)
        tail = jnp.where(lane < 41, pltpu.roll(total[:8], 47, 1), pltpu.roll(total[8:], 88, 1))
        out[:16] = total[:, :span]
        out[16:] = tail[:, :span]
    else:
        out[...] = total[:, :span]


def grad_kernel(w1_far, tall, after, grad, hs, hk, w1, sem):
    copy = pltpu.make_async_copy(w1_far, w1, sem.at[0])
    copy.start()
    frames, rows, cols, chan = grad.shape
    cells = frames * rows * cols
    clear_edges(hs, cols)
    for f in range(2):
        for r in range(4):
            spread(hs, f * 4 + r, cols, tall[f, r])
            spread(hs, (2 + f) * 4 + r, cols, after[f, r])
    for k in range(3):
        hk[k] = hs[:, EDGE + 1 - k : EDGE + 1 - k + cols, :].astype(BF)
    copy.wait()
    acc = jnp.zeros((cells, chan), F32)
    for i in range(3):
        for j in range(3):
            for k in range(3):
                part = [hk[k, (f + i) * 4 + 2 - j : (f + i) * 4 + 4 - j] for f in range(2)]
                patch = jnp.concatenate(part, axis=0).reshape(cells, chan)
                acc += transposed_dot(patch, w1[i * 9 + j * 3 + k])
    grad[...] = acc.reshape(frames, rows, cols, chan)


def call(body, name, limit, shapes, args, scratch, far=(), scalars=(), sems=0):
    spaces = [pltpu.SMEM] * len(scalars) + [pltpu.HBM] * len(far) + [pltpu.VMEM] * len(args)
    far = [pltpu.with_memory_space_constraint(value, pltpu.HBM) for value in far]
    outs = [jax.ShapeDtypeStruct(shape, kind) for shape, kind in shapes]
    buffers = [pltpu.VMEM(shape, kind) for shape, kind in scratch]
    if sems:
        buffers.append(pltpu.SemaphoreType.DMA((sems,)))
    return pl.pallas_call(
        body,
        name=name,
        out_shape=outs,
        in_specs=[pl.BlockSpec(memory_space=space) for space in spaces],
        out_specs=[pl.BlockSpec(memory_space=pltpu.VMEM)] * len(outs),
        scratch_shapes=buffers,
        compiler_params=pltpu.CompilerParams(vmem_limit_bytes=limit * MIB),
    )(*scalars, *far, *args)


def local(clip_input, out_grad, weight_one, weight_two, lengths):
    frames, rows, cols, chan = clip_input.shape[1:]
    cells = frames * rows * cols
    peers = lax.axis_size("row")
    clips = lax.axis_size("clip")
    steps = lax.axis_size("tm")
    width = chan // peers
    x = clip_input[0]
    g = out_grad[0]
    w1 = weight_one.reshape(27, chan, chan)
    w2 = weight_two.reshape(27, chan, chan)

    xprev = move(x, ("tm",), (1,))
    gnext = move(g[:frames], ("tm",), (-1,))
    (band,) = call(
        band_kernel,
        "band",
        4,
        [((5 * frames, rows, cols, chan), BF)],
        (xprev, gnext),
        [],
        far=(x, g),
        sems=2,
    )
    above = move(band, ("row",), (1,))
    below = move(band, ("row",), (-1,))

    pay, tall = call(
        first_kernel,
        "hidden_and_pairs",
        28,
        [
            ((peers, cells + cells // 2 + 5 * width, 128), BF),
            ((frames, rows + 2, cols, chan), BF),
        ],
        (above, below, xprev, gnext),
        [
            ((24, WIDE, chan), F32),
            ((30, WIDE, chan), F32),
            ((3, 24, cols, chan), BF),
            ((3, 30, cols, chan), BF),
            (x.shape, BF),
            (g.shape, BF),
            (w1.shape, BF),
            (w2.shape, BF),
        ],
        far=(x, g, w1, w2),
        scalars=(lengths,),
        sems=4,
    )
    after = move(tall, ("tm",), (-1,))
    got = lax.all_to_all(pay, "row", 0, 0)
    got, after = lax.optimization_barrier((got, after))

    blocks = clips * steps
    span = 27 * chan // blocks
    shape = (16, 128) if packed(width, span) else (width, (span + 127) // 128 * 128)
    (part,) = call(
        functools.partial(second_kernel, span),
        "kernel_grad_part",
        16,
        [((blocks,) + shape, BF)],
        (got,),
        [
            ((2 * peers * 2 * PITCH, chan), BF),
            ((27 * width, 2 * peers * 128), F32),
            ((27 * width, 256), F32),
        ],
    )
    by_clip = lax.all_to_all(part.reshape((clips, steps * shape[0], shape[1])), "clip", 0, 0)
    (summed,) = call(
        clip_kernel,
        "clip_sum",
        4,
        [((steps * shape[0], shape[1]), BF)],
        (by_clip,),
        [],
    )
    by_step = lax.all_to_all(summed.reshape((steps,) + shape), "tm", 0, 0)
    total = clips * 2 * frames * steps * rows * peers * cols
    (kernel_grad,) = call(
        functools.partial(last_kernel, 1.0 / math.sqrt(total)),
        "kernel_grad_sum",
        4,
        [((width, span), F32)],
        (by_step,),
        [],
    )
    (input_grad,) = call(
        grad_kernel,
        "input_grad",
        16,
        [((frames, rows, cols, chan), F32)],
        (tall, after),
        [((16, WIDE, chan), F32), ((3, 16, cols, chan), BF), (w1.shape, BF)],
        far=(w1,),
        sems=1,
    )
    return (input_grad[None], kernel_grad.T)


def solution(mesh):
    return jax.shard_map(
        local,
        mesh=mesh,
        in_specs=(
            P("clip", "tm", "row", None, None),
            P("clip", "tm", "row", None, None),
            P(),
            P(),
            P("clip"),
        ),
        out_specs=(P("clip", "tm", "row", None, None), P(("clip", "tm"), "row")),
        check_vma=False,
    )
```

```python
import functools
import math

import jax
import jax.numpy as jnp
from jax import lax
from jax.experimental import pallas as pl
from jax.experimental.pallas import tpu as pltpu
from jax.sharding import PartitionSpec as P

BF = jnp.bfloat16
F32 = jnp.float32
EDGE = 16
PITCH = 64
WIDE = 72
MIB = 1024 * 1024


def route(sizes, steps):
    total = math.prod(sizes)
    pairs = []
    for source in range(total):
        index, rest = [], source
        for size in reversed(sizes):
            index.append(rest % size)
            rest //= size
        index = index[::-1]
        there = [a + b for a, b in zip(index, steps)]
        if all(0 <= a < size for a, size in zip(there, sizes)):
            target = 0
            for a, size in zip(there, sizes):
                target = target * size + a
            pairs.append((source, target))
    return pairs


def move(value, axes, steps):
    sizes = [lax.axis_size(axis) for axis in axes]
    return lax.ppermute(value, axes if len(axes) > 1 else axes[0], route(sizes, steps))


def digits(size):
    stages, stride = [], size
    while stride > 1:
        radix = 4 if stride % 4 == 0 else stride
        stride //= radix
        stages.append((stride, radix))
    return stages


def rotate(value, axis, stride, radix, by):
    pairs = []
    for source in range(lax.axis_size(axis)):
        digit = source // stride % radix
        pairs.append((source, source + ((digit + by) % radix - digit) * stride))
    return lax.ppermute(value, axis, pairs)


def exchange(parts, axis, stride, radix):
    return [parts[0]] + [rotate(parts[d], axis, stride, radix, d) for d in range(1, radix)]


def digit_of(axis, stride, radix):
    return lax.rem(lax.div(lax.axis_index(axis), stride), radix)


def spread(ref, index, cols, value):
    ref[index, EDGE : EDGE + cols, :] = value.astype(F32)


def clear_edges(ref, cols):
    blocks, width, chan = ref.shape
    ref[:, 0:EDGE, :] = jnp.zeros((blocks, EDGE, chan), F32)
    ref[:, EDGE + cols :, :] = jnp.zeros((blocks, width - EDGE - cols, chan), F32)


def transposed_dot(a, b):
    return lax.dot_general(a, b, (((1,), (1,)), ((), ())), preferred_element_type=F32)


def band_kernel(x, g, xprev, gnext, band, sem):
    nx, ng = x.shape[0], g.shape[0]
    copies = [
        pltpu.make_async_copy(x, band.at[0:nx], sem.at[0]),
        pltpu.make_async_copy(g, band.at[2 * nx : 2 * nx + ng], sem.at[1]),
    ]
    for copy in copies:
        copy.start()
    band[nx : 2 * nx] = xprev[...]
    band[2 * nx + ng :] = gnext[...]
    for copy in copies:
        copy.wait()


def packed(width, span):
    return (width, span) == (24, 81)


def first_kernel(
    lengths, x_far, g_far, w1_far, w2_far, above, below, xprev, gnext,
    pay, tall,
    xs, ps, xk, pk, x, g, w1, w2, sem,
):
    pairs = ((x_far, x), (w1_far, w1), (g_far, g), (w2_far, w2))
    copies = [pltpu.make_async_copy(a, b, sem.at[n]) for n, (a, b) in enumerate(pairs)]
    for copy in copies:
        copy.start()
    frames, rows, cols, chan = x.shape
    cells = frames * rows * cols
    reach = 2 * cells
    peers = pay.shape[0]
    width = chan // peers
    block = lax.axis_index("tm")
    clear_edges(xs, cols)
    clear_edges(ps, cols)
    copies[0].wait()
    for f in range(2):
        for r in range(2):
            spread(xs, f * 6 + r, cols, above[2 + f, r])
            spread(xs, f * 6 + 2 + r, cols, xprev[f, r])
            spread(xs, f * 6 + 4 + r, cols, below[2 + f, r])
            spread(xs, (2 + f) * 6 + r, cols, above[f, r])
            spread(xs, (2 + f) * 6 + 2 + r, cols, x[f, r])
            spread(xs, (2 + f) * 6 + 4 + r, cols, below[f, r])
    for k in range(3):
        xk[k] = xs[:, EDGE - 1 + k : EDGE - 1 + k + cols, :].astype(BF)
    copies[1].wait()
    hidden = jnp.zeros((reach, chan), F32)
    for i in range(3):
        for j in range(3):
            for k in range(3):
                part = [xk[k, (f + 2 - i) * 6 + j : (f + 2 - i) * 6 + j + 4] for f in range(2)]
                patch = jnp.concatenate(part, axis=0).reshape(reach, chan)
                hidden += jnp.dot(patch, w1[i * 9 + j * 3 + k], preferred_element_type=F32)
    sigma = 1.0 / (1.0 + jnp.exp(-hidden))
    act = (hidden * sigma).reshape(frames, rows + 2, cols, chan)[:, 1 : 1 + rows]
    act = act.reshape(cells, chan).astype(BF)
    limit = 2 * lengths[0] - 2 * frames * block

    def cotangent(f, r):
        if r < 2:
            value = above[2 * frames + f, r]
        elif r > 3:
            value = below[2 * frames + f, r - 4]
        elif f >= 2 * frames:
            value = gnext[f - 2 * frames, r - 2]
        else:
            value = g[f, r - 2]
        value = value.astype(F32)
        return jnp.where(f < limit, value, jnp.zeros_like(value))

    copies[2].wait()
    for r in range(6):
        field = [cotangent(f, r) for f in range(6)]
        for a in range(5):
            spread(ps, a * 6 + r, cols, field[a] + field[a + 1])
    for k in range(3):
        pk[k] = ps[:, EDGE + 1 - k : EDGE + 1 - k + cols, :].astype(BF)
    copies[3].wait()
    pair = jnp.zeros((reach, chan), F32)
    for i in range(3):
        for j in range(3):
            for k in range(3):
                part = [pk[k, (2 * t + i) * 6 + 2 - j : (2 * t + i) * 6 + 6 - j] for t in range(2)]
                patch = jnp.concatenate(part, axis=0).reshape(reach, chan)
                pair += transposed_dot(patch, w2[i * 9 + j * 3 + k])
    grad = (pair * sigma * (1.0 + hidden * (1.0 - sigma))).reshape(frames, rows + 2, cols, chan)
    band = lax.axis_index("row")
    none = jnp.zeros((frames, cols, chan), F32)
    tall[:, 0] = jnp.where(band > 0, grad[:, 0], none).astype(BF)
    tall[:, 1 : 1 + rows] = grad[:, 1 : 1 + rows].astype(BF)
    tall[:, 1 + rows] = jnp.where(band < peers - 1, grad[:, 1 + rows], none).astype(BF)
    half = cells // 2
    wide = act.astype(F32)
    low = wide[:, :128].astype(BF)
    high = jnp.concatenate([wide[:half, 128:], wide[half:, 128:]], axis=1).astype(BF)
    turned = [
        jnp.transpose(ps[a * 6 + 2 : a * 6 + 4, 0:PITCH, :].reshape(2 * PITCH, chan))
        for a in range(5)
    ]
    for p in range(peers):
        pay[p, 0:cells, :] = low
        pay[p, cells : cells + half, :] = high
        mine = jnp.concatenate([v[p * width : (p + 1) * width] for v in turned], axis=0)
        pay[p, cells + half :, :] = mine.astype(BF)


def second_kernel(span, got, *refs):
    *outs, out, field, left, prod = refs
    peers = got.shape[0]
    cells = field.shape[0] // peers // (4 * PITCH) * 192
    half = cells // 2
    chan = field.shape[1]
    width = chan // peers
    cols = 48
    blocks, _, lanes = out.shape
    field[...] = jnp.zeros(field.shape, BF)
    low_lane = lax.broadcasted_iota(jnp.int32, (width, 128), 1) < PITCH
    for q in range(peers):
        low = got[q, 0:cells, :]
        high = got[q, cells : cells + half, :].astype(F32)
        high = [high[:, 0:64].astype(BF), high[:, 64:128].astype(BF)]
        for t in range(2):
            for r in range(2):
                at = ((t * peers + q) * 2 + r) * PITCH + EDGE
                field[at : at + cols, 0:128] = low[(t * 2 + r) * cols : (t * 2 + r + 1) * cols]
                field[at : at + cols, 128:192] = high[t][r * cols : (r + 1) * cols]
    base = cells + half
    for a in range(5):
        plain = [
            got[q, base + a * width : base + (a + 1) * width, :].astype(F32) for q in range(peers)
        ]
        swapped = [pltpu.roll(v, PITCH, 1) for v in plain]
        zero = jnp.zeros((width, 128), F32)
        ring = [zero] + swapped + [zero]
        for q in range(peers):
            rows_of = [
                jnp.where(low_lane, ring[q + 1], ring[q + 2]),
                plain[q],
                jnp.where(low_lane, ring[q], ring[q + 1]),
            ]
            for j in range(3):
                for k in range(3):
                    value = rows_of[j]
                    if k != 1:
                        value = pltpu.roll(value, 127 if k == 0 else 1, 1)
                    for t in range(2):
                        i = a - 2 * t
                        if 0 <= i < 3:
                            tap = i * 9 + j * 3 + k
                            at = (t * peers + q) * 128
                            left[tap * width : (tap + 1) * width, at : at + 128] = value
    prod[:, 192:256] = jnp.zeros((prod.shape[0], 64), F32)
    for i in range(3):
        rows = slice(i * 9 * width, (i + 1) * 9 * width)
        prod[rows, 0:192] = jnp.dot(
            left[rows, :].astype(BF), field[...], preferred_element_type=F32
        )
    lane = lax.broadcasted_iota(jnp.int32, (width, 256), 1)
    for b in range(blocks):
        pieces = []
        done = 0
        while done < span:
            tap, start = divmod(b * span + done, chan)
            size = min(span - done, chan - start)
            pieces.append((tap, start, size, done))
            done += size
        for chunk in range(0, lanes, 128):
            value = None
            for tap, start, size, at in pieces:
                if at + size <= chunk or at >= chunk + 128:
                    continue
                shift = (at - chunk - start) % 256
                part = prod[tap * width : (tap + 1) * width, :]
                if shift:
                    part = pltpu.roll(part, shift, 1)
                part = part[:, :128]
                if value is None:
                    value = part
                else:
                    value = jnp.where(lane[:, :128] < at - chunk, value, part)
            if value is None:
                value = jnp.zeros((width, 128), F32)
            if packed(width, span):
                tail = value[16:24]
                tail = jnp.concatenate([pltpu.roll(tail, 81, 1), pltpu.roll(tail, 40, 1)], axis=0)
                value = jnp.where(lane[:16, :128] < span, value[:16], tail)
            out[b, :, chunk : chunk + 128] = value.astype(BF)
    send(out, outs, "clip", 1)


def send(source, outs, axis, stride):
    digit = digit_of(axis, stride, len(outs))
    size = source.shape[0] // len(outs)
    for d, out in enumerate(outs):
        at = lax.rem(digit + d, len(outs)) * size
        out[...] = source[pl.ds(at, size)]


def summed(refs):
    total = refs[0][...].astype(F32)
    for ref in refs[1:]:
        total += ref[...].astype(F32)
    return total


def sum_kernel(count, stride, *refs):
    total = refs[-1]
    total[...] = summed(refs[:count]).astype(BF)
    send(total, refs[count:-1], "tm", stride)


def last_kernel(scale, *refs):
    out = refs[-1]
    width, span = out.shape
    total = summed(refs[:-1])[0]
    total = total * scale
    if packed(width, span):
        lane = lax.broadcasted_iota(jnp.int32, (8, 128), 1)
        tail = jnp.where(lane < 41, pltpu.roll(total[:8], 47, 1), pltpu.roll(total[8:], 88, 1))
        out[:16] = total[:, :span]
        out[16:] = tail[:, :span]
    else:
        out[...] = total[:, :span]


def grad_kernel(w1_far, tall, after, grad, hs, hk, w1, sem):
    copy = pltpu.make_async_copy(w1_far, w1, sem.at[0])
    copy.start()
    frames, rows, cols, chan = grad.shape
    cells = frames * rows * cols
    clear_edges(hs, cols)
    for f in range(2):
        for r in range(4):
            spread(hs, f * 4 + r, cols, tall[f, r])
            spread(hs, (2 + f) * 4 + r, cols, after[f, r])
    for k in range(3):
        hk[k] = hs[:, EDGE + 1 - k : EDGE + 1 - k + cols, :].astype(BF)
    copy.wait()
    acc = jnp.zeros((cells, chan), F32)
    for i in range(3):
        for j in range(3):
            for k in range(3):
                part = [hk[k, (f + i) * 4 + 2 - j : (f + i) * 4 + 4 - j] for f in range(2)]
                patch = jnp.concatenate(part, axis=0).reshape(cells, chan)
                acc += transposed_dot(patch, w1[i * 9 + j * 3 + k])
    grad[...] = acc.reshape(frames, rows, cols, chan)


def call(body, name, limit, shapes, args, scratch, far=(), scalars=(), sems=0):
    spaces = [pltpu.SMEM] * len(scalars) + [pltpu.HBM] * len(far) + [pltpu.VMEM] * len(args)
    far = [pltpu.with_memory_space_constraint(value, pltpu.HBM) for value in far]
    outs = [jax.ShapeDtypeStruct(shape, kind) for shape, kind in shapes]
    buffers = [pltpu.VMEM(shape, kind) for shape, kind in scratch]
    if sems:
        buffers.append(pltpu.SemaphoreType.DMA((sems,)))
    return pl.pallas_call(
        body,
        name=name,
        out_shape=outs,
        in_specs=[pl.BlockSpec(memory_space=space) for space in spaces],
        out_specs=[pl.BlockSpec(memory_space=pltpu.VMEM)] * len(outs),
        scratch_shapes=buffers,
        compiler_params=pltpu.CompilerParams(vmem_limit_bytes=limit * MIB),
    )(*scalars, *far, *args)


def local(clip_input, out_grad, weight_one, weight_two, lengths):
    frames, rows, cols, chan = clip_input.shape[1:]
    cells = frames * rows * cols
    peers = lax.axis_size("row")
    clips = lax.axis_size("clip")
    steps = lax.axis_size("tm")
    width = chan // peers
    x = clip_input[0]
    g = out_grad[0]
    w1 = weight_one.reshape(27, chan, chan)
    w2 = weight_two.reshape(27, chan, chan)

    xprev = move(x, ("tm",), (1,))
    gnext = move(g[:frames], ("tm",), (-1,))
    (band,) = call(
        band_kernel,
        "band",
        4,
        [((5 * frames, rows, cols, chan), BF)],
        (xprev, gnext),
        [],
        far=(x, g),
        sems=2,
    )
    above = move(band, ("row",), (1,))
    below = move(band, ("row",), (-1,))

    pay, tall = call(
        first_kernel,
        "hidden_and_pairs",
        28,
        [
            ((peers, cells + cells // 2 + 5 * width, 128), BF),
            ((frames, rows + 2, cols, chan), BF),
        ],
        (above, below, xprev, gnext),
        [
            ((24, WIDE, chan), F32),
            ((30, WIDE, chan), F32),
            ((3, 24, cols, chan), BF),
            ((3, 30, cols, chan), BF),
            (x.shape, BF),
            (g.shape, BF),
            (w1.shape, BF),
            (w2.shape, BF),
        ],
        far=(x, g, w1, w2),
        scalars=(lengths,),
        sems=4,
    )
    after = move(tall, ("tm",), (-1,))
    got = lax.all_to_all(pay, "row", 0, 0)
    got, after = lax.optimization_barrier((got, after))

    blocks = clips * steps
    span = 27 * chan // blocks
    shape = (16, 128) if packed(width, span) else (width, (span + 127) // 128 * 128)
    parts = call(
        functools.partial(second_kernel, span),
        "kernel_grad_part",
        20,
        [((steps,) + shape, BF)] * clips,
        (got,),
        [
            ((blocks,) + shape, BF),
            ((2 * peers * 2 * PITCH, chan), BF),
            ((27 * width, 2 * peers * 128), F32),
            ((27 * width, 256), F32),
        ],
    )
    parts = exchange(parts, "clip", 1, clips)
    held = steps
    for stride, radix in digits(steps):
        parts = call(
            functools.partial(sum_kernel, len(parts), stride),
            f"sum_before_{stride}",
            4,
            [((held // radix,) + shape, BF)] * radix,
            parts,
            [((held,) + shape, BF)],
        )
        parts = exchange(parts, "tm", stride, radix)
        held //= radix
    total = clips * 2 * frames * steps * rows * peers * cols
    (kernel_grad,) = call(
        functools.partial(last_kernel, 1.0 / math.sqrt(total)),
        "kernel_grad_sum",
        4,
        [((width, span), F32)],
        parts,
        [],
    )
    (input_grad,) = call(
        grad_kernel,
        "input_grad",
        16,
        [((frames, rows, cols, chan), F32)],
        (tall, after),
        [((16, WIDE, chan), F32), ((3, 16, cols, chan), BF), (w1.shape, BF)],
        far=(w1,),
        sems=1,
    )
    return (input_grad[None], kernel_grad.T)


def solution(mesh):
    return jax.shard_map(
        local,
        mesh=mesh,
        in_specs=(
            P("clip", "tm", "row", None, None),
            P("clip", "tm", "row", None, None),
            P(),
            P(),
            P("clip"),
        ),
        out_specs=(P("clip", "tm", "row", None, None), P(("clip", "tm"), "row")),
        check_vma=False,
    )
```

```python
import functools
import math

import jax
import jax.numpy as jnp
from jax import lax
from jax.experimental import pallas as pl
from jax.experimental.pallas import tpu as pltpu
from jax.sharding import PartitionSpec as P

BF = jnp.bfloat16
F32 = jnp.float32
EDGE = 16
PITCH = 64
WIDE = 72
MIB = 1024 * 1024


def route(sizes, steps):
    total = math.prod(sizes)
    pairs = []
    for source in range(total):
        index, rest = [], source
        for size in reversed(sizes):
            index.append(rest % size)
            rest //= size
        index = index[::-1]
        there = [a + b for a, b in zip(index, steps)]
        if all(0 <= a < size for a, size in zip(there, sizes)):
            target = 0
            for a, size in zip(there, sizes):
                target = target * size + a
            pairs.append((source, target))
    return pairs


def move(value, axes, steps):
    sizes = [lax.axis_size(axis) for axis in axes]
    return lax.ppermute(value, axes if len(axes) > 1 else axes[0], route(sizes, steps))


def spread(ref, index, cols, value):
    ref[index, EDGE : EDGE + cols, :] = value.astype(F32)


def clear_edges(ref, cols):
    blocks, width, chan = ref.shape
    ref[:, 0:EDGE, :] = jnp.zeros((blocks, EDGE, chan), F32)
    ref[:, EDGE + cols :, :] = jnp.zeros((blocks, width - EDGE - cols, chan), F32)


def transposed_dot(a, b):
    return lax.dot_general(a, b, (((1,), (1,)), ((), ())), preferred_element_type=F32)


def band_kernel(x, g, xprev, gnext, band, top, bot, sem):
    nx, ng = x.shape[0], g.shape[0]
    pairs = [(x, band.at[0:nx]), (g, band.at[2 * nx : 2 * nx + ng])]
    pairs += [(x.at[:, row], out.at[0:nx]) for row, out in ((0, top), (1, bot))]
    copies = [pltpu.make_async_copy(a, b, sem.at[n]) for n, (a, b) in enumerate(pairs)]
    for copy in copies:
        copy.start()
    band[nx : 2 * nx] = xprev[...]
    band[2 * nx + ng :] = gnext[...]
    top[nx:] = xprev[:, 0]
    bot[nx:] = xprev[:, 1]
    for copy in copies:
        copy.wait()


def packed(width, span):
    return (width, span) == (24, 81)


def silu_kernel(
    lengths, x_far, g_far, w_far, above, below, xprev, gnext, pay, xs, ps, xk, x, g, w, sem
):
    pairs = ((x_far, x), (w_far, w), (g_far, g))
    copies = [pltpu.make_async_copy(a, b, sem.at[n]) for n, (a, b) in enumerate(pairs)]
    for copy in copies:
        copy.start()
    frames, rows, cols, chan = x.shape
    cells = frames * rows * cols
    peers = pay.shape[0]
    width = chan // peers
    clear_edges(xs, cols)
    for f in range(2):
        for r in range(2):
            spread(xs, f * 4 + 1 + r, cols, xprev[f, r])
        spread(xs, f * 4, cols, above[2 + f])
        spread(xs, f * 4 + 3, cols, below[2 + f])
        spread(xs, (2 + f) * 4, cols, above[f])
        spread(xs, (2 + f) * 4 + 3, cols, below[f])
    copies[0].wait()
    for f in range(2):
        for r in range(2):
            spread(xs, (2 + f) * 4 + 1 + r, cols, x[f, r])
    for k in range(3):
        piece = xs[:, EDGE - 1 + k : EDGE - 1 + k + cols, :].astype(BF)
        xk[:, :, k * chan : (k + 1) * chan] = piece
    copies[2].wait()
    limit = 2 * lengths[0] - 2 * frames * lax.axis_index("tm")
    ps[:, 0:EDGE, :] = jnp.zeros((10, EDGE, chan), F32)
    for r in range(2):
        field = masked_frames([g[f, r] for f in range(4)] + [gnext[f, r] for f in range(2)], limit)
        for a in range(5):
            ps[a * 2 + r, EDGE : EDGE + cols, :] = field[a] + field[a + 1]
    turned = [
        jnp.transpose(ps[2 * a : 2 * a + 2].reshape(2 * PITCH, chan)).astype(BF) for a in range(5)
    ]
    copies[1].wait()
    hidden = jnp.zeros((cells, chan), F32)
    for i in range(3):
        for j in range(3):
            part = [xk[(f + 2 - i) * 4 + j : (f + 2 - i) * 4 + j + 2] for f in range(2)]
            patch = jnp.concatenate(part, axis=0).reshape(cells, 3 * chan)
            rows_of = slice((i * 3 + j) * 3 * chan, (i * 3 + j + 1) * 3 * chan)
            hidden += jnp.dot(patch, w[rows_of, :], preferred_element_type=F32)
    act = (hidden / (1.0 + jnp.exp(-hidden))).astype(BF)
    half = cells // 2
    wide = act.astype(F32)
    low = wide[:, :128].astype(BF)
    high = jnp.concatenate([wide[:half, 128:], wide[half:, 128:]], axis=1).astype(BF)
    for p in range(peers):
        pay[p, 0:cells, :] = low
        pay[p, cells : cells + half, :] = high
        mine = jnp.concatenate([v[p * width : (p + 1) * width] for v in turned], axis=0)
        pay[p, cells + half :, :] = mine


def masked_frames(values, limit):
    return [jnp.where(f < limit, v.astype(F32), 0.0) for f, v in enumerate(values)]


def hidden_grad_kernel(
    lengths, x_far, g_far, w1_far, w2_far, above, below, xprev, gnext,
    tall,
    xs, ps, xk, pk, x, g, w1, w2, sem,
):
    pairs = ((x_far, x), (w1_far, w1), (g_far, g), (w2_far, w2))
    copies = [pltpu.make_async_copy(a, b, sem.at[n]) for n, (a, b) in enumerate(pairs)]
    for copy in copies:
        copy.start()
    frames, rows, cols, chan = x.shape
    reach = 2 * frames * rows * cols
    clear_edges(xs, cols)
    clear_edges(ps, cols)
    copies[0].wait()
    for f in range(2):
        for r in range(2):
            spread(xs, f * 6 + r, cols, above[2 + f, r])
            spread(xs, f * 6 + 2 + r, cols, xprev[f, r])
            spread(xs, f * 6 + 4 + r, cols, below[2 + f, r])
            spread(xs, (2 + f) * 6 + r, cols, above[f, r])
            spread(xs, (2 + f) * 6 + 2 + r, cols, x[f, r])
            spread(xs, (2 + f) * 6 + 4 + r, cols, below[f, r])
    for k in range(3):
        piece = xs[:, EDGE - 1 + k : EDGE - 1 + k + cols, :].astype(BF)
        xk[:, :, k * chan : (k + 1) * chan] = piece
    copies[1].wait()
    hidden = jnp.zeros((reach, chan), F32)
    for i in range(3):
        for j in range(3):
            part = [xk[(f + 2 - i) * 6 + j : (f + 2 - i) * 6 + j + 4] for f in range(2)]
            patch = jnp.concatenate(part, axis=0).reshape(reach, 3 * chan)
            rows_of = slice((i * 3 + j) * 3 * chan, (i * 3 + j + 1) * 3 * chan)
            hidden += jnp.dot(patch, w1[rows_of, :], preferred_element_type=F32)
    sigma = 1.0 / (1.0 + jnp.exp(-hidden))
    slope = sigma * (1.0 + hidden * (1.0 - sigma))
    limit = 2 * lengths[0] - 2 * frames * lax.axis_index("tm")
    copies[2].wait()
    for r in range(6):
        if r < 2:
            values = [above[4 + f, r] for f in range(6)]
        elif r > 3:
            values = [below[4 + f, r - 4] for f in range(6)]
        else:
            values = [g[f, r - 2] for f in range(4)] + [gnext[f, r - 2] for f in range(2)]
        field = masked_frames(values, limit)
        for a in range(5):
            spread(ps, a * 6 + r, cols, field[a] + field[a + 1])
    for k in range(3):
        pk[k] = ps[:, EDGE + 1 - k : EDGE + 1 - k + cols, :].astype(BF)
    copies[3].wait()
    pair = jnp.zeros((reach, chan), F32)
    for i in range(3):
        for j in range(3):
            for k in range(3):
                part = [pk[k, (2 * t + i) * 6 + 2 - j : (2 * t + i) * 6 + 6 - j] for t in range(2)]
                patch = jnp.concatenate(part, axis=0).reshape(reach, chan)
                pair += transposed_dot(patch, w2[i * 9 + j * 3 + k])
    grad = (pair * slope).reshape(frames, rows + 2, cols, chan)
    band = lax.axis_index("row")
    none = jnp.zeros((frames, cols, chan), F32)
    tall[:, 0] = jnp.where(band > 0, grad[:, 0], none).astype(BF)
    tall[:, 1 : 1 + rows] = grad[:, 1 : 1 + rows].astype(BF)
    last = band == lax.axis_size("row") - 1
    tall[:, 1 + rows] = jnp.where(last, none, grad[:, 1 + rows]).astype(BF)


def second_kernel(span, got, out, field, left, prod):
    peers = got.shape[0]
    cells = field.shape[0] // peers // (4 * PITCH) * 192
    half = cells // 2
    chan = field.shape[1]
    width = chan // peers
    cols = 48
    blocks, _, lanes = out.shape
    field[...] = jnp.zeros(field.shape, BF)
    low_lane = lax.broadcasted_iota(jnp.int32, (width, 128), 1) < PITCH
    for q in range(peers):
        low = got[q, 0:cells, :]
        high = got[q, cells : cells + half, :].astype(F32)
        high = [high[:, 0:64].astype(BF), high[:, 64:128].astype(BF)]
        for t in range(2):
            for r in range(2):
                at = ((t * peers + q) * 2 + r) * PITCH + EDGE
                field[at : at + cols, 0:128] = low[(t * 2 + r) * cols : (t * 2 + r + 1) * cols]
                field[at : at + cols, 128:192] = high[t][r * cols : (r + 1) * cols]
    base = cells + half
    for a in range(5):
        plain = [
            got[q, base + a * width : base + (a + 1) * width, :].astype(F32) for q in range(peers)
        ]
        swapped = [pltpu.roll(v, PITCH, 1) for v in plain]
        zero = jnp.zeros((width, 128), F32)
        ring = [zero] + swapped + [zero]
        for q in range(peers):
            rows_of = [
                jnp.where(low_lane, ring[q + 1], ring[q + 2]),
                plain[q],
                jnp.where(low_lane, ring[q], ring[q + 1]),
            ]
            for j in range(3):
                for k in range(3):
                    value = rows_of[j]
                    if k != 1:
                        value = pltpu.roll(value, 127 if k == 0 else 1, 1)
                    for t in range(2):
                        i = a - 2 * t
                        if 0 <= i < 3:
                            tap = i * 9 + j * 3 + k
                            at = (t * peers + q) * 128
                            left[tap * width : (tap + 1) * width, at : at + 128] = value
    prod[:, 192:256] = jnp.zeros((prod.shape[0], 64), F32)
    for i in range(3):
        rows = slice(i * 9 * width, (i + 1) * 9 * width)
        prod[rows, 0:192] = jnp.dot(
            left[rows, :].astype(BF), field[...], preferred_element_type=F32
        )
    lane = lax.broadcasted_iota(jnp.int32, (width, 256), 1)
    for b in range(blocks):
        pieces = []
        done = 0
        while done < span:
            tap, start = divmod(b * span + done, chan)
            size = min(span - done, chan - start)
            pieces.append((tap, start, size, done))
            done += size
        for chunk in range(0, lanes, 128):
            value = None
            for tap, start, size, at in pieces:
                if at + size <= chunk or at >= chunk + 128:
                    continue
                shift = (at - chunk - start) % 256
                part = prod[tap * width : (tap + 1) * width, :]
                if shift:
                    part = pltpu.roll(part, shift, 1)
                part = part[:, :128]
                if value is None:
                    value = part
                else:
                    value = jnp.where(lane[:, :128] < at - chunk, value, part)
            if value is None:
                value = jnp.zeros((width, 128), F32)
            if packed(width, span):
                tail = value[16:24]
                tail = jnp.concatenate([pltpu.roll(tail, 81, 1), pltpu.roll(tail, 40, 1)], axis=0)
                value = jnp.where(lane[:16, :128] < span, value[:16], tail)
            out[b, :, chunk : chunk + 128] = value.astype(BF)


def clip_kernel(got, out):
    total = got[0].astype(F32)
    for p in range(1, got.shape[0]):
        total += got[p].astype(F32)
    out[...] = total.astype(BF)


def last_kernel(scale, got, out):
    width, span = out.shape
    total = got[0].astype(F32)
    for p in range(1, got.shape[0]):
        total += got[p].astype(F32)
    total = total * scale
    if packed(width, span):
        lane = lax.broadcasted_iota(jnp.int32, (8, 128), 1)
        tail = jnp.where(lane < 41, pltpu.roll(total[:8], 47, 1), pltpu.roll(total[8:], 88, 1))
        out[:16] = total[:, :span]
        out[16:] = tail[:, :span]
    else:
        out[...] = total[:, :span]


def grad_kernel(w1_far, tall, after, grad, hs, hk, w1, sem):
    copy = pltpu.make_async_copy(w1_far, w1, sem.at[0])
    copy.start()
    frames, rows, cols, chan = grad.shape
    cells = frames * rows * cols
    clear_edges(hs, cols)
    for f in range(2):
        for r in range(4):
            spread(hs, f * 4 + r, cols, tall[f, r])
            spread(hs, (2 + f) * 4 + r, cols, after[f, r])
    for k in range(3):
        hk[k] = hs[:, EDGE + 1 - k : EDGE + 1 - k + cols, :].astype(BF)
    copy.wait()
    acc = jnp.zeros((cells, chan), F32)
    for i in range(3):
        for j in range(3):
            for k in range(3):
                part = [hk[k, (f + i) * 4 + 2 - j : (f + i) * 4 + 4 - j] for f in range(2)]
                patch = jnp.concatenate(part, axis=0).reshape(cells, chan)
                acc += transposed_dot(patch, w1[i * 9 + j * 3 + k])
    grad[...] = acc.reshape(frames, rows, cols, chan)


def call(body, name, limit, shapes, args, scratch, far=(), scalars=(), sems=0):
    spaces = [pltpu.SMEM] * len(scalars) + [pltpu.HBM] * len(far) + [pltpu.VMEM] * len(args)
    far = [pltpu.with_memory_space_constraint(value, pltpu.HBM) for value in far]
    outs = [jax.ShapeDtypeStruct(shape, kind) for shape, kind in shapes]
    buffers = [pltpu.VMEM(shape, kind) for shape, kind in scratch]
    if sems:
        buffers.append(pltpu.SemaphoreType.DMA((sems,)))
    return pl.pallas_call(
        body,
        name=name,
        out_shape=outs,
        in_specs=[pl.BlockSpec(memory_space=space) for space in spaces],
        out_specs=[pl.BlockSpec(memory_space=pltpu.VMEM)] * len(outs),
        scratch_shapes=buffers,
        compiler_params=pltpu.CompilerParams(vmem_limit_bytes=limit * MIB),
    )(*scalars, *far, *args)


def local(clip_input, out_grad, weight_one, weight_two, lengths):
    frames, rows, cols, chan = clip_input.shape[1:]
    cells = frames * rows * cols
    peers = lax.axis_size("row")
    clips = lax.axis_size("clip")
    steps = lax.axis_size("tm")
    width = chan // peers
    x = clip_input[0]
    g = out_grad[0]
    w1 = weight_one.reshape(27, chan, chan)
    w2 = weight_two.reshape(27, chan, chan)

    xprev = move(x, ("tm",), (1,))
    gnext = move(g[:frames], ("tm",), (-1,))
    edge = (2 * frames, cols, chan)
    band, top, bot = call(
        band_kernel,
        "band",
        4,
        [((5 * frames, rows, cols, chan), BF), (edge, BF), (edge, BF)],
        (xprev, gnext),
        [],
        far=(x, g),
        sems=4,
    )
    above_edge = move(bot, ("row",), (1,))
    below_edge = move(top, ("row",), (-1,))
    above = move(band, ("row",), (1,))
    below = move(band, ("row",), (-1,))
    w1_flat = weight_one.reshape(27 * chan, chan)
    (pay,) = call(
        silu_kernel,
        "hidden_and_act",
        16,
        [((peers, cells + cells // 2 + 5 * width, 128), BF)],
        (above_edge, below_edge, xprev, gnext),
        [
            ((16, WIDE, chan), F32),
            ((10, PITCH, chan), F32),
            ((16, cols, 3 * chan), BF),
            (x.shape, BF),
            (g.shape, BF),
            (w1_flat.shape, BF),
        ],
        far=(x, g, w1_flat),
        scalars=(lengths,),
        sems=3,
    )
    got = lax.all_to_all(pay, "row", 0, 0)
    (tall,) = call(
        hidden_grad_kernel,
        "hidden_grad",
        28,
        [((frames, rows + 2, cols, chan), BF)],
        (above, below, xprev, gnext),
        [
            ((24, WIDE, chan), F32),
            ((30, WIDE, chan), F32),
            ((24, cols, 3 * chan), BF),
            ((3, 30, cols, chan), BF),
            (x.shape, BF),
            (g.shape, BF),
            (w1_flat.shape, BF),
            (w2.shape, BF),
        ],
        far=(x, g, w1_flat, w2),
        scalars=(lengths,),
        sems=4,
    )
    got, tall = lax.optimization_barrier((got, tall))
    after = move(tall, ("tm",), (-1,))

    blocks = clips * steps
    span = 27 * chan // blocks
    shape = (16, 128) if packed(width, span) else (width, (span + 127) // 128 * 128)
    (part,) = call(
        functools.partial(second_kernel, span),
        "kernel_grad_part",
        16,
        [((blocks,) + shape, BF)],
        (got,),
        [
            ((2 * peers * 2 * PITCH, chan), BF),
            ((27 * width, 2 * peers * 128), F32),
            ((27 * width, 256), F32),
        ],
    )
    by_clip = lax.all_to_all(part.reshape((clips, steps * shape[0], shape[1])), "clip", 0, 0)
    (summed,) = call(
        clip_kernel,
        "clip_sum",
        4,
        [((steps * shape[0], shape[1]), BF)],
        (by_clip,),
        [],
    )
    summed, after = lax.optimization_barrier((summed, after))
    by_step = lax.all_to_all(summed.reshape((steps,) + shape), "tm", 0, 0)
    total = clips * 2 * frames * steps * rows * peers * cols
    (kernel_grad,) = call(
        functools.partial(last_kernel, 1.0 / math.sqrt(total)),
        "kernel_grad_sum",
        4,
        [((width, span), F32)],
        (by_step,),
        [],
    )
    (input_grad,) = call(
        grad_kernel,
        "input_grad",
        16,
        [((frames, rows, cols, chan), F32)],
        (tall, after),
        [((16, WIDE, chan), F32), ((3, 16, cols, chan), BF), (w1.shape, BF)],
        far=(w1,),
        sems=1,
    )
    return (input_grad[None], kernel_grad.T)


def solution(mesh):
    return jax.shard_map(
        local,
        mesh=mesh,
        in_specs=(
            P("clip", "tm", "row", None, None),
            P("clip", "tm", "row", None, None),
            P(),
            P(),
            P("clip"),
        ),
        out_specs=(P("clip", "tm", "row", None, None), P(("clip", "tm"), "row")),
        check_vma=False,
    )
```

```python
import functools
import math

import jax
import jax.numpy as jnp
from jax import lax
from jax.experimental import pallas as pl
from jax.experimental.pallas import tpu as pltpu
from jax.sharding import PartitionSpec as P

BF = jnp.bfloat16
F32 = jnp.float32
EDGE = 16
PITCH = 64
MIB = 1024 * 1024


def route(sizes, steps):
    total = math.prod(sizes)
    pairs = []
    for source in range(total):
        index, rest = [], source
        for size in reversed(sizes):
            index.append(rest % size)
            rest //= size
        index = index[::-1]
        there = [a + b for a, b in zip(index, steps)]
        if all(0 <= a < size for a, size in zip(there, sizes)):
            target = 0
            for a, size in zip(there, sizes):
                target = target * size + a
            pairs.append((source, target))
    return pairs


def move(value, axes, steps):
    sizes = [lax.axis_size(axis) for axis in axes]
    return lax.ppermute(value, axes if len(axes) > 1 else axes[0], route(sizes, steps))


def transposed_dot(a, b):
    return lax.dot_general(a, b, (((1,), (1,)), ((), ())), preferred_element_type=F32)


def plain_dot(a, b):
    return jnp.dot(a, b, preferred_element_type=F32)


def column_shift(value, by, cols):
    cells, chan = value.shape
    moved = pltpu.roll(value, by % cells, 0).reshape(cells // cols, cols, chan)
    column = lax.broadcasted_iota(jnp.int32, moved.shape, 1)
    moved = jnp.where(column == (0 if by > 0 else cols - 1), 0.0, moved)
    return moved.reshape(cells, chan)


def conv(patch, weight, dot, first_shift, cols):
    total = None
    for k in (1, 0, 2):
        part = None
        for i in range(3):
            for j in range(3):
                term = dot(patch(i, j), weight[i * 9 + j * 3 + k])
                part = term if part is None else part + term
        if k != 1:
            part = column_shift(part, first_shift if k == 0 else -first_shift, cols)
        total = part if total is None else total + part
    return total


def blocks_of(ref, starts, count):
    value = jnp.concatenate([ref[at : at + count] for at in starts], axis=0)
    return value.reshape(-1, value.shape[-1])


def start_copies(pairs, sem):
    copies = [pltpu.make_async_copy(a, b, sem.at[n]) for n, (a, b) in enumerate(pairs)]
    for copy in copies:
        copy.start()
    return copies


def band_kernel(x, g, xprev, gnext, band, sem):
    nx, ng = x.shape[0], g.shape[0]
    copies = start_copies(((x, band.at[0:nx]), (g, band.at[2 * nx : 2 * nx + ng])), sem)
    band[nx : 2 * nx] = xprev[...]
    band[2 * nx + ng :] = gnext[...]
    for copy in copies:
        copy.wait()


def packed(width, span):
    return (width, span) == (24, 81)


def masked_frames(values, limit):
    return [jnp.where(f < limit, v.astype(F32), 0.0) for f, v in enumerate(values)]


def silu_kernel(
    lengths, x_far, g_far, w_far, above, below, xprev, gnext, pay, xe, ps, g, w, sem
):
    frames, rows, cols, chan = xprev.shape
    cells = frames * rows * cols
    peers = pay.shape[0]
    width = chan // peers
    pairs = [(g_far, g), (w_far, w)]
    pairs += [(x_far.at[f], xe.at[(2 + f) * 4 + 1 : (2 + f) * 4 + 3]) for f in range(2)]
    copies = start_copies(pairs, sem)
    for f in range(2):
        xe[f * 4] = above[2 + f, 1]
        xe[f * 4 + 1 : f * 4 + 3] = xprev[f]
        xe[f * 4 + 3] = below[2 + f, 0]
        xe[(2 + f) * 4] = above[f, 1]
        xe[(2 + f) * 4 + 3] = below[f, 0]
    limit = 2 * lengths[0] - 2 * frames * lax.axis_index("tm")
    ps[:, 0:EDGE, :] = jnp.zeros((10, EDGE, chan), F32)
    copies[0].wait()
    for r in range(2):
        field = masked_frames([g[f, r] for f in range(4)] + [gnext[f, r] for f in range(2)], limit)
        for a in range(5):
            ps[a * 2 + r, EDGE : EDGE + cols, :] = field[a] + field[a + 1]
    turned = [
        jnp.transpose(ps[2 * a : 2 * a + 2].reshape(2 * PITCH, chan)) for a in range(5)
    ]
    for p in range(peers):
        mine = jnp.concatenate([v[p * width : (p + 1) * width] for v in turned], axis=0)
        pay[p, cells + cells // 2 :, :] = mine.astype(BF)
    for copy in copies[1:]:
        copy.wait()

    def patch(i, j):
        return blocks_of(xe, [(f + 2 - i) * 4 + j for f in range(2)], 2)

    hidden = conv(patch, w, plain_dot, 1, cols)
    act = hidden / (1.0 + jnp.exp(-hidden))
    half = cells // 2
    low = act[:, :128].astype(BF)
    high = jnp.concatenate([act[:half, 128:], act[half:, 128:]], axis=1).astype(BF)
    for p in range(peers):
        pay[p, 0:cells, :] = low
        pay[p, cells : cells + half, :] = high


def hidden_grad_kernel(
    lengths, x_far, g_far, w1_far, w2_far, above, below, xprev, gnext,
    tall,
    xe, pe, g, w1, w2, sem,
):
    frames, rows, cols, chan = xprev.shape
    pairs = [(g_far, g), (w1_far, w1), (w2_far, w2)]
    pairs += [(x_far.at[f], xe.at[(2 + f) * 6 + 2 : (2 + f) * 6 + 4]) for f in range(2)]
    copies = start_copies(pairs, sem)
    for f in range(2):
        xe[f * 6 : f * 6 + 2] = above[2 + f]
        xe[f * 6 + 2 : f * 6 + 4] = xprev[f]
        xe[f * 6 + 4 : f * 6 + 6] = below[2 + f]
        xe[(2 + f) * 6 : (2 + f) * 6 + 2] = above[f]
        xe[(2 + f) * 6 + 4 : (2 + f) * 6 + 6] = below[f]
    limit = 2 * lengths[0] - 2 * frames * lax.axis_index("tm")
    copies[0].wait()
    for r in range(6):
        if r < 2:
            values = [above[4 + f, r] for f in range(6)]
        elif r > 3:
            values = [below[4 + f, r - 4] for f in range(6)]
        else:
            values = [g[f, r - 2] for f in range(4)] + [gnext[f, r - 2] for f in range(2)]
        field = masked_frames(values, limit)
        for a in range(5):
            pe[a * 6 + r] = (field[a] + field[a + 1]).astype(BF)
    for copy in copies[1:]:
        copy.wait()

    def patch(i, j):
        return blocks_of(xe, [(f + 2 - i) * 6 + j for f in range(2)], 4)

    def pair_patch(i, j):
        return blocks_of(pe, [(2 * t + i) * 6 + 2 - j for t in range(2)], 4)

    hidden = conv(patch, w1, plain_dot, 1, cols)
    pair = conv(pair_patch, w2, transposed_dot, -1, cols)
    sigma = 1.0 / (1.0 + jnp.exp(-hidden))
    grad = pair * sigma * (1.0 + hidden * (1.0 - sigma))
    grad = grad.reshape(frames, rows + 2, cols, chan)
    band = lax.axis_index("row")
    none = jnp.zeros((frames, cols, chan), F32)
    tall[:, 0] = jnp.where(band > 0, grad[:, 0], none).astype(BF)
    tall[:, 1 : 1 + rows] = grad[:, 1 : 1 + rows].astype(BF)
    last = band == lax.axis_size("row") - 1
    tall[:, 1 + rows] = jnp.where(last, none, grad[:, 1 + rows]).astype(BF)


def second_kernel(span, got, out, field, left, prod):
    peers = got.shape[0]
    cells = field.shape[0] // peers // (4 * PITCH) * 192
    half = cells // 2
    chan = field.shape[1]
    width = chan // peers
    cols = 48
    blocks, _, lanes = out.shape
    field[...] = jnp.zeros(field.shape, BF)
    low_lane = lax.broadcasted_iota(jnp.int32, (width, 128), 1) < PITCH
    for q in range(peers):
        low = got[q, 0:cells, :]
        high = got[q, cells : cells + half, :].astype(F32)
        high = [high[:, 0:64].astype(BF), high[:, 64:128].astype(BF)]
        for t in range(2):
            for r in range(2):
                at = ((t * peers + q) * 2 + r) * PITCH + EDGE
                field[at : at + cols, 0:128] = low[(t * 2 + r) * cols : (t * 2 + r + 1) * cols]
                field[at : at + cols, 128:192] = high[t][r * cols : (r + 1) * cols]
    base = cells + half
    for a in range(5):
        plain = [
            got[q, base + a * width : base + (a + 1) * width, :].astype(F32) for q in range(peers)
        ]
        swapped = [pltpu.roll(v, PITCH, 1) for v in plain]
        zero = jnp.zeros((width, 128), F32)
        ring = [zero] + swapped + [zero]
        for q in range(peers):
            rows_of = [
                jnp.where(low_lane, ring[q + 1], ring[q + 2]),
                plain[q],
                jnp.where(low_lane, ring[q], ring[q + 1]),
            ]
            for j in range(3):
                for k in range(3):
                    value = rows_of[j]
                    if k != 1:
                        value = pltpu.roll(value, 127 if k == 0 else 1, 1)
                    for t in range(2):
                        i = a - 2 * t
                        if 0 <= i < 3:
                            tap = i * 9 + j * 3 + k
                            at = (t * peers + q) * 128
                            left[tap * width : (tap + 1) * width, at : at + 128] = value
    prod[:, 192:256] = jnp.zeros((prod.shape[0], 64), F32)
    for i in range(3):
        rows = slice(i * 9 * width, (i + 1) * 9 * width)
        prod[rows, 0:192] = jnp.dot(
            left[rows, :].astype(BF), field[...], preferred_element_type=F32
        )
    lane = lax.broadcasted_iota(jnp.int32, (width, 256), 1)
    for b in range(blocks):
        pieces = []
        done = 0
        while done < span:
            tap, start = divmod(b * span + done, chan)
            size = min(span - done, chan - start)
            pieces.append((tap, start, size, done))
            done += size
        for chunk in range(0, lanes, 128):
            value = None
            for tap, start, size, at in pieces:
                if at + size <= chunk or at >= chunk + 128:
                    continue
                shift = (at - chunk - start) % 256
                part = prod[tap * width : (tap + 1) * width, :]
                if shift:
                    part = pltpu.roll(part, shift, 1)
                part = part[:, :128]
                if value is None:
                    value = part
                else:
                    value = jnp.where(lane[:, :128] < at - chunk, value, part)
            if value is None:
                value = jnp.zeros((width, 128), F32)
            if packed(width, span):
                tail = value[16:24]
                tail = jnp.concatenate([pltpu.roll(tail, 81, 1), pltpu.roll(tail, 40, 1)], axis=0)
                value = jnp.where(lane[:16, :128] < span, value[:16], tail)
            out[b, :, chunk : chunk + 128] = value.astype(BF)


def clip_kernel(got, out):
    total = got[0].astype(F32)
    for p in range(1, got.shape[0]):
        total += got[p].astype(F32)
    out[...] = total.astype(BF)


def last_kernel(scale, got, out):
    width, span = out.shape
    total = got[0].astype(F32)
    for p in range(1, got.shape[0]):
        total += got[p].astype(F32)
    total = total * scale
    if packed(width, span):
        lane = lax.broadcasted_iota(jnp.int32, (8, 128), 1)
        tail = jnp.where(lane < 41, pltpu.roll(total[:8], 47, 1), pltpu.roll(total[8:], 88, 1))
        out[:16] = total[:, :span]
        out[16:] = tail[:, :span]
    else:
        out[...] = total[:, :span]


def grad_kernel(w1_far, tall, after, grad, w1, sem):
    copies = start_copies([(w1_far, w1)], sem)
    frames, rows, cols, chan = grad.shape
    fields = [tall[0], tall[1], after[0], after[1]]

    def patch(i, j):
        value = jnp.concatenate([fields[f + i][2 - j : 4 - j] for f in range(2)], axis=0)
        return value.reshape(-1, chan)

    copies[0].wait()
    grad[...] = conv(patch, w1, transposed_dot, -1, cols).reshape(grad.shape)


def call(body, name, limit, shapes, args, scratch, far=(), scalars=(), sems=0):
    spaces = [pltpu.SMEM] * len(scalars) + [pltpu.HBM] * len(far) + [pltpu.VMEM] * len(args)
    far = [pltpu.with_memory_space_constraint(value, pltpu.HBM) for value in far]
    outs = [jax.ShapeDtypeStruct(shape, kind) for shape, kind in shapes]
    buffers = [pltpu.VMEM(shape, kind) for shape, kind in scratch]
    if sems:
        buffers.append(pltpu.SemaphoreType.DMA((sems,)))
    return pl.pallas_call(
        body,
        name=name,
        out_shape=outs,
        in_specs=[pl.BlockSpec(memory_space=space) for space in spaces],
        out_specs=[pl.BlockSpec(memory_space=pltpu.VMEM)] * len(outs),
        scratch_shapes=buffers,
        compiler_params=pltpu.CompilerParams(vmem_limit_bytes=limit * MIB),
    )(*scalars, *far, *args)


def local(clip_input, out_grad, weight_one, weight_two, lengths):
    frames, rows, cols, chan = clip_input.shape[1:]
    cells = frames * rows * cols
    peers = lax.axis_size("row")
    clips = lax.axis_size("clip")
    steps = lax.axis_size("tm")
    width = chan // peers
    x = clip_input[0]
    g = out_grad[0]
    w1 = weight_one.reshape(27, chan, chan)
    w2 = weight_two.reshape(27, chan, chan)

    xprev = move(x, ("tm",), (1,))
    gnext = move(g[:frames], ("tm",), (-1,))
    (band,) = call(
        band_kernel,
        "band",
        4,
        [((5 * frames, rows, cols, chan), BF)],
        (xprev, gnext),
        [],
        far=(x, g),
        sems=2,
    )
    above = move(band, ("row",), (1,))
    below = move(band, ("row",), (-1,))
    (pay,) = call(
        silu_kernel,
        "hidden_and_act",
        16,
        [((peers, cells + cells // 2 + 5 * width, 128), BF)],
        (above, below, xprev, gnext),
        [
            ((16, cols, chan), BF),
            ((10, PITCH, chan), F32),
            (g.shape, BF),
            (w1.shape, BF),
        ],
        far=(x, g, w1),
        scalars=(lengths,),
        sems=4,
    )
    got = lax.all_to_all(pay, "row", 0, 0)
    (tall,) = call(
        hidden_grad_kernel,
        "hidden_grad",
        28,
        [((frames, rows + 2, cols, chan), BF)],
        (above, below, xprev, gnext),
        [
            ((24, cols, chan), BF),
            ((30, cols, chan), BF),
            (g.shape, BF),
            (w1.shape, BF),
            (w2.shape, BF),
        ],
        far=(x, g, w1, w2),
        scalars=(lengths,),
        sems=5,
    )
    got, tall = lax.optimization_barrier((got, tall))
    after = move(tall, ("tm",), (-1,))

    blocks = clips * steps
    span = 27 * chan // blocks
    shape = (16, 128) if packed(width, span) else (width, (span + 127) // 128 * 128)
    (part,) = call(
        functools.partial(second_kernel, span),
        "kernel_grad_part",
        16,
        [((blocks,) + shape, BF)],
        (got,),
        [
            ((2 * peers * 2 * PITCH, chan), BF),
            ((27 * width, 2 * peers * 128), F32),
            ((27 * width, 256), F32),
        ],
    )
    by_clip = lax.all_to_all(part.reshape((clips, steps * shape[0], shape[1])), "clip", 0, 0)
    (summed,) = call(
        clip_kernel,
        "clip_sum",
        4,
        [((steps * shape[0], shape[1]), BF)],
        (by_clip,),
        [],
    )
    summed, after = lax.optimization_barrier((summed, after))
    by_step = lax.all_to_all(summed.reshape((steps,) + shape), "tm", 0, 0)
    total = clips * 2 * frames * steps * rows * peers * cols
    (kernel_grad,) = call(
        functools.partial(last_kernel, 1.0 / math.sqrt(total)),
        "kernel_grad_sum",
        4,
        [((width, span), F32)],
        (by_step,),
        [],
    )
    (input_grad,) = call(
        grad_kernel,
        "input_grad",
        16,
        [((frames, rows, cols, chan), F32)],
        (tall, after),
        [(w1.shape, BF)],
        far=(w1,),
        sems=1,
    )
    return (input_grad[None], kernel_grad.T)


def solution(mesh):
    return jax.shard_map(
        local,
        mesh=mesh,
        in_specs=(
            P("clip", "tm", "row", None, None),
            P("clip", "tm", "row", None, None),
            P(),
            P(),
            P("clip"),
        ),
        out_specs=(P("clip", "tm", "row", None, None), P(("clip", "tm"), "row")),
        check_vma=False,
    )
```

```python
import functools
import math

import jax
import jax.numpy as jnp
from jax import lax
from jax.experimental import pallas as pl
from jax.experimental.pallas import tpu as pltpu
from jax.sharding import PartitionSpec as P

BF = jnp.bfloat16
F32 = jnp.float32
EDGE = 16
PITCH = 64
MIB = 1024 * 1024


def route(sizes, steps):
    total = math.prod(sizes)
    pairs = []
    for source in range(total):
        index, rest = [], source
        for size in reversed(sizes):
            index.append(rest % size)
            rest //= size
        index = index[::-1]
        there = [a + b for a, b in zip(index, steps)]
        if all(0 <= a < size for a, size in zip(there, sizes)):
            target = 0
            for a, size in zip(there, sizes):
                target = target * size + a
            pairs.append((source, target))
    return pairs


def move(value, axes, steps):
    sizes = [lax.axis_size(axis) for axis in axes]
    return lax.ppermute(value, axes if len(axes) > 1 else axes[0], route(sizes, steps))


def transposed_dot(a, b):
    return lax.dot_general(a, b, (((1,), (1,)), ((), ())), preferred_element_type=F32)


def plain_dot(a, b):
    return jnp.dot(a, b, preferred_element_type=F32)


def column_shift(value, by, cols):
    cells, chan = value.shape
    moved = pltpu.roll(value, by % cells, 0).reshape(cells // cols, cols, chan)
    column = lax.broadcasted_iota(jnp.int32, moved.shape, 1)
    moved = jnp.where(column == (0 if by > 0 else cols - 1), 0.0, moved)
    return moved.reshape(cells, chan)


def conv(patch, weight, dot, first_shift, cols):
    total = None
    for k in (1, 0, 2):
        part = None
        for i in range(3):
            for j in range(3):
                term = dot(patch(i, j), weight[i * 9 + j * 3 + k])
                part = term if part is None else part + term
        if k != 1:
            part = column_shift(part, first_shift if k == 0 else -first_shift, cols)
        total = part if total is None else total + part
    return total


def blocks_of(ref, starts, count):
    value = jnp.concatenate([ref[at : at + count] for at in starts], axis=0)
    return value.reshape(-1, value.shape[-1])


def start_copies(pairs, sem):
    copies = [pltpu.make_async_copy(a, b, sem.at[n]) for n, (a, b) in enumerate(pairs)]
    for copy in copies:
        copy.start()
    return copies


def band_kernel(x, g, xprev, gnext, band, sem):
    nx, ng = x.shape[0], g.shape[0]
    copies = start_copies(((x, band.at[0:nx]), (g, band.at[2 * nx : 2 * nx + ng])), sem)
    band[nx : 2 * nx] = xprev[...]
    band[2 * nx + ng :] = gnext[...]
    for copy in copies:
        copy.wait()


def packed(width, span):
    return (width, span) == (24, 81)


def masked_frames(values, limit):
    return [jnp.where(f < limit, v.astype(F32), 0.0) for f, v in enumerate(values)]


def silu_kernel(
    lengths, x_far, g_far, w_far, above, below, xprev, gnext, pay, xe, ps, g, w, sem
):
    frames, rows, cols, chan = xprev.shape
    cells = frames * rows * cols
    peers = pay.shape[0]
    width = chan // peers
    pairs = [(g_far, g), (w_far, w)]
    pairs += [(x_far.at[f], xe.at[(2 + f) * 4 + 1 : (2 + f) * 4 + 3]) for f in range(2)]
    copies = start_copies(pairs, sem)
    for f in range(2):
        xe[f * 4] = above[2 + f, 1]
        xe[f * 4 + 1 : f * 4 + 3] = xprev[f]
        xe[f * 4 + 3] = below[2 + f, 0]
        xe[(2 + f) * 4] = above[f, 1]
        xe[(2 + f) * 4 + 3] = below[f, 0]
    limit = 2 * lengths[0] - 2 * frames * lax.axis_index("tm")
    ps[:, 0:EDGE, :] = jnp.zeros((10, EDGE, chan), F32)
    copies[0].wait()
    for r in range(2):
        field = masked_frames([g[f, r] for f in range(4)] + [gnext[f, r] for f in range(2)], limit)
        for a in range(5):
            ps[a * 2 + r, EDGE : EDGE + cols, :] = field[a] + field[a + 1]
    turned = [
        jnp.transpose(ps[2 * a : 2 * a + 2].reshape(2 * PITCH, chan)) for a in range(5)
    ]
    for p in range(peers):
        mine = jnp.concatenate([v[p * width : (p + 1) * width] for v in turned], axis=0)
        pay[p, cells + cells // 2 :, :] = mine.astype(BF)
    for copy in copies[1:]:
        copy.wait()

    def patch(i, j):
        return blocks_of(xe, [(f + 2 - i) * 4 + j for f in range(2)], 2)

    hidden = conv(patch, w, plain_dot, 1, cols)
    act = hidden / (1.0 + jnp.exp(-hidden))
    half = cells // 2
    low = act[:, :128].astype(BF)
    high = jnp.concatenate([act[:half, 128:], act[half:, 128:]], axis=1).astype(BF)
    for p in range(peers):
        pay[p, 0:cells, :] = low
        pay[p, cells : cells + half, :] = high


def hidden_grad_kernel(
    lengths, x_far, g_far, w1_far, w2_far, above, below, xprev, gnext,
    tall,
    xe, pe, g, w1, w2, sem,
):
    frames, rows, cols, chan = xprev.shape
    pairs = [(g_far, g), (w1_far, w1), (w2_far, w2)]
    pairs += [(x_far.at[f], xe.at[(2 + f) * 6 + 2 : (2 + f) * 6 + 4]) for f in range(2)]
    copies = start_copies(pairs, sem)
    for f in range(2):
        xe[f * 6 : f * 6 + 2] = above[2 + f]
        xe[f * 6 + 2 : f * 6 + 4] = xprev[f]
        xe[f * 6 + 4 : f * 6 + 6] = below[2 + f]
        xe[(2 + f) * 6 : (2 + f) * 6 + 2] = above[f]
        xe[(2 + f) * 6 + 4 : (2 + f) * 6 + 6] = below[f]
    limit = 2 * lengths[0] - 2 * frames * lax.axis_index("tm")
    copies[0].wait()
    for r in range(6):
        if r < 2:
            values = [above[4 + f, r] for f in range(6)]
        elif r > 3:
            values = [below[4 + f, r - 4] for f in range(6)]
        else:
            values = [g[f, r - 2] for f in range(4)] + [gnext[f, r - 2] for f in range(2)]
        field = masked_frames(values, limit)
        for a in range(5):
            pe[a * 6 + r] = (field[a] + field[a + 1]).astype(BF)
    for copy in copies[1:]:
        copy.wait()

    def patch(i, j):
        return blocks_of(xe, [(f + 2 - i) * 6 + j for f in range(2)], 4)

    def pair_patch(i, j):
        return blocks_of(pe, [(2 * t + i) * 6 + 2 - j for t in range(2)], 4)

    hidden = conv(patch, w1, plain_dot, 1, cols)
    pair = conv(pair_patch, w2, transposed_dot, -1, cols)
    sigma = 1.0 / (1.0 + jnp.exp(-hidden))
    grad = pair * sigma * (1.0 + hidden * (1.0 - sigma))
    grad = grad.reshape(frames, rows + 2, cols, chan)
    band = lax.axis_index("row")
    none = jnp.zeros((frames, cols, chan), F32)
    tall[:, 0] = jnp.where(band > 0, grad[:, 0], none).astype(BF)
    tall[:, 1 : 1 + rows] = grad[:, 1 : 1 + rows].astype(BF)
    last = band == lax.axis_size("row") - 1
    tall[:, 1 + rows] = jnp.where(last, none, grad[:, 1 + rows]).astype(BF)


def second_kernel(span, got, out, field, left, prod):
    peers = got.shape[0]
    cells = field.shape[0] // peers // (4 * PITCH) * 192
    half = cells // 2
    chan = field.shape[1]
    width = chan // peers
    cols = 48
    blocks, _, lanes = out.shape
    field[...] = jnp.zeros(field.shape, BF)
    low_lane = lax.broadcasted_iota(jnp.int32, (width, 128), 1) < PITCH
    for q in range(peers):
        low = got[q, 0:cells, :]
        high = got[q, cells : cells + half, :].astype(F32)
        high = [high[:, 0:64].astype(BF), high[:, 64:128].astype(BF)]
        for t in range(2):
            for r in range(2):
                at = ((t * peers + q) * 2 + r) * PITCH + EDGE
                field[at : at + cols, 0:128] = low[(t * 2 + r) * cols : (t * 2 + r + 1) * cols]
                field[at : at + cols, 128:192] = high[t][r * cols : (r + 1) * cols]
    base = cells + half
    for a in range(5):
        plain = [
            got[q, base + a * width : base + (a + 1) * width, :].astype(F32) for q in range(peers)
        ]
        swapped = [pltpu.roll(v, PITCH, 1) for v in plain]
        zero = jnp.zeros((width, 128), F32)
        ring = [zero] + swapped + [zero]
        for q in range(peers):
            rows_of = [
                jnp.where(low_lane, ring[q + 1], ring[q + 2]),
                plain[q],
                jnp.where(low_lane, ring[q], ring[q + 1]),
            ]
            for j in range(3):
                for k in range(3):
                    value = rows_of[j]
                    if k != 1:
                        value = pltpu.roll(value, 127 if k == 0 else 1, 1)
                    for t in range(2):
                        i = a - 2 * t
                        if 0 <= i < 3:
                            tap = i * 9 + j * 3 + k
                            at = (t * peers + q) * 128
                            left[tap * width : (tap + 1) * width, at : at + 128] = value
    prod[:, 192:256] = jnp.zeros((prod.shape[0], 64), F32)
    for i in range(3):
        rows = slice(i * 9 * width, (i + 1) * 9 * width)
        prod[rows, 0:192] = jnp.dot(
            left[rows, :].astype(BF), field[...], preferred_element_type=F32
        )
    lane = lax.broadcasted_iota(jnp.int32, (width, 256), 1)
    for b in range(blocks):
        pieces = []
        done = 0
        while done < span:
            tap, start = divmod(b * span + done, chan)
            size = min(span - done, chan - start)
            pieces.append((tap, start, size, done))
            done += size
        for chunk in range(0, lanes, 128):
            value = None
            for tap, start, size, at in pieces:
                if at + size <= chunk or at >= chunk + 128:
                    continue
                shift = (at - chunk - start) % 256
                part = prod[tap * width : (tap + 1) * width, :]
                if shift:
                    part = pltpu.roll(part, shift, 1)
                part = part[:, :128]
                if value is None:
                    value = part
                else:
                    value = jnp.where(lane[:, :128] < at - chunk, value, part)
            if value is None:
                value = jnp.zeros((width, 128), F32)
            if packed(width, span):
                tail = value[16:24]
                tail = jnp.concatenate([pltpu.roll(tail, 81, 1), pltpu.roll(tail, 40, 1)], axis=0)
                value = jnp.where(lane[:16, :128] < span, value[:16], tail)
            out[b, :, chunk : chunk + 128] = value.astype(BF)


def clip_kernel(got, out):
    total = got[0].astype(F32)
    for p in range(1, got.shape[0]):
        total += got[p].astype(F32)
    out[...] = total.astype(BF)


def last_kernel(scale, got, out):
    width, span = out.shape
    total = got[0].astype(F32)
    for p in range(1, got.shape[0]):
        total += got[p].astype(F32)
    total = total * scale
    if packed(width, span):
        lane = lax.broadcasted_iota(jnp.int32, (8, 128), 1)
        tail = jnp.where(lane < 41, pltpu.roll(total[:8], 47, 1), pltpu.roll(total[8:], 88, 1))
        out[:16] = total[:, :span]
        out[16:] = tail[:, :span]
    else:
        out[...] = total[:, :span]


def grad_kernel(w1_far, tall, after, grad, w1, sem):
    copies = start_copies([(w1_far, w1)], sem)
    frames, rows, cols, chan = grad.shape
    fields = [tall[0], tall[1], after[0], after[1]]

    def patch(i, j):
        value = jnp.concatenate([fields[f + i][2 - j : 4 - j] for f in range(2)], axis=0)
        return value.reshape(-1, chan)

    copies[0].wait()
    grad[...] = conv(patch, w1, transposed_dot, -1, cols).reshape(grad.shape)


def call(body, name, limit, shapes, args, scratch, far=(), scalars=(), sems=0):
    spaces = [pltpu.SMEM] * len(scalars) + [pltpu.HBM] * len(far) + [pltpu.VMEM] * len(args)
    far = [pltpu.with_memory_space_constraint(value, pltpu.HBM) for value in far]
    outs = [jax.ShapeDtypeStruct(shape, kind) for shape, kind in shapes]
    buffers = [pltpu.VMEM(shape, kind) for shape, kind in scratch]
    if sems:
        buffers.append(pltpu.SemaphoreType.DMA((sems,)))
    return pl.pallas_call(
        body,
        name=name,
        out_shape=outs,
        in_specs=[pl.BlockSpec(memory_space=space) for space in spaces],
        out_specs=[pl.BlockSpec(memory_space=pltpu.VMEM)] * len(outs),
        scratch_shapes=buffers,
        compiler_params=pltpu.CompilerParams(vmem_limit_bytes=limit * MIB),
    )(*scalars, *far, *args)


def local(clip_input, out_grad, weight_one, weight_two, lengths):
    frames, rows, cols, chan = clip_input.shape[1:]
    cells = frames * rows * cols
    peers = lax.axis_size("row")
    clips = lax.axis_size("clip")
    steps = lax.axis_size("tm")
    width = chan // peers
    x = clip_input[0]
    g = out_grad[0]
    w1 = weight_one.reshape(27, chan, chan)
    w2 = weight_two.reshape(27, chan, chan)

    xprev = move(x, ("tm",), (1,))
    gnext = move(g[:frames], ("tm",), (-1,))
    (band,) = call(
        band_kernel,
        "band",
        4,
        [((5 * frames, rows, cols, chan), BF)],
        (xprev, gnext),
        [],
        far=(x, g),
        sems=2,
    )
    above = move(band, ("row",), (1,))
    below = move(band, ("row",), (-1,))
    (pay,) = call(
        silu_kernel,
        "hidden_and_act",
        16,
        [((peers, cells + cells // 2 + 5 * width, 128), BF)],
        (above, below, xprev, gnext),
        [
            ((16, cols, chan), BF),
            ((10, PITCH, chan), F32),
            (g.shape, BF),
            (w1.shape, BF),
        ],
        far=(x, g, w1),
        scalars=(lengths,),
        sems=4,
    )
    got = lax.all_to_all(pay, "row", 0, 0)
    (tall,) = call(
        hidden_grad_kernel,
        "hidden_grad",
        28,
        [((frames, rows + 2, cols, chan), BF)],
        (above, below, xprev, gnext),
        [
            ((24, cols, chan), BF),
            ((30, cols, chan), BF),
            (g.shape, BF),
            (w1.shape, BF),
            (w2.shape, BF),
        ],
        far=(x, g, w1, w2),
        scalars=(lengths,),
        sems=5,
    )
    after = move(tall, ("tm",), (-1,))
    got, after = lax.optimization_barrier((got, after))

    blocks = clips * steps
    span = 27 * chan // blocks
    shape = (16, 128) if packed(width, span) else (width, (span + 127) // 128 * 128)
    (part,) = call(
        functools.partial(second_kernel, span),
        "kernel_grad_part",
        16,
        [((blocks,) + shape, BF)],
        (got,),
        [
            ((2 * peers * 2 * PITCH, chan), BF),
            ((27 * width, 2 * peers * 128), F32),
            ((27 * width, 256), F32),
        ],
    )
    by_clip = lax.all_to_all(part.reshape((clips, steps * shape[0], shape[1])), "clip", 0, 0)
    (summed,) = call(
        clip_kernel,
        "clip_sum",
        4,
        [((steps * shape[0], shape[1]), BF)],
        (by_clip,),
        [],
    )
    by_step = lax.all_to_all(summed.reshape((steps,) + shape), "tm", 0, 0)
    total = clips * 2 * frames * steps * rows * peers * cols
    (kernel_grad,) = call(
        functools.partial(last_kernel, 1.0 / math.sqrt(total)),
        "kernel_grad_sum",
        4,
        [((width, span), F32)],
        (by_step,),
        [],
    )
    (input_grad,) = call(
        grad_kernel,
        "input_grad",
        16,
        [((frames, rows, cols, chan), F32)],
        (tall, after),
        [(w1.shape, BF)],
        far=(w1,),
        sems=1,
    )
    return (input_grad[None], kernel_grad.T)


def solution(mesh):
    return jax.shard_map(
        local,
        mesh=mesh,
        in_specs=(
            P("clip", "tm", "row", None, None),
            P("clip", "tm", "row", None, None),
            P(),
            P(),
            P("clip"),
        ),
        out_specs=(P("clip", "tm", "row", None, None), P(("clip", "tm"), "row")),
        check_vma=False,
    )
```

```python
import functools
import math

import jax
import jax.numpy as jnp
from jax import lax
from jax.experimental import pallas as pl
from jax.experimental.pallas import tpu as pltpu
from jax.sharding import PartitionSpec as P

BF = jnp.bfloat16
F32 = jnp.float32
EDGE = 16
PITCH = 64
MIB = 1024 * 1024


def route(sizes, steps):
    total = math.prod(sizes)
    pairs = []
    for source in range(total):
        index, rest = [], source
        for size in reversed(sizes):
            index.append(rest % size)
            rest //= size
        index = index[::-1]
        there = [a + b for a, b in zip(index, steps)]
        if all(0 <= a < size for a, size in zip(there, sizes)):
            target = 0
            for a, size in zip(there, sizes):
                target = target * size + a
            pairs.append((source, target))
    return pairs


def move(value, axes, steps):
    sizes = [lax.axis_size(axis) for axis in axes]
    return lax.ppermute(value, axes if len(axes) > 1 else axes[0], route(sizes, steps))


def transposed_dot(a, b):
    return lax.dot_general(a, b, (((1,), (1,)), ((), ())), preferred_element_type=F32)


def plain_dot(a, b):
    return jnp.dot(a, b, preferred_element_type=F32)


def column_shift(value, by, cols):
    cells, chan = value.shape
    moved = pltpu.roll(value, by % cells, 0).reshape(cells // cols, cols, chan)
    column = lax.broadcasted_iota(jnp.int32, moved.shape, 1)
    moved = jnp.where(column == (0 if by > 0 else cols - 1), 0.0, moved)
    return moved.reshape(cells, chan)


def conv(patch, weight, dot, first_shift, cols):
    total = None
    for k in (1, 0, 2):
        part = None
        for i in range(3):
            for j in range(3):
                term = dot(patch(i, j), weight[i * 9 + j * 3 + k])
                part = term if part is None else part + term
        if k != 1:
            part = column_shift(part, first_shift if k == 0 else -first_shift, cols)
        total = part if total is None else total + part
    return total


def blocks_of(ref, starts, count):
    value = jnp.concatenate([ref[at : at + count] for at in starts], axis=0)
    return value.reshape(-1, value.shape[-1])


def start_copies(pairs, sem):
    copies = [pltpu.make_async_copy(a, b, sem.at[n]) for n, (a, b) in enumerate(pairs)]
    for copy in copies:
        copy.start()
    return copies


def band_kernel(lengths, x, g_far, xprev, gnext, band, g, sem):
    frames = xprev.shape[0]
    copies = start_copies(((g_far, g), (x, band.at[0:frames])), sem)
    band[frames : 2 * frames] = xprev[...]
    limit = 2 * lengths[0] - 2 * frames * lax.axis_index("tm")
    copies[0].wait()
    for r in range(2):
        values = [g[f, r] for f in range(4)] + [gnext[f, r] for f in range(2)]
        field = [jnp.where(f < limit, v.astype(F32), 0.0) for f, v in enumerate(values)]
        for a in range(5):
            band[2 * frames + a, r] = (field[a] + field[a + 1]).astype(BF)
    copies[1].wait()


def packed(width, span):
    return (width, span) == (24, 81)


def silu_kernel(w_far, above, below, band, pay, xe, ps, w, sem):
    _, rows, cols, chan = band.shape
    frames = 2
    cells = frames * rows * cols
    peers = pay.shape[0]
    width = chan // peers
    copies = start_copies([(w_far, w)], sem)
    for f in range(2 * frames):
        slot = (f + frames) % (2 * frames) * 4
        xe[slot] = above[f, 1]
        xe[slot + 1 : slot + 3] = band[f]
        xe[slot + 3] = below[f, 0]
    ps[:, 0:EDGE, :] = jnp.zeros((10, EDGE, chan), F32)
    for a in range(5):
        for r in range(2):
            ps[a * 2 + r, EDGE : EDGE + cols, :] = band[4 + a, r].astype(F32)
    turned = [
        jnp.transpose(ps[2 * a : 2 * a + 2].reshape(2 * PITCH, chan)) for a in range(5)
    ]
    for p in range(peers):
        mine = jnp.concatenate([v[p * width : (p + 1) * width] for v in turned], axis=0)
        pay[p, cells + cells // 2 :, :] = mine.astype(BF)
    copies[0].wait()

    def patch(i, j):
        return blocks_of(xe, [(f + 2 - i) * 4 + j for f in range(2)], 2)

    hidden = conv(patch, w, plain_dot, 1, cols)
    act = hidden / (1.0 + jnp.exp(-hidden))
    half = cells // 2
    low = act[:, :128].astype(BF)
    high = jnp.concatenate([act[:half, 128:], act[half:, 128:]], axis=1).astype(BF)
    for p in range(peers):
        pay[p, 0:cells, :] = low
        pay[p, cells : cells + half, :] = high


def hidden_grad_kernel(w1_far, w2_far, above, below, own, tall, xe, pe, w1, w2, sem):
    _, rows, cols, chan = own.shape
    frames = 2
    copies = start_copies([(w1_far, w1), (w2_far, w2)], sem)
    for f in range(2 * frames + 5):
        target, slot = (xe, (f + frames) % (2 * frames) * 6) if f < 4 else (pe, (f - 4) * 6)
        target[slot : slot + 2] = above[f]
        target[slot + 2 : slot + 4] = own[f]
        target[slot + 4 : slot + 6] = below[f]
    for copy in copies:
        copy.wait()

    def patch(i, j):
        return blocks_of(xe, [(f + 2 - i) * 6 + j for f in range(2)], 4)

    def pair_patch(i, j):
        return blocks_of(pe, [(2 * t + i) * 6 + 2 - j for t in range(2)], 4)

    hidden = conv(patch, w1, plain_dot, 1, cols)
    pair = conv(pair_patch, w2, transposed_dot, -1, cols)
    sigma = 1.0 / (1.0 + jnp.exp(-hidden))
    grad = pair * sigma * (1.0 + hidden * (1.0 - sigma))
    grad = grad.reshape(frames, rows + 2, cols, chan)
    band = lax.axis_index("row")
    none = jnp.zeros((frames, cols, chan), F32)
    tall[:, 0] = jnp.where(band > 0, grad[:, 0], none).astype(BF)
    tall[:, 1 : 1 + rows] = grad[:, 1 : 1 + rows].astype(BF)
    last = band == lax.axis_size("row") - 1
    tall[:, 1 + rows] = jnp.where(last, none, grad[:, 1 + rows]).astype(BF)


def second_kernel(span, got, out, field, left, prod):
    peers = got.shape[0]
    cells = field.shape[0] // peers // (4 * PITCH) * 192
    half = cells // 2
    chan = field.shape[1]
    width = chan // peers
    cols = 48
    blocks, _, lanes = out.shape
    field[...] = jnp.zeros(field.shape, BF)
    low_lane = lax.broadcasted_iota(jnp.int32, (width, 128), 1) < PITCH
    for q in range(peers):
        low = got[q, 0:cells, :]
        high = got[q, cells : cells + half, :].astype(F32)
        high = [high[:, 0:64].astype(BF), high[:, 64:128].astype(BF)]
        for t in range(2):
            for r in range(2):
                at = ((t * peers + q) * 2 + r) * PITCH + EDGE
                field[at : at + cols, 0:128] = low[(t * 2 + r) * cols : (t * 2 + r + 1) * cols]
                field[at : at + cols, 128:192] = high[t][r * cols : (r + 1) * cols]
    base = cells + half
    for a in range(5):
        plain = [
            got[q, base + a * width : base + (a + 1) * width, :].astype(F32) for q in range(peers)
        ]
        swapped = [pltpu.roll(v, PITCH, 1) for v in plain]
        zero = jnp.zeros((width, 128), F32)
        ring = [zero] + swapped + [zero]
        for q in range(peers):
            rows_of = [
                jnp.where(low_lane, ring[q + 1], ring[q + 2]),
                plain[q],
                jnp.where(low_lane, ring[q], ring[q + 1]),
            ]
            for j in range(3):
                for k in range(3):
                    value = rows_of[j]
                    if k != 1:
                        value = pltpu.roll(value, 127 if k == 0 else 1, 1)
                    for t in range(2):
                        i = a - 2 * t
                        if 0 <= i < 3:
                            tap = i * 9 + j * 3 + k
                            at = (t * peers + q) * 128
                            left[tap * width : (tap + 1) * width, at : at + 128] = value
    prod[:, 192:256] = jnp.zeros((prod.shape[0], 64), F32)
    for i in range(3):
        rows = slice(i * 9 * width, (i + 1) * 9 * width)
        prod[rows, 0:192] = jnp.dot(
            left[rows, :].astype(BF), field[...], preferred_element_type=F32
        )
    lane = lax.broadcasted_iota(jnp.int32, (width, 256), 1)
    for b in range(blocks):
        pieces = []
        done = 0
        while done < span:
            tap, start = divmod(b * span + done, chan)
            size = min(span - done, chan - start)
            pieces.append((tap, start, size, done))
            done += size
        for chunk in range(0, lanes, 128):
            value = None
            for tap, start, size, at in pieces:
                if at + size <= chunk or at >= chunk + 128:
                    continue
                shift = (at - chunk - start) % 256
                part = prod[tap * width : (tap + 1) * width, :]
                if shift:
                    part = pltpu.roll(part, shift, 1)
                part = part[:, :128]
                if value is None:
                    value = part
                else:
                    value = jnp.where(lane[:, :128] < at - chunk, value, part)
            if value is None:
                value = jnp.zeros((width, 128), F32)
            if packed(width, span):
                tail = value[16:24]
                tail = jnp.concatenate([pltpu.roll(tail, 81, 1), pltpu.roll(tail, 40, 1)], axis=0)
                value = jnp.where(lane[:16, :128] < span, value[:16], tail)
            out[b, :, chunk : chunk + 128] = value.astype(BF)


def clip_kernel(got, out):
    total = got[0].astype(F32)
    for p in range(1, got.shape[0]):
        total += got[p].astype(F32)
    out[...] = total.astype(BF)


def last_kernel(scale, got, out):
    width, span = out.shape
    total = got[0].astype(F32)
    for p in range(1, got.shape[0]):
        total += got[p].astype(F32)
    total = total * scale
    if packed(width, span):
        lane = lax.broadcasted_iota(jnp.int32, (8, 128), 1)
        tail = jnp.where(lane < 41, pltpu.roll(total[:8], 47, 1), pltpu.roll(total[8:], 88, 1))
        out[:16] = total[:, :span]
        out[16:] = tail[:, :span]
    else:
        out[...] = total[:, :span]


def grad_kernel(w1_far, tall, after, grad, w1, sem):
    copies = start_copies([(w1_far, w1)], sem)
    frames, rows, cols, chan = grad.shape
    fields = [tall[0], tall[1], after[0], after[1]]

    def patch(i, j):
        value = jnp.concatenate([fields[f + i][2 - j : 4 - j] for f in range(2)], axis=0)
        return value.reshape(-1, chan)

    copies[0].wait()
    grad[...] = conv(patch, w1, transposed_dot, -1, cols).reshape(grad.shape)


def call(body, name, limit, shapes, args, scratch, far=(), scalars=(), sems=0):
    spaces = [pltpu.SMEM] * len(scalars) + [pltpu.HBM] * len(far) + [pltpu.VMEM] * len(args)
    far = [pltpu.with_memory_space_constraint(value, pltpu.HBM) for value in far]
    outs = [jax.ShapeDtypeStruct(shape, kind) for shape, kind in shapes]
    buffers = [pltpu.VMEM(shape, kind) for shape, kind in scratch]
    if sems:
        buffers.append(pltpu.SemaphoreType.DMA((sems,)))
    return pl.pallas_call(
        body,
        name=name,
        out_shape=outs,
        in_specs=[pl.BlockSpec(memory_space=space) for space in spaces],
        out_specs=[pl.BlockSpec(memory_space=pltpu.VMEM)] * len(outs),
        scratch_shapes=buffers,
        compiler_params=pltpu.CompilerParams(vmem_limit_bytes=limit * MIB),
    )(*scalars, *far, *args)


def local(clip_input, out_grad, weight_one, weight_two, lengths):
    frames, rows, cols, chan = clip_input.shape[1:]
    cells = frames * rows * cols
    peers = lax.axis_size("row")
    clips = lax.axis_size("clip")
    steps = lax.axis_size("tm")
    width = chan // peers
    x = clip_input[0]
    g = out_grad[0]
    w1 = weight_one.reshape(27, chan, chan)
    w2 = weight_two.reshape(27, chan, chan)

    xprev = move(x, ("tm",), (1,))
    gnext = move(g[:frames], ("tm",), (-1,))
    (band,) = call(
        band_kernel,
        "band",
        4,
        [((2 * frames + 5, rows, cols, chan), BF)],
        (xprev, gnext),
        [(g.shape, BF)],
        far=(x, g),
        scalars=(lengths,),
        sems=2,
    )
    above = move(band, ("row",), (1,))
    below = move(band, ("row",), (-1,))
    (pay,) = call(
        silu_kernel,
        "hidden_and_act",
        16,
        [((peers, cells + cells // 2 + 5 * width, 128), BF)],
        (above, below, band),
        [((16, cols, chan), BF), ((10, PITCH, chan), F32), (w1.shape, BF)],
        far=(w1,),
        sems=1,
    )
    got = lax.all_to_all(pay, "row", 0, 0)
    (tall,) = call(
        hidden_grad_kernel,
        "hidden_grad",
        28,
        [((frames, rows + 2, cols, chan), BF)],
        (above, below, band),
        [
            ((24, cols, chan), BF),
            ((30, cols, chan), BF),
            (w1.shape, BF),
            (w2.shape, BF),
        ],
        far=(w1, w2),
        sems=2,
    )
    after = move(tall, ("tm",), (-1,))

    blocks = clips * steps
    span = 27 * chan // blocks
    shape = (16, 128) if packed(width, span) else (width, (span + 127) // 128 * 128)
    (part,) = call(
        functools.partial(second_kernel, span),
        "kernel_grad_part",
        16,
        [((blocks,) + shape, BF)],
        (got,),
        [
            ((2 * peers * 2 * PITCH, chan), BF),
            ((27 * width, 2 * peers * 128), F32),
            ((27 * width, 256), F32),
        ],
    )
    part, after = lax.optimization_barrier((part, after))
    by_clip = lax.all_to_all(part.reshape((clips, steps * shape[0], shape[1])), "clip", 0, 0)
    (summed,) = call(
        clip_kernel,
        "clip_sum",
        4,
        [((steps * shape[0], shape[1]), BF)],
        (by_clip,),
        [],
    )
    by_step = lax.all_to_all(summed.reshape((steps,) + shape), "tm", 0, 0)
    total = clips * 2 * frames * steps * rows * peers * cols
    (kernel_grad,) = call(
        functools.partial(last_kernel, 1.0 / math.sqrt(total)),
        "kernel_grad_sum",
        4,
        [((width, span), F32)],
        (by_step,),
        [],
    )
    (input_grad,) = call(
        grad_kernel,
        "input_grad",
        16,
        [((frames, rows, cols, chan), F32)],
        (tall, after),
        [(w1.shape, BF)],
        far=(w1,),
        sems=1,
    )
    return (input_grad[None], kernel_grad.T)


def solution(mesh):
    return jax.shard_map(
        local,
        mesh=mesh,
        in_specs=(
            P("clip", "tm", "row", None, None),
            P("clip", "tm", "row", None, None),
            P(),
            P(),
            P("clip"),
        ),
        out_specs=(P("clip", "tm", "row", None, None), P(("clip", "tm"), "row")),
        check_vma=False,
    )
```

```python
import functools
import math

import jax
import jax.numpy as jnp
from jax import lax
from jax.experimental import pallas as pl
from jax.experimental.pallas import tpu as pltpu
from jax.sharding import PartitionSpec as P

BF = jnp.bfloat16
F32 = jnp.float32
EDGE = 16
PITCH = 64
MIB = 1024 * 1024


def route(sizes, steps):
    total = math.prod(sizes)
    pairs = []
    for source in range(total):
        index, rest = [], source
        for size in reversed(sizes):
            index.append(rest % size)
            rest //= size
        index = index[::-1]
        there = [a + b for a, b in zip(index, steps)]
        if all(0 <= a < size for a, size in zip(there, sizes)):
            target = 0
            for a, size in zip(there, sizes):
                target = target * size + a
            pairs.append((source, target))
    return pairs


def move(value, axes, steps):
    sizes = [lax.axis_size(axis) for axis in axes]
    return lax.ppermute(value, axes if len(axes) > 1 else axes[0], route(sizes, steps))


def transposed_dot(a, b):
    return lax.dot_general(a, b, (((1,), (1,)), ((), ())), preferred_element_type=F32)


def plain_dot(a, b):
    return jnp.dot(a, b, preferred_element_type=F32)


def column_shift(value, by, cols):
    cells, chan = value.shape
    moved = pltpu.roll(value, by % cells, 0).reshape(cells // cols, cols, chan)
    column = lax.broadcasted_iota(jnp.int32, moved.shape, 1)
    moved = jnp.where(column == (0 if by > 0 else cols - 1), 0.0, moved)
    return moved.reshape(cells, chan)


def conv(patch, weight, dot, first_shift, cols, row_taps=(0, 1, 2)):
    total = None
    for k in (1, 0, 2):
        part = None
        for i in range(3):
            for j in row_taps:
                term = dot(patch(i, j), weight[i * 9 + j * 3 + k])
                part = term if part is None else part + term
        if k != 1:
            part = column_shift(part, first_shift if k == 0 else -first_shift, cols)
        total = part if total is None else total + part
    return total


def blocks_of(ref, starts, count):
    value = jnp.concatenate([ref[at : at + count] for at in starts], axis=0)
    return value.reshape(-1, value.shape[-1])


def start_copies(pairs, sem):
    copies = [pltpu.make_async_copy(a, b, sem.at[n]) for n, (a, b) in enumerate(pairs)]
    for copy in copies:
        copy.start()
    return copies


def band_kernel(lengths, x, g_far, xprev, gnext, band, g, sem):
    frames = xprev.shape[0]
    copies = start_copies(((g_far, g), (x, band.at[0:frames])), sem)
    band[frames : 2 * frames] = xprev[...]
    limit = 2 * lengths[0] - 2 * frames * lax.axis_index("tm")
    copies[0].wait()
    for r in range(2):
        values = [g[f, r] for f in range(4)] + [gnext[f, r] for f in range(2)]
        field = [jnp.where(f < limit, v.astype(F32), 0.0) for f, v in enumerate(values)]
        for a in range(5):
            band[2 * frames + a, r] = (field[a] + field[a + 1]).astype(BF)
    copies[1].wait()


def packed(width, span):
    return (width, span) == (24, 81)


def own_kernel(w_far, band, turned, part, w, xe, ps, sem):
    _, rows, cols, chan = band.shape
    frames = 2
    peers = turned.shape[0]
    width = chan // peers
    copies = start_copies([(w_far, w)], sem)
    none = jnp.zeros((cols, chan), BF)
    for f in range(2 * frames):
        slot = (f + frames) % (2 * frames) * 4
        xe[slot] = none
        xe[slot + 1 : slot + 3] = band[f]
        xe[slot + 3] = none
    ps[:, 0:EDGE, :] = jnp.zeros((10, EDGE, chan), F32)
    for a in range(5):
        for r in range(2):
            ps[a * 2 + r, EDGE : EDGE + cols, :] = band[4 + a, r].astype(F32)
    fields = [jnp.transpose(ps[2 * a : 2 * a + 2].reshape(2 * PITCH, chan)) for a in range(5)]
    for p in range(peers):
        mine = jnp.concatenate([v[p * width : (p + 1) * width] for v in fields], axis=0)
        turned[p] = mine.astype(BF)
    copies[0].wait()

    def patch(i, j):
        return blocks_of(xe, [(f + 2 - i) * 4 + j for f in range(2)], 2)

    part[...] = conv(patch, w, plain_dot, 1, cols)


def silu_kernel(turned, w, part, above, below, pay, own, sem):
    _, rows, cols, chan = above.shape
    frames = 2
    cells = frames * rows * cols
    half = cells // 2
    peers = pay.shape[0]
    copies = [pltpu.make_async_copy(turned, pay.at[:, cells + half :], sem.at[peers])]
    copies[0].start()

    def top_patch(i, j):
        frame = [above[(f + 2 - i + frames) % (2 * frames), 1] for f in range(2)]
        return jnp.concatenate(frame, axis=0)

    def bottom_patch(i, j):
        frame = [below[(f + 2 - i + frames) % (2 * frames), 0] for f in range(2)]
        return jnp.concatenate(frame, axis=0)

    top = conv(top_patch, w, plain_dot, 1, cols, (0,)).reshape(frames, 1, cols, chan)
    bottom = conv(bottom_patch, w, plain_dot, 1, cols, (2,)).reshape(frames, 1, cols, chan)
    hidden = part[...] + jnp.concatenate([top, bottom], axis=1).reshape(cells, chan)
    act = hidden / (1.0 + jnp.exp(-hidden))
    own[0:cells] = act[:, :128].astype(BF)
    own[cells:] = jnp.concatenate([act[:half, 128:], act[half:, 128:]], axis=1).astype(BF)
    for p in range(peers):
        copies.append(pltpu.make_async_copy(own, pay.at[p, 0 : cells + half], sem.at[p]))
        copies[-1].start()
    for copy in copies:
        copy.wait()


def hidden_grad_kernel(w2_far, w1, above, below, own, tall, xe, pe, w2, sem):
    _, rows, cols, chan = own.shape
    frames = 2
    copies = start_copies([(w2_far, w2)], sem)
    for f in range(2 * frames + 5):
        target, slot = (xe, (f + frames) % (2 * frames) * 6) if f < 4 else (pe, (f - 4) * 6)
        target[slot : slot + 2] = above[f]
        target[slot + 2 : slot + 4] = own[f]
        target[slot + 4 : slot + 6] = below[f]
    for copy in copies:
        copy.wait()

    def patch(i, j):
        return blocks_of(xe, [(f + 2 - i) * 6 + j for f in range(2)], 4)

    def pair_patch(i, j):
        return blocks_of(pe, [(2 * t + i) * 6 + 2 - j for t in range(2)], 4)

    hidden = conv(patch, w1, plain_dot, 1, cols)
    pair = conv(pair_patch, w2, transposed_dot, -1, cols)
    sigma = 1.0 / (1.0 + jnp.exp(-hidden))
    grad = pair * sigma * (1.0 + hidden * (1.0 - sigma))
    grad = grad.reshape(frames, rows + 2, cols, chan)
    band = lax.axis_index("row")
    none = jnp.zeros((frames, cols, chan), F32)
    tall[:, 0] = jnp.where(band > 0, grad[:, 0], none).astype(BF)
    tall[:, 1 : 1 + rows] = grad[:, 1 : 1 + rows].astype(BF)
    last = band == lax.axis_size("row") - 1
    tall[:, 1 + rows] = jnp.where(last, none, grad[:, 1 + rows]).astype(BF)


def second_kernel(span, got, out, field, left, prod):
    peers = got.shape[0]
    cells = field.shape[0] // peers // (4 * PITCH) * 192
    half = cells // 2
    chan = field.shape[1]
    width = chan // peers
    cols = 48
    blocks, _, lanes = out.shape
    field[...] = jnp.zeros(field.shape, BF)
    low_lane = lax.broadcasted_iota(jnp.int32, (width, 128), 1) < PITCH
    for q in range(peers):
        low = got[q, 0:cells, :]
        high = got[q, cells : cells + half, :].astype(F32)
        high = [high[:, 0:64].astype(BF), high[:, 64:128].astype(BF)]
        for t in range(2):
            for r in range(2):
                at = ((t * peers + q) * 2 + r) * PITCH + EDGE
                field[at : at + cols, 0:128] = low[(t * 2 + r) * cols : (t * 2 + r + 1) * cols]
                field[at : at + cols, 128:192] = high[t][r * cols : (r + 1) * cols]
    base = cells + half
    for a in range(5):
        plain = [
            got[q, base + a * width : base + (a + 1) * width, :].astype(F32) for q in range(peers)
        ]
        swapped = [pltpu.roll(v, PITCH, 1) for v in plain]
        zero = jnp.zeros((width, 128), F32)
        ring = [zero] + swapped + [zero]
        for q in range(peers):
            rows_of = [
                jnp.where(low_lane, ring[q + 1], ring[q + 2]),
                plain[q],
                jnp.where(low_lane, ring[q], ring[q + 1]),
            ]
            for j in range(3):
                for k in range(3):
                    value = rows_of[j]
                    if k != 1:
                        value = pltpu.roll(value, 127 if k == 0 else 1, 1)
                    for t in range(2):
                        i = a - 2 * t
                        if 0 <= i < 3:
                            tap = i * 9 + j * 3 + k
                            at = (t * peers + q) * 128
                            left[tap * width : (tap + 1) * width, at : at + 128] = value
    prod[:, 192:256] = jnp.zeros((prod.shape[0], 64), F32)
    for i in range(3):
        rows = slice(i * 9 * width, (i + 1) * 9 * width)
        prod[rows, 0:192] = jnp.dot(
            left[rows, :].astype(BF), field[...], preferred_element_type=F32
        )
    lane = lax.broadcasted_iota(jnp.int32, (width, 256), 1)
    for b in range(blocks):
        pieces = []
        done = 0
        while done < span:
            tap, start = divmod(b * span + done, chan)
            size = min(span - done, chan - start)
            pieces.append((tap, start, size, done))
            done += size
        for chunk in range(0, lanes, 128):
            value = None
            for tap, start, size, at in pieces:
                if at + size <= chunk or at >= chunk + 128:
                    continue
                shift = (at - chunk - start) % 256
                part = prod[tap * width : (tap + 1) * width, :]
                if shift:
                    part = pltpu.roll(part, shift, 1)
                part = part[:, :128]
                if value is None:
                    value = part
                else:
                    value = jnp.where(lane[:, :128] < at - chunk, value, part)
            if value is None:
                value = jnp.zeros((width, 128), F32)
            if packed(width, span):
                tail = value[16:24]
                tail = jnp.concatenate([pltpu.roll(tail, 81, 1), pltpu.roll(tail, 40, 1)], axis=0)
                value = jnp.where(lane[:16, :128] < span, value[:16], tail)
            out[b, :, chunk : chunk + 128] = value.astype(BF)


def clip_kernel(got, out):
    total = got[0].astype(F32)
    for p in range(1, got.shape[0]):
        total += got[p].astype(F32)
    out[...] = total.astype(BF)


def last_kernel(scale, got, out):
    width, span = out.shape
    total = got[0].astype(F32)
    for p in range(1, got.shape[0]):
        total += got[p].astype(F32)
    total = total * scale
    if packed(width, span):
        lane = lax.broadcasted_iota(jnp.int32, (8, 128), 1)
        tail = jnp.where(lane < 41, pltpu.roll(total[:8], 47, 1), pltpu.roll(total[8:], 88, 1))
        out[:16] = total[:, :span]
        out[16:] = tail[:, :span]
    else:
        out[...] = total[:, :span]


def grad_kernel(w1_far, tall, after, grad, w1, sem):
    copies = start_copies([(w1_far, w1)], sem)
    frames, rows, cols, chan = grad.shape
    fields = [tall[0], tall[1], after[0], after[1]]

    def patch(i, j):
        value = jnp.concatenate([fields[f + i][2 - j : 4 - j] for f in range(2)], axis=0)
        return value.reshape(-1, chan)

    copies[0].wait()
    grad[...] = conv(patch, w1, transposed_dot, -1, cols).reshape(grad.shape)


def call(body, name, limit, shapes, args, scratch, far=(), scalars=(), sems=0, out_far=False):
    spaces = [pltpu.SMEM] * len(scalars) + [pltpu.HBM] * len(far) + [pltpu.VMEM] * len(args)
    far = [pltpu.with_memory_space_constraint(value, pltpu.HBM) for value in far]
    made = pltpu.HBM if out_far else jax.ShapeDtypeStruct
    outs = [made(shape, kind) for shape, kind in shapes]
    buffers = [pltpu.VMEM(shape, kind) for shape, kind in scratch]
    if sems:
        buffers.append(pltpu.SemaphoreType.DMA((sems,)))
    return pl.pallas_call(
        body,
        name=name,
        out_shape=outs,
        in_specs=[pl.BlockSpec(memory_space=space) for space in spaces],
        out_specs=[pl.BlockSpec(memory_space=pltpu.HBM if out_far else pltpu.VMEM)] * len(outs),
        scratch_shapes=buffers,
        compiler_params=pltpu.CompilerParams(vmem_limit_bytes=limit * MIB),
    )(*scalars, *far, *args)


def local(clip_input, out_grad, weight_one, weight_two, lengths):
    frames, rows, cols, chan = clip_input.shape[1:]
    cells = frames * rows * cols
    peers = lax.axis_size("row")
    clips = lax.axis_size("clip")
    steps = lax.axis_size("tm")
    width = chan // peers
    x = clip_input[0]
    g = out_grad[0]
    w1 = weight_one.reshape(27, chan, chan)
    w2 = weight_two.reshape(27, chan, chan)

    xprev = move(x, ("tm",), (1,))
    gnext = move(g[:frames], ("tm",), (-1,))
    (band,) = call(
        band_kernel,
        "band",
        4,
        [((2 * frames + 5, rows, cols, chan), BF)],
        (xprev, gnext),
        [(g.shape, BF)],
        far=(x, g),
        scalars=(lengths,),
        sems=2,
    )
    above = move(band, ("row",), (1,))
    below = move(band, ("row",), (-1,))
    turned, own_part, w1_near = call(
        own_kernel,
        "own_rows",
        8,
        [((peers, 5 * width, 128), BF), ((cells, chan), F32), (w1.shape, BF)],
        (band,),
        [((16, cols, chan), BF), ((10, PITCH, chan), F32)],
        far=(w1,),
        sems=1,
    )
    (pay,) = call(
        silu_kernel,
        "hidden_and_act",
        4,
        [((peers, cells + cells // 2 + 5 * width, 128), BF)],
        (turned, w1_near, own_part, above, below),
        [((cells + cells // 2, 128), BF)],
        sems=peers + 1,
        out_far=True,
    )
    got = lax.all_to_all(pay, "row", 0, 0)
    (tall,) = call(
        hidden_grad_kernel,
        "hidden_grad",
        14,
        [((frames, rows + 2, cols, chan), BF)],
        (w1_near, above, below, band),
        [((24, cols, chan), BF), ((30, cols, chan), BF), (w2.shape, BF)],
        far=(w2,),
        sems=1,
    )
    after = move(tall, ("tm",), (-1,))

    blocks = clips * steps
    span = 27 * chan // blocks
    shape = (16, 128) if packed(width, span) else (width, (span + 127) // 128 * 128)
    (part,) = call(
        functools.partial(second_kernel, span),
        "kernel_grad_part",
        13,
        [((blocks,) + shape, BF)],
        (got,),
        [
            ((2 * peers * 2 * PITCH, chan), BF),
            ((27 * width, 2 * peers * 128), F32),
            ((27 * width, 256), F32),
        ],
    )
    part, after = lax.optimization_barrier((part, after))
    by_clip = lax.all_to_all(part.reshape((clips, steps * shape[0], shape[1])), "clip", 0, 0)
    (summed,) = call(
        clip_kernel,
        "clip_sum",
        4,
        [((steps * shape[0], shape[1]), BF)],
        (by_clip,),
        [],
    )
    by_step = lax.all_to_all(summed.reshape((steps,) + shape), "tm", 0, 0)
    total = clips * 2 * frames * steps * rows * peers * cols
    (kernel_grad,) = call(
        functools.partial(last_kernel, 1.0 / math.sqrt(total)),
        "kernel_grad_sum",
        4,
        [((width, span), F32)],
        (by_step,),
        [],
    )
    (input_grad,) = call(
        grad_kernel,
        "input_grad",
        8,
        [((frames, rows, cols, chan), F32)],
        (tall, after),
        [(w1.shape, BF)],
        far=(w1,),
        sems=1,
    )
    return (input_grad[None], kernel_grad.T)


def solution(mesh):
    return jax.shard_map(
        local,
        mesh=mesh,
        in_specs=(
            P("clip", "tm", "row", None, None),
            P("clip", "tm", "row", None, None),
            P(),
            P(),
            P("clip"),
        ),
        out_specs=(P("clip", "tm", "row", None, None), P(("clip", "tm"), "row")),
        check_vma=False,
    )
```

```python
import functools
import math

import jax
import jax.numpy as jnp
from jax import lax
from jax.experimental import pallas as pl
from jax.experimental.pallas import tpu as pltpu
from jax.sharding import PartitionSpec as P

BF = jnp.bfloat16
F32 = jnp.float32
EDGE = 16
PITCH = 64
MIB = 1024 * 1024


def route(sizes, steps):
    total = math.prod(sizes)
    pairs = []
    for source in range(total):
        index, rest = [], source
        for size in reversed(sizes):
            index.append(rest % size)
            rest //= size
        index = index[::-1]
        there = [a + b for a, b in zip(index, steps)]
        if all(0 <= a < size for a, size in zip(there, sizes)):
            target = 0
            for a, size in zip(there, sizes):
                target = target * size + a
            pairs.append((source, target))
    return pairs


def move(value, axes, steps):
    sizes = [lax.axis_size(axis) for axis in axes]
    return lax.ppermute(value, axes if len(axes) > 1 else axes[0], route(sizes, steps))


def transposed_dot(a, b):
    return lax.dot_general(a, b, (((1,), (1,)), ((), ())), preferred_element_type=F32)


def plain_dot(a, b):
    return jnp.dot(a, b, preferred_element_type=F32)


def column_shift(value, by, cols):
    cells, chan = value.shape
    moved = pltpu.roll(value, by % cells, 0).reshape(cells // cols, cols, chan)
    column = lax.broadcasted_iota(jnp.int32, moved.shape, 1)
    moved = jnp.where(column == (0 if by > 0 else cols - 1), 0.0, moved)
    return moved.reshape(cells, chan)


def conv(patch, weight, dot, first_shift, cols, row_taps=(0, 1, 2)):
    total = None
    for k in (1, 0, 2):
        part = None
        for i in range(3):
            for j in row_taps:
                term = dot(patch(i, j), weight[i * 9 + j * 3 + k])
                part = term if part is None else part + term
        if k != 1:
            part = column_shift(part, first_shift if k == 0 else -first_shift, cols)
        total = part if total is None else total + part
    return total


def blocks_of(ref, starts, count):
    value = jnp.concatenate([ref[at : at + count] for at in starts], axis=0)
    return value.reshape(-1, value.shape[-1])


def start_copies(pairs, sem):
    copies = [pltpu.make_async_copy(a, b, sem.at[n]) for n, (a, b) in enumerate(pairs)]
    for copy in copies:
        copy.start()
    return copies


def band_kernel(lengths, x, g_far, xprev, gnext, band, g, sem):
    frames = xprev.shape[0]
    copies = start_copies(((g_far, g), (x, band.at[0:frames])), sem)
    band[frames : 2 * frames] = xprev[...]
    limit = 2 * lengths[0] - 2 * frames * lax.axis_index("tm")
    copies[0].wait()
    for r in range(2):
        values = [g[f, r] for f in range(4)] + [gnext[f, r] for f in range(2)]
        field = [jnp.where(f < limit, v.astype(F32), 0.0) for f, v in enumerate(values)]
        for a in range(5):
            band[2 * frames + a, r] = (field[a] + field[a + 1]).astype(BF)
    copies[1].wait()


def packed(width, span):
    return (width, span) == (24, 81)


def own_kernel(w_far, band, turned, part, w, xe, ps, sem):
    _, rows, cols, chan = band.shape
    frames = 2
    peers = turned.shape[0]
    width = chan // peers
    copies = start_copies([(w_far, w)], sem)
    none = jnp.zeros((cols, chan), BF)
    for f in range(2 * frames):
        slot = (f + frames) % (2 * frames) * 4
        xe[slot] = none
        xe[slot + 1 : slot + 3] = band[f]
        xe[slot + 3] = none
    ps[:, 0:EDGE, :] = jnp.zeros((10, EDGE, chan), F32)
    for a in range(5):
        for r in range(2):
            ps[a * 2 + r, EDGE : EDGE + cols, :] = band[4 + a, r].astype(F32)
    fields = [jnp.transpose(ps[2 * a : 2 * a + 2].reshape(2 * PITCH, chan)) for a in range(5)]
    for p in range(peers):
        mine = jnp.concatenate([v[p * width : (p + 1) * width] for v in fields], axis=0)
        turned[p] = mine.astype(BF)
    copies[0].wait()

    def patch(i, j):
        return blocks_of(xe, [(f + 2 - i) * 4 + j for f in range(2)], 2)

    part[...] = conv(patch, w, plain_dot, 1, cols)


def silu_kernel(turned, w, part, above, below, pay, own, sem):
    _, rows, cols, chan = above.shape
    frames = 2
    cells = frames * rows * cols
    half = cells // 2
    peers = pay.shape[0]
    copies = [pltpu.make_async_copy(turned, pay.at[:, cells + half :], sem.at[peers])]
    copies[0].start()

    def top_patch(i, j):
        frame = [above[(f + 2 - i + frames) % (2 * frames), 1] for f in range(2)]
        return jnp.concatenate(frame, axis=0)

    def bottom_patch(i, j):
        frame = [below[(f + 2 - i + frames) % (2 * frames), 0] for f in range(2)]
        return jnp.concatenate(frame, axis=0)

    top = conv(top_patch, w, plain_dot, 1, cols, (0,)).reshape(frames, 1, cols, chan)
    bottom = conv(bottom_patch, w, plain_dot, 1, cols, (2,)).reshape(frames, 1, cols, chan)
    hidden = part[...] + jnp.concatenate([top, bottom], axis=1).reshape(cells, chan)
    act = hidden / (1.0 + jnp.exp(-hidden))
    own[0:cells] = act[:, :128].astype(BF)
    own[cells:] = jnp.concatenate([act[:half, 128:], act[half:, 128:]], axis=1).astype(BF)
    for p in range(peers):
        copies.append(pltpu.make_async_copy(own, pay.at[p, 0 : cells + half], sem.at[p]))
        copies[-1].start()
    for copy in copies:
        copy.wait()


def hidden_grad_kernel(w1_far, w2_far, above, below, own, tall, xe, pe, w1, w2, sem):
    _, rows, cols, chan = own.shape
    frames = 2
    copies = start_copies([(w1_far, w1), (w2_far, w2)], sem)
    for f in range(2 * frames + 5):
        target, slot = (xe, (f + frames) % (2 * frames) * 6) if f < 4 else (pe, (f - 4) * 6)
        target[slot : slot + 2] = above[f]
        target[slot + 2 : slot + 4] = own[f]
        target[slot + 4 : slot + 6] = below[f]
    for copy in copies:
        copy.wait()

    def patch(i, j):
        return blocks_of(xe, [(f + 2 - i) * 6 + j for f in range(2)], 4)

    def pair_patch(i, j):
        return blocks_of(pe, [(2 * t + i) * 6 + 2 - j for t in range(2)], 4)

    hidden = conv(patch, w1, plain_dot, 1, cols)
    pair = conv(pair_patch, w2, transposed_dot, -1, cols)
    sigma = 1.0 / (1.0 + jnp.exp(-hidden))
    grad = pair * sigma * (1.0 + hidden * (1.0 - sigma))
    grad = grad.reshape(frames, rows + 2, cols, chan)
    band = lax.axis_index("row")
    none = jnp.zeros((frames, cols, chan), F32)
    tall[:, 0] = jnp.where(band > 0, grad[:, 0], none).astype(BF)
    tall[:, 1 : 1 + rows] = grad[:, 1 : 1 + rows].astype(BF)
    last = band == lax.axis_size("row") - 1
    tall[:, 1 + rows] = jnp.where(last, none, grad[:, 1 + rows]).astype(BF)


def second_kernel(span, got, out, field, left, prod):
    peers = got.shape[0]
    cells = field.shape[0] // peers // (4 * PITCH) * 192
    half = cells // 2
    chan = field.shape[1]
    width = chan // peers
    cols = 48
    blocks, _, lanes = out.shape
    field[...] = jnp.zeros(field.shape, BF)
    low_lane = lax.broadcasted_iota(jnp.int32, (width, 128), 1) < PITCH
    for q in range(peers):
        low = got[q, 0:cells, :]
        high = got[q, cells : cells + half, :].astype(F32)
        high = [high[:, 0:64].astype(BF), high[:, 64:128].astype(BF)]
        for t in range(2):
            for r in range(2):
                at = ((t * peers + q) * 2 + r) * PITCH + EDGE
                field[at : at + cols, 0:128] = low[(t * 2 + r) * cols : (t * 2 + r + 1) * cols]
                field[at : at + cols, 128:192] = high[t][r * cols : (r + 1) * cols]
    base = cells + half
    for a in range(5):
        plain = [
            got[q, base + a * width : base + (a + 1) * width, :].astype(F32) for q in range(peers)
        ]
        swapped = [pltpu.roll(v, PITCH, 1) for v in plain]
        zero = jnp.zeros((width, 128), F32)
        ring = [zero] + swapped + [zero]
        for q in range(peers):
            rows_of = [
                jnp.where(low_lane, ring[q + 1], ring[q + 2]),
                plain[q],
                jnp.where(low_lane, ring[q], ring[q + 1]),
            ]
            for j in range(3):
                for k in range(3):
                    value = rows_of[j]
                    if k != 1:
                        value = pltpu.roll(value, 127 if k == 0 else 1, 1)
                    for t in range(2):
                        i = a - 2 * t
                        if 0 <= i < 3:
                            tap = i * 9 + j * 3 + k
                            at = (t * peers + q) * 128
                            left[tap * width : (tap + 1) * width, at : at + 128] = value
    prod[:, 192:256] = jnp.zeros((prod.shape[0], 64), F32)
    for i in range(3):
        rows = slice(i * 9 * width, (i + 1) * 9 * width)
        prod[rows, 0:192] = jnp.dot(
            left[rows, :].astype(BF), field[...], preferred_element_type=F32
        )
    lane = lax.broadcasted_iota(jnp.int32, (width, 256), 1)
    for b in range(blocks):
        pieces = []
        done = 0
        while done < span:
            tap, start = divmod(b * span + done, chan)
            size = min(span - done, chan - start)
            pieces.append((tap, start, size, done))
            done += size
        for chunk in range(0, lanes, 128):
            value = None
            for tap, start, size, at in pieces:
                if at + size <= chunk or at >= chunk + 128:
                    continue
                shift = (at - chunk - start) % 256
                part = prod[tap * width : (tap + 1) * width, :]
                if shift:
                    part = pltpu.roll(part, shift, 1)
                part = part[:, :128]
                if value is None:
                    value = part
                else:
                    value = jnp.where(lane[:, :128] < at - chunk, value, part)
            if value is None:
                value = jnp.zeros((width, 128), F32)
            if packed(width, span):
                tail = value[16:24]
                tail = jnp.concatenate([pltpu.roll(tail, 81, 1), pltpu.roll(tail, 40, 1)], axis=0)
                value = jnp.where(lane[:16, :128] < span, value[:16], tail)
            out[b, :, chunk : chunk + 128] = value.astype(BF)


def clip_kernel(got, out):
    total = got[0].astype(F32)
    for p in range(1, got.shape[0]):
        total += got[p].astype(F32)
    out[...] = total.astype(BF)


def last_kernel(scale, got, out):
    width, span = out.shape
    total = got[0].astype(F32)
    for p in range(1, got.shape[0]):
        total += got[p].astype(F32)
    total = total * scale
    if packed(width, span):
        lane = lax.broadcasted_iota(jnp.int32, (8, 128), 1)
        tail = jnp.where(lane < 41, pltpu.roll(total[:8], 47, 1), pltpu.roll(total[8:], 88, 1))
        out[:16] = total[:, :span]
        out[16:] = tail[:, :span]
    else:
        out[...] = total[:, :span]


def grad_kernel(w1_far, tall, after, grad, w1, sem):
    copies = start_copies([(w1_far, w1)], sem)
    frames, rows, cols, chan = grad.shape
    fields = [tall[0], tall[1], after[0], after[1]]

    def patch(i, j):
        value = jnp.concatenate([fields[f + i][2 - j : 4 - j] for f in range(2)], axis=0)
        return value.reshape(-1, chan)

    copies[0].wait()
    grad[...] = conv(patch, w1, transposed_dot, -1, cols).reshape(grad.shape)


def call(body, name, limit, shapes, args, scratch, far=(), scalars=(), sems=0, out_far=False):
    spaces = [pltpu.SMEM] * len(scalars) + [pltpu.HBM] * len(far) + [pltpu.VMEM] * len(args)
    far = [pltpu.with_memory_space_constraint(value, pltpu.HBM) for value in far]
    made = pltpu.HBM if out_far else jax.ShapeDtypeStruct
    outs = [made(shape, kind) for shape, kind in shapes]
    buffers = [pltpu.VMEM(shape, kind) for shape, kind in scratch]
    if sems:
        buffers.append(pltpu.SemaphoreType.DMA((sems,)))
    return pl.pallas_call(
        body,
        name=name,
        out_shape=outs,
        in_specs=[pl.BlockSpec(memory_space=space) for space in spaces],
        out_specs=[pl.BlockSpec(memory_space=pltpu.HBM if out_far else pltpu.VMEM)] * len(outs),
        scratch_shapes=buffers,
        compiler_params=pltpu.CompilerParams(vmem_limit_bytes=limit * MIB),
    )(*scalars, *far, *args)


def local(clip_input, out_grad, weight_one, weight_two, lengths):
    frames, rows, cols, chan = clip_input.shape[1:]
    cells = frames * rows * cols
    peers = lax.axis_size("row")
    clips = lax.axis_size("clip")
    steps = lax.axis_size("tm")
    width = chan // peers
    x = clip_input[0]
    g = out_grad[0]
    w1 = weight_one.reshape(27, chan, chan)
    w2 = weight_two.reshape(27, chan, chan)

    xprev = move(x, ("tm",), (1,))
    gnext = move(g[:frames], ("tm",), (-1,))
    (band,) = call(
        band_kernel,
        "band",
        4,
        [((2 * frames + 5, rows, cols, chan), BF)],
        (xprev, gnext),
        [(g.shape, BF)],
        far=(x, g),
        scalars=(lengths,),
        sems=2,
    )
    above = move(band, ("row",), (1,))
    below = move(band, ("row",), (-1,))
    turned, own_part, w1_near = call(
        own_kernel,
        "own_rows",
        8,
        [((peers, 5 * width, 128), BF), ((cells, chan), F32), (w1.shape, BF)],
        (band,),
        [((16, cols, chan), BF), ((10, PITCH, chan), F32)],
        far=(w1,),
        sems=1,
    )
    (pay,) = call(
        silu_kernel,
        "hidden_and_act",
        4,
        [((peers, cells + cells // 2 + 5 * width, 128), BF)],
        (turned, w1_near, own_part, above, below),
        [((cells + cells // 2, 128), BF)],
        sems=peers + 1,
        out_far=True,
    )
    got = lax.all_to_all(pay, "row", 0, 0)
    (tall,) = call(
        hidden_grad_kernel,
        "hidden_grad",
        14,
        [((frames, rows + 2, cols, chan), BF)],
        (above, below, band),
        [
            ((24, cols, chan), BF),
            ((30, cols, chan), BF),
            (w1.shape, BF),
            (w2.shape, BF),
        ],
        far=(w1, w2),
        sems=2,
    )
    after = move(tall, ("tm",), (-1,))

    blocks = clips * steps
    span = 27 * chan // blocks
    shape = (16, 128) if packed(width, span) else (width, (span + 127) // 128 * 128)
    (part,) = call(
        functools.partial(second_kernel, span),
        "kernel_grad_part",
        13,
        [((blocks,) + shape, BF)],
        (got,),
        [
            ((2 * peers * 2 * PITCH, chan), BF),
            ((27 * width, 2 * peers * 128), F32),
            ((27 * width, 256), F32),
        ],
    )
    part, after = lax.optimization_barrier((part, after))
    by_clip = lax.all_to_all(part.reshape((clips, steps * shape[0], shape[1])), "clip", 0, 0)
    (summed,) = call(
        clip_kernel,
        "clip_sum",
        4,
        [((steps * shape[0], shape[1]), BF)],
        (by_clip,),
        [],
    )
    by_step = lax.all_to_all(summed.reshape((steps,) + shape), "tm", 0, 0)
    total = clips * 2 * frames * steps * rows * peers * cols
    (kernel_grad,) = call(
        functools.partial(last_kernel, 1.0 / math.sqrt(total)),
        "kernel_grad_sum",
        4,
        [((width, span), F32)],
        (by_step,),
        [],
    )
    (input_grad,) = call(
        grad_kernel,
        "input_grad",
        8,
        [((frames, rows, cols, chan), F32)],
        (tall, after),
        [(w1.shape, BF)],
        far=(w1,),
        sems=1,
    )
    return (input_grad[None], kernel_grad.T)


def solution(mesh):
    return jax.shard_map(
        local,
        mesh=mesh,
        in_specs=(
            P("clip", "tm", "row", None, None),
            P("clip", "tm", "row", None, None),
            P(),
            P(),
            P("clip"),
        ),
        out_specs=(P("clip", "tm", "row", None, None), P(("clip", "tm"), "row")),
        check_vma=False,
    )
```

```python
import functools
import math

import jax
import jax.numpy as jnp
from jax import lax
from jax.experimental import pallas as pl
from jax.experimental.pallas import tpu as pltpu
from jax.sharding import PartitionSpec as P

BF = jnp.bfloat16
F32 = jnp.float32
EDGE = 16
PITCH = 64
MIB = 1024 * 1024


def route(sizes, steps):
    total = math.prod(sizes)
    pairs = []
    for source in range(total):
        index, rest = [], source
        for size in reversed(sizes):
            index.append(rest % size)
            rest //= size
        index = index[::-1]
        there = [a + b for a, b in zip(index, steps)]
        if all(0 <= a < size for a, size in zip(there, sizes)):
            target = 0
            for a, size in zip(there, sizes):
                target = target * size + a
            pairs.append((source, target))
    return pairs


def move(value, axes, steps):
    sizes = [lax.axis_size(axis) for axis in axes]
    return lax.ppermute(value, axes if len(axes) > 1 else axes[0], route(sizes, steps))


def transposed_dot(a, b):
    return lax.dot_general(a, b, (((1,), (1,)), ((), ())), preferred_element_type=F32)


def plain_dot(a, b):
    return jnp.dot(a, b, preferred_element_type=F32)


def column_shift(value, by, cols):
    cells, chan = value.shape
    moved = pltpu.roll(value, by % cells, 0).reshape(cells // cols, cols, chan)
    column = lax.broadcasted_iota(jnp.int32, moved.shape, 1)
    moved = jnp.where(column == (0 if by > 0 else cols - 1), 0.0, moved)
    return moved.reshape(cells, chan)


def conv(patch, weight, dot, first_shift, cols, row_taps=(0, 1, 2)):
    total = None
    for k in (1, 0, 2):
        part = None
        for i in range(3):
            for j in row_taps:
                term = dot(patch(i, j), weight[i * 9 + j * 3 + k])
                part = term if part is None else part + term
        if k != 1:
            part = column_shift(part, first_shift if k == 0 else -first_shift, cols)
        total = part if total is None else total + part
    return total


def blocks_of(ref, starts, count):
    value = jnp.concatenate([ref[at : at + count] for at in starts], axis=0)
    return value.reshape(-1, value.shape[-1])


def start_copies(pairs, sem):
    copies = [pltpu.make_async_copy(a, b, sem.at[n]) for n, (a, b) in enumerate(pairs)]
    for copy in copies:
        copy.start()
    return copies


def band_kernel(lengths, x, g_far, xprev, gnext, band, g, sem):
    frames = xprev.shape[0]
    copies = start_copies(((g_far, g), (x, band.at[0:frames])), sem)
    band[frames : 2 * frames] = xprev[...]
    limit = 2 * lengths[0] - 2 * frames * lax.axis_index("tm")
    copies[0].wait()
    for r in range(2):
        values = [g[f, r] for f in range(4)] + [gnext[f, r] for f in range(2)]
        field = [jnp.where(f < limit, v.astype(F32), 0.0) for f, v in enumerate(values)]
        for a in range(5):
            band[2 * frames + a, r] = (field[a] + field[a + 1]).astype(BF)
    copies[1].wait()


def packed(width, span):
    return (width, span) == (24, 81)


def own_kernel(w_far, band, turned, part, w, xe, ps, sem):
    _, rows, cols, chan = band.shape
    frames = 2
    peers = turned.shape[0]
    width = chan // peers
    copies = start_copies([(w_far, w)], sem)
    none = jnp.zeros((cols, chan), BF)
    for f in range(2 * frames):
        slot = (f + frames) % (2 * frames) * 4
        xe[slot] = none
        xe[slot + 1 : slot + 3] = band[f]
        xe[slot + 3] = none
    ps[:, 0:EDGE, :] = jnp.zeros((10, EDGE, chan), F32)
    for a in range(5):
        for r in range(2):
            ps[a * 2 + r, EDGE : EDGE + cols, :] = band[4 + a, r].astype(F32)
    fields = [jnp.transpose(ps[2 * a : 2 * a + 2].reshape(2 * PITCH, chan)) for a in range(5)]
    for p in range(peers):
        mine = jnp.concatenate([v[p * width : (p + 1) * width] for v in fields], axis=0)
        turned[p] = mine.astype(BF)
    copies[0].wait()

    def patch(i, j):
        return blocks_of(xe, [(f + 2 - i) * 4 + j for f in range(2)], 2)

    part[...] = conv(patch, w, plain_dot, 1, cols)


def silu_kernel(turned, w, part, above, below, pay, own, sem):
    _, rows, cols, chan = above.shape
    frames = 2
    cells = frames * rows * cols
    half = cells // 2
    peers = pay.shape[0]
    copies = [pltpu.make_async_copy(turned, pay.at[:, cells + half :], sem.at[peers])]
    copies[0].start()

    def top_patch(i, j):
        frame = [above[(f + 2 - i + frames) % (2 * frames), 1] for f in range(2)]
        return jnp.concatenate(frame, axis=0)

    def bottom_patch(i, j):
        frame = [below[(f + 2 - i + frames) % (2 * frames), 0] for f in range(2)]
        return jnp.concatenate(frame, axis=0)

    top = conv(top_patch, w, plain_dot, 1, cols, (0,)).reshape(frames, 1, cols, chan)
    bottom = conv(bottom_patch, w, plain_dot, 1, cols, (2,)).reshape(frames, 1, cols, chan)
    hidden = part[...] + jnp.concatenate([top, bottom], axis=1).reshape(cells, chan)
    act = hidden / (1.0 + jnp.exp(-hidden))
    own[0:cells] = act[:, :128].astype(BF)
    own[cells:] = jnp.concatenate([act[:half, 128:], act[half:, 128:]], axis=1).astype(BF)
    for p in range(peers):
        copies.append(pltpu.make_async_copy(own, pay.at[p, 0 : cells + half], sem.at[p]))
        copies[-1].start()
    for copy in copies:
        copy.wait()


def hidden_grad_kernel(w1_far, w2_far, above, below, own, tall, xe, pe, w1, w2, sem):
    _, rows, cols, chan = own.shape
    frames = 2
    copies = start_copies([(w1_far, w1), (w2_far, w2)], sem)
    for f in range(2 * frames + 5):
        target, slot = (xe, (f + frames) % (2 * frames) * 6) if f < 4 else (pe, (f - 4) * 6)
        target[slot : slot + 2] = above[f]
        target[slot + 2 : slot + 4] = own[f]
        target[slot + 4 : slot + 6] = below[f]
    for copy in copies:
        copy.wait()

    def patch(i, j):
        return blocks_of(xe, [(f + 2 - i) * 6 + j for f in range(2)], 4)

    def pair_patch(i, j):
        return blocks_of(pe, [(2 * t + i) * 6 + 2 - j for t in range(2)], 4)

    hidden = conv(patch, w1, plain_dot, 1, cols)
    pair = conv(pair_patch, w2, transposed_dot, -1, cols)
    sigma = 1.0 / (1.0 + jnp.exp(-hidden))
    grad = pair * sigma * (1.0 + hidden * (1.0 - sigma))
    grad = grad.reshape(frames, rows + 2, cols, chan)
    band = lax.axis_index("row")
    none = jnp.zeros((frames, cols, chan), F32)
    tall[:, 0] = jnp.where(band > 0, grad[:, 0], none).astype(BF)
    tall[:, 1 : 1 + rows] = grad[:, 1 : 1 + rows].astype(BF)
    last = band == lax.axis_size("row") - 1
    tall[:, 1 + rows] = jnp.where(last, none, grad[:, 1 + rows]).astype(BF)


def second_kernel(span, got, out, field, left, prod):
    peers = got.shape[0]
    cells = field.shape[0] // peers // (4 * PITCH) * 192
    half = cells // 2
    chan = field.shape[1]
    width = chan // peers
    cols = 48
    blocks, _, lanes = out.shape
    field[...] = jnp.zeros(field.shape, BF)
    low_lane = lax.broadcasted_iota(jnp.int32, (width, 128), 1) < PITCH
    for q in range(peers):
        low = got[q, 0:cells, :]
        high = got[q, cells : cells + half, :].astype(F32)
        high = [high[:, 0:64].astype(BF), high[:, 64:128].astype(BF)]
        for t in range(2):
            for r in range(2):
                at = ((t * peers + q) * 2 + r) * PITCH + EDGE
                field[at : at + cols, 0:128] = low[(t * 2 + r) * cols : (t * 2 + r + 1) * cols]
                field[at : at + cols, 128:192] = high[t][r * cols : (r + 1) * cols]
    base = cells + half
    for a in range(5):
        plain = [
            got[q, base + a * width : base + (a + 1) * width, :].astype(F32) for q in range(peers)
        ]
        swapped = [pltpu.roll(v, PITCH, 1) for v in plain]
        zero = jnp.zeros((width, 128), F32)
        ring = [zero] + swapped + [zero]
        for q in range(peers):
            rows_of = [
                jnp.where(low_lane, ring[q + 1], ring[q + 2]),
                plain[q],
                jnp.where(low_lane, ring[q], ring[q + 1]),
            ]
            for j in range(3):
                for k in range(3):
                    value = rows_of[j]
                    if k != 1:
                        value = pltpu.roll(value, 127 if k == 0 else 1, 1)
                    for t in range(2):
                        i = a - 2 * t
                        if 0 <= i < 3:
                            tap = i * 9 + j * 3 + k
                            at = (t * peers + q) * 128
                            left[tap * width : (tap + 1) * width, at : at + 128] = value
    prod[:, 192:256] = jnp.zeros((prod.shape[0], 64), F32)
    for i in range(3):
        rows = slice(i * 9 * width, (i + 1) * 9 * width)
        prod[rows, 0:192] = jnp.dot(
            left[rows, :].astype(BF), field[...], preferred_element_type=F32
        )
    lane = lax.broadcasted_iota(jnp.int32, (width, 256), 1)
    for b in range(blocks):
        pieces = []
        done = 0
        while done < span:
            tap, start = divmod(b * span + done, chan)
            size = min(span - done, chan - start)
            pieces.append((tap, start, size, done))
            done += size
        for chunk in range(0, lanes, 128):
            value = None
            for tap, start, size, at in pieces:
                if at + size <= chunk or at >= chunk + 128:
                    continue
                shift = (at - chunk - start) % 256
                part = prod[tap * width : (tap + 1) * width, :]
                if shift:
                    part = pltpu.roll(part, shift, 1)
                part = part[:, :128]
                if value is None:
                    value = part
                else:
                    value = jnp.where(lane[:, :128] < at - chunk, value, part)
            if value is None:
                value = jnp.zeros((width, 128), F32)
            if packed(width, span):
                tail = value[16:24]
                tail = jnp.concatenate([pltpu.roll(tail, 81, 1), pltpu.roll(tail, 40, 1)], axis=0)
                value = jnp.where(lane[:16, :128] < span, value[:16], tail)
            out[b, :, chunk : chunk + 128] = value.astype(BF)


def clip_kernel(got, out):
    total = got[0].astype(F32)
    for p in range(1, got.shape[0]):
        total += got[p].astype(F32)
    out[...] = total.astype(BF)


def last_kernel(scale, got, out):
    width, span = out.shape
    total = got[0].astype(F32)
    for p in range(1, got.shape[0]):
        total += got[p].astype(F32)
    total = total * scale
    if packed(width, span):
        lane = lax.broadcasted_iota(jnp.int32, (8, 128), 1)
        tail = jnp.where(lane < 41, pltpu.roll(total[:8], 47, 1), pltpu.roll(total[8:], 88, 1))
        out[:16] = total[:, :span]
        out[16:] = tail[:, :span]
    else:
        out[...] = total[:, :span]


def grad_kernel(w1_far, tall, after, grad, w1, sem):
    copies = start_copies([(w1_far, w1)], sem)
    frames, rows, cols, chan = grad.shape
    fields = [tall[0], tall[1], after[0], after[1]]

    def patch(i, j):
        value = jnp.concatenate([fields[f + i][2 - j : 4 - j] for f in range(2)], axis=0)
        return value.reshape(-1, chan)

    copies[0].wait()
    grad[...] = conv(patch, w1, transposed_dot, -1, cols).reshape(grad.shape)


def call(body, name, limit, shapes, args, scratch, far=(), scalars=(), sems=0, out_far=False):
    spaces = [pltpu.SMEM] * len(scalars) + [pltpu.HBM] * len(far) + [pltpu.VMEM] * len(args)
    far = [pltpu.with_memory_space_constraint(value, pltpu.HBM) for value in far]
    made = pltpu.HBM if out_far else jax.ShapeDtypeStruct
    outs = [made(shape, kind) for shape, kind in shapes]
    buffers = [pltpu.VMEM(shape, kind) for shape, kind in scratch]
    if sems:
        buffers.append(pltpu.SemaphoreType.DMA((sems,)))
    return pl.pallas_call(
        body,
        name=name,
        out_shape=outs,
        in_specs=[pl.BlockSpec(memory_space=space) for space in spaces],
        out_specs=[pl.BlockSpec(memory_space=pltpu.HBM if out_far else pltpu.VMEM)] * len(outs),
        scratch_shapes=buffers,
        compiler_params=pltpu.CompilerParams(vmem_limit_bytes=limit * MIB),
    )(*scalars, *far, *args)


def local(clip_input, out_grad, weight_one, weight_two, lengths):
    frames, rows, cols, chan = clip_input.shape[1:]
    cells = frames * rows * cols
    peers = lax.axis_size("row")
    clips = lax.axis_size("clip")
    steps = lax.axis_size("tm")
    width = chan // peers
    x = clip_input[0]
    g = out_grad[0]
    w1 = weight_one.reshape(27, chan, chan)
    w2 = weight_two.reshape(27, chan, chan)

    xprev = move(x, ("tm",), (1,))
    gnext = move(g[:frames], ("tm",), (-1,))
    (band,) = call(
        band_kernel,
        "band",
        4,
        [((2 * frames + 5, rows, cols, chan), BF)],
        (xprev, gnext),
        [(g.shape, BF)],
        far=(x, g),
        scalars=(lengths,),
        sems=2,
    )
    above = move(band, ("row",), (1,))
    below = move(band, ("row",), (-1,))
    turned, own_part, w1_near = call(
        own_kernel,
        "own_rows",
        8,
        [((peers, 5 * width, 128), BF), ((cells, chan), F32), (w1.shape, BF)],
        (band,),
        [((16, cols, chan), BF), ((10, PITCH, chan), F32)],
        far=(w1,),
        sems=1,
    )
    (pay,) = call(
        silu_kernel,
        "hidden_and_act",
        4,
        [((peers, cells + cells // 2 + 5 * width, 128), BF)],
        (turned, w1_near, own_part, above, below),
        [((cells + cells // 2, 128), BF)],
        sems=peers + 1,
        out_far=True,
    )
    got = lax.all_to_all(pay, "row", 0, 0)
    (tall,) = call(
        hidden_grad_kernel,
        "hidden_grad",
        14,
        [((frames, rows + 2, cols, chan), BF)],
        (above, below, band),
        [
            ((24, cols, chan), BF),
            ((30, cols, chan), BF),
            (w1.shape, BF),
            (w2.shape, BF),
        ],
        far=(w1, w2),
        sems=2,
    )
    got, tall = lax.optimization_barrier((got, tall))

    blocks = clips * steps
    span = 27 * chan // blocks
    shape = (16, 128) if packed(width, span) else (width, (span + 127) // 128 * 128)
    (part,) = call(
        functools.partial(second_kernel, span),
        "kernel_grad_part",
        13,
        [((blocks,) + shape, BF)],
        (got,),
        [
            ((2 * peers * 2 * PITCH, chan), BF),
            ((27 * width, 2 * peers * 128), F32),
            ((27 * width, 256), F32),
        ],
    )
    by_clip = lax.all_to_all(part.reshape((clips, steps * shape[0], shape[1])), "clip", 0, 0)
    (summed,) = call(
        clip_kernel,
        "clip_sum",
        4,
        [((steps * shape[0], shape[1]), BF)],
        (by_clip,),
        [],
    )
    after = move(tall, ("tm",), (-1,))
    by_step = lax.all_to_all(summed.reshape((steps,) + shape), "tm", 0, 0)
    total = clips * 2 * frames * steps * rows * peers * cols
    (kernel_grad,) = call(
        functools.partial(last_kernel, 1.0 / math.sqrt(total)),
        "kernel_grad_sum",
        4,
        [((width, span), F32)],
        (by_step,),
        [],
    )
    (input_grad,) = call(
        grad_kernel,
        "input_grad",
        8,
        [((frames, rows, cols, chan), F32)],
        (tall, after),
        [(w1.shape, BF)],
        far=(w1,),
        sems=1,
    )
    return (input_grad[None], kernel_grad.T)


def solution(mesh):
    return jax.shard_map(
        local,
        mesh=mesh,
        in_specs=(
            P("clip", "tm", "row", None, None),
            P("clip", "tm", "row", None, None),
            P(),
            P(),
            P("clip"),
        ),
        out_specs=(P("clip", "tm", "row", None, None), P(("clip", "tm"), "row")),
        check_vma=False,
    )
```

```python
import functools
import math

import jax
import jax.numpy as jnp
from jax import lax
from jax.experimental import pallas as pl
from jax.experimental.pallas import tpu as pltpu
from jax.sharding import PartitionSpec as P

BF = jnp.bfloat16
F32 = jnp.float32
EDGE = 16
PITCH = 64
MIB = 1024 * 1024


def route(sizes, steps):
    total = math.prod(sizes)
    pairs = []
    for source in range(total):
        index, rest = [], source
        for size in reversed(sizes):
            index.append(rest % size)
            rest //= size
        index = index[::-1]
        there = [a + b for a, b in zip(index, steps)]
        if all(0 <= a < size for a, size in zip(there, sizes)):
            target = 0
            for a, size in zip(there, sizes):
                target = target * size + a
            pairs.append((source, target))
    return pairs


def move(value, axes, steps):
    sizes = [lax.axis_size(axis) for axis in axes]
    return lax.ppermute(value, axes if len(axes) > 1 else axes[0], route(sizes, steps))


def transposed_dot(a, b):
    return lax.dot_general(a, b, (((1,), (1,)), ((), ())), preferred_element_type=F32)


def plain_dot(a, b):
    return jnp.dot(a, b, preferred_element_type=F32)


def column_shift(value, by, cols):
    cells, chan = value.shape
    moved = pltpu.roll(value, by % cells, 0).reshape(cells // cols, cols, chan)
    column = lax.broadcasted_iota(jnp.int32, moved.shape, 1)
    moved = jnp.where(column == (0 if by > 0 else cols - 1), 0.0, moved)
    return moved.reshape(cells, chan)


def conv(patch, weight, dot, first_shift, cols, row_taps=(0, 1, 2)):
    total = None
    for k in (1, 0, 2):
        part = None
        for i in range(3):
            for j in row_taps:
                term = dot(patch(i, j), weight[i * 9 + j * 3 + k])
                part = term if part is None else part + term
        if k != 1:
            part = column_shift(part, first_shift if k == 0 else -first_shift, cols)
        total = part if total is None else total + part
    return total


def blocks_of(ref, starts, count):
    value = jnp.concatenate([ref[at : at + count] for at in starts], axis=0)
    return value.reshape(-1, value.shape[-1])


def start_copies(pairs, sem):
    copies = [pltpu.make_async_copy(a, b, sem.at[n]) for n, (a, b) in enumerate(pairs)]
    for copy in copies:
        copy.start()
    return copies


def band_kernel(lengths, x, g_far, xprev, gnext, band, top, bot, g, sem):
    frames = xprev.shape[0]
    copies = start_copies(((g_far, g), (x, band.at[0:frames])), sem)
    band[frames : 2 * frames] = xprev[...]
    limit = 2 * lengths[0] - 2 * frames * lax.axis_index("tm")
    copies[0].wait()
    for r in range(2):
        values = [g[f, r] for f in range(4)] + [gnext[f, r] for f in range(2)]
        field = [jnp.where(f < limit, v.astype(F32), 0.0) for f, v in enumerate(values)]
        for a in range(5):
            band[2 * frames + a, r] = (field[a] + field[a + 1]).astype(BF)
    copies[1].wait()
    top[...] = band[:, 0]
    bot[...] = band[:, 1]


def packed(width, span):
    return (width, span) == (24, 81)


def own_kernel(w_far, band, turned, part, w, xe, ps, sem):
    _, rows, cols, chan = band.shape
    frames = 2
    peers = turned.shape[0]
    width = chan // peers
    copies = start_copies([(w_far, w)], sem)
    none = jnp.zeros((cols, chan), BF)
    for f in range(2 * frames):
        slot = (f + frames) % (2 * frames) * 4
        xe[slot] = none
        xe[slot + 1 : slot + 3] = band[f]
        xe[slot + 3] = none
    ps[:, 0:EDGE, :] = jnp.zeros((10, EDGE, chan), F32)
    for a in range(5):
        for r in range(2):
            ps[a * 2 + r, EDGE : EDGE + cols, :] = band[4 + a, r].astype(F32)
    fields = [jnp.transpose(ps[2 * a : 2 * a + 2].reshape(2 * PITCH, chan)) for a in range(5)]
    for p in range(peers):
        mine = jnp.concatenate([v[p * width : (p + 1) * width] for v in fields], axis=0)
        turned[p] = mine.astype(BF)
    copies[0].wait()

    def patch(i, j):
        return blocks_of(xe, [(f + 2 - i) * 4 + j for f in range(2)], 2)

    part[...] = conv(patch, w, plain_dot, 1, cols)


def silu_kernel(turned, w, part, above, below, pay, own, sem):
    _, cols, chan = above.shape
    frames = 2
    cells = part.shape[0]
    half = cells // 2
    peers = pay.shape[0]
    copies = [pltpu.make_async_copy(turned, pay.at[:, cells + half :], sem.at[peers])]
    copies[0].start()

    def top_patch(i, j):
        frame = [above[(f + 2 - i + frames) % (2 * frames)] for f in range(2)]
        return jnp.concatenate(frame, axis=0)

    def bottom_patch(i, j):
        frame = [below[(f + 2 - i + frames) % (2 * frames)] for f in range(2)]
        return jnp.concatenate(frame, axis=0)

    top = conv(top_patch, w, plain_dot, 1, cols, (0,)).reshape(frames, 1, cols, chan)
    bottom = conv(bottom_patch, w, plain_dot, 1, cols, (2,)).reshape(frames, 1, cols, chan)
    hidden = part[...] + jnp.concatenate([top, bottom], axis=1).reshape(cells, chan)
    act = hidden / (1.0 + jnp.exp(-hidden))
    own[0:cells] = act[:, :128].astype(BF)
    own[cells:] = jnp.concatenate([act[:half, 128:], act[half:, 128:]], axis=1).astype(BF)
    for p in range(peers):
        copies.append(pltpu.make_async_copy(own, pay.at[p, 0 : cells + half], sem.at[p]))
        copies[-1].start()
    for copy in copies:
        copy.wait()


def hidden_grad_kernel(
    w1_far, w2_far, above, below, own, grad, top, bot, xe, pe, w1, w2, sem
):
    _, rows, cols, chan = own.shape
    frames = 2
    copies = start_copies([(w1_far, w1), (w2_far, w2)], sem)
    for f in range(2 * frames + 5):
        target, slot = (xe, (f + frames) % (2 * frames) * 4) if f < 4 else (pe, (f - 4) * 4)
        target[slot] = above[f]
        target[slot + 1 : slot + 3] = own[f]
        target[slot + 3] = below[f]
    for copy in copies:
        copy.wait()

    def patch(i, j):
        return blocks_of(xe, [(f + 2 - i) * 4 + j for f in range(2)], 2)

    def pair_patch(i, j):
        return blocks_of(pe, [(2 * t + i) * 4 + 2 - j for t in range(2)], 2)

    hidden = conv(patch, w1, plain_dot, 1, cols)
    pair = conv(pair_patch, w2, transposed_dot, -1, cols)
    sigma = 1.0 / (1.0 + jnp.exp(-hidden))
    value = (pair * sigma * (1.0 + hidden * (1.0 - sigma))).astype(BF)
    value = value.reshape(frames, rows, cols, chan)
    grad[...] = value
    top[...] = value[:, 0]
    bot[...] = value[:, 1]


def tall_kernel(grad, above, below, tall):
    tall[:, 0] = above[...]
    tall[:, 1:3] = grad[...]
    tall[:, 3] = below[...]


def second_kernel(span, got, out, field, left, prod):
    peers = got.shape[0]
    cells = field.shape[0] // peers // (4 * PITCH) * 192
    half = cells // 2
    chan = field.shape[1]
    width = chan // peers
    cols = 48
    blocks, _, lanes = out.shape
    field[...] = jnp.zeros(field.shape, BF)
    low_lane = lax.broadcasted_iota(jnp.int32, (width, 128), 1) < PITCH
    for q in range(peers):
        low = got[q, 0:cells, :]
        high = got[q, cells : cells + half, :].astype(F32)
        high = [high[:, 0:64].astype(BF), high[:, 64:128].astype(BF)]
        for t in range(2):
            for r in range(2):
                at = ((t * peers + q) * 2 + r) * PITCH + EDGE
                field[at : at + cols, 0:128] = low[(t * 2 + r) * cols : (t * 2 + r + 1) * cols]
                field[at : at + cols, 128:192] = high[t][r * cols : (r + 1) * cols]
    base = cells + half
    for a in range(5):
        plain = [
            got[q, base + a * width : base + (a + 1) * width, :].astype(F32) for q in range(peers)
        ]
        swapped = [pltpu.roll(v, PITCH, 1) for v in plain]
        zero = jnp.zeros((width, 128), F32)
        ring = [zero] + swapped + [zero]
        for q in range(peers):
            rows_of = [
                jnp.where(low_lane, ring[q + 1], ring[q + 2]),
                plain[q],
                jnp.where(low_lane, ring[q], ring[q + 1]),
            ]
            for j in range(3):
                for k in range(3):
                    value = rows_of[j]
                    if k != 1:
                        value = pltpu.roll(value, 127 if k == 0 else 1, 1)
                    for t in range(2):
                        i = a - 2 * t
                        if 0 <= i < 3:
                            tap = i * 9 + j * 3 + k
                            at = (t * peers + q) * 128
                            left[tap * width : (tap + 1) * width, at : at + 128] = value
    prod[:, 192:256] = jnp.zeros((prod.shape[0], 64), F32)
    for i in range(3):
        rows = slice(i * 9 * width, (i + 1) * 9 * width)
        prod[rows, 0:192] = jnp.dot(
            left[rows, :].astype(BF), field[...], preferred_element_type=F32
        )
    lane = lax.broadcasted_iota(jnp.int32, (width, 256), 1)
    for b in range(blocks):
        pieces = []
        done = 0
        while done < span:
            tap, start = divmod(b * span + done, chan)
            size = min(span - done, chan - start)
            pieces.append((tap, start, size, done))
            done += size
        for chunk in range(0, lanes, 128):
            value = None
            for tap, start, size, at in pieces:
                if at + size <= chunk or at >= chunk + 128:
                    continue
                shift = (at - chunk - start) % 256
                part = prod[tap * width : (tap + 1) * width, :]
                if shift:
                    part = pltpu.roll(part, shift, 1)
                part = part[:, :128]
                if value is None:
                    value = part
                else:
                    value = jnp.where(lane[:, :128] < at - chunk, value, part)
            if value is None:
                value = jnp.zeros((width, 128), F32)
            if packed(width, span):
                tail = value[16:24]
                tail = jnp.concatenate([pltpu.roll(tail, 81, 1), pltpu.roll(tail, 40, 1)], axis=0)
                value = jnp.where(lane[:16, :128] < span, value[:16], tail)
            out[b, :, chunk : chunk + 128] = value.astype(BF)


def clip_kernel(got, out):
    total = got[0].astype(F32)
    for p in range(1, got.shape[0]):
        total += got[p].astype(F32)
    out[...] = total.astype(BF)


def last_kernel(scale, got, out):
    width, span = out.shape
    total = got[0].astype(F32)
    for p in range(1, got.shape[0]):
        total += got[p].astype(F32)
    total = total * scale
    if packed(width, span):
        lane = lax.broadcasted_iota(jnp.int32, (8, 128), 1)
        tail = jnp.where(lane < 41, pltpu.roll(total[:8], 47, 1), pltpu.roll(total[8:], 88, 1))
        out[:16] = total[:, :span]
        out[16:] = tail[:, :span]
    else:
        out[...] = total[:, :span]


def grad_kernel(w1_far, tall, after, grad, w1, sem):
    copies = start_copies([(w1_far, w1)], sem)
    frames, rows, cols, chan = grad.shape
    fields = [tall[0], tall[1], after[0], after[1]]

    def patch(i, j):
        value = jnp.concatenate([fields[f + i][2 - j : 4 - j] for f in range(2)], axis=0)
        return value.reshape(-1, chan)

    copies[0].wait()
    grad[...] = conv(patch, w1, transposed_dot, -1, cols).reshape(grad.shape)


def call(body, name, limit, shapes, args, scratch, far=(), scalars=(), sems=0, out_far=False):
    spaces = [pltpu.SMEM] * len(scalars) + [pltpu.HBM] * len(far) + [pltpu.VMEM] * len(args)
    far = [pltpu.with_memory_space_constraint(value, pltpu.HBM) for value in far]
    made = pltpu.HBM if out_far else jax.ShapeDtypeStruct
    outs = [made(shape, kind) for shape, kind in shapes]
    buffers = [pltpu.VMEM(shape, kind) for shape, kind in scratch]
    if sems:
        buffers.append(pltpu.SemaphoreType.DMA((sems,)))
    return pl.pallas_call(
        body,
        name=name,
        out_shape=outs,
        in_specs=[pl.BlockSpec(memory_space=space) for space in spaces],
        out_specs=[pl.BlockSpec(memory_space=pltpu.HBM if out_far else pltpu.VMEM)] * len(outs),
        scratch_shapes=buffers,
        compiler_params=pltpu.CompilerParams(vmem_limit_bytes=limit * MIB),
    )(*scalars, *far, *args)


def local(clip_input, out_grad, weight_one, weight_two, lengths):
    frames, rows, cols, chan = clip_input.shape[1:]
    cells = frames * rows * cols
    peers = lax.axis_size("row")
    clips = lax.axis_size("clip")
    steps = lax.axis_size("tm")
    width = chan // peers
    x = clip_input[0]
    g = out_grad[0]
    w1 = weight_one.reshape(27, chan, chan)
    w2 = weight_two.reshape(27, chan, chan)

    xprev = move(x, ("tm",), (1,))
    gnext = move(g[:frames], ("tm",), (-1,))
    held = 2 * frames + 5
    band, top, bot = call(
        band_kernel,
        "band",
        4,
        [((held, rows, cols, chan), BF)] + [((held, cols, chan), BF)] * 2,
        (xprev, gnext),
        [(g.shape, BF)],
        far=(x, g),
        scalars=(lengths,),
        sems=2,
    )
    above = move(bot, ("row",), (1,))
    below = move(top, ("row",), (-1,))
    turned, own_part, w1_near = call(
        own_kernel,
        "own_rows",
        8,
        [((peers, 5 * width, 128), BF), ((cells, chan), F32), (w1.shape, BF)],
        (band,),
        [((16, cols, chan), BF), ((10, PITCH, chan), F32)],
        far=(w1,),
        sems=1,
    )
    (pay,) = call(
        silu_kernel,
        "hidden_and_act",
        4,
        [((peers, cells + cells // 2 + 5 * width, 128), BF)],
        (turned, w1_near, own_part, above, below),
        [((cells + cells // 2, 128), BF)],
        sems=peers + 1,
        out_far=True,
    )
    got = lax.all_to_all(pay, "row", 0, 0)
    edge = (frames, cols, chan)
    grad, grad_top, grad_bot = call(
        hidden_grad_kernel,
        "hidden_grad",
        14,
        [((frames, rows, cols, chan), BF), (edge, BF), (edge, BF)],
        (above, below, band),
        [
            ((16, cols, chan), BF),
            ((20, cols, chan), BF),
            (w1.shape, BF),
            (w2.shape, BF),
        ],
        far=(w1, w2),
        sems=2,
    )
    above_grad = move(grad_bot, ("row",), (1,))
    below_grad = move(grad_top, ("row",), (-1,))
    (tall,) = call(
        tall_kernel,
        "tall_band",
        4,
        [((frames, rows + 2, cols, chan), BF)],
        (grad, above_grad, below_grad),
        [],
    )
    got, tall = lax.optimization_barrier((got, tall))

    blocks = clips * steps
    span = 27 * chan // blocks
    shape = (16, 128) if packed(width, span) else (width, (span + 127) // 128 * 128)
    (part,) = call(
        functools.partial(second_kernel, span),
        "kernel_grad_part",
        13,
        [((blocks,) + shape, BF)],
        (got,),
        [
            ((2 * peers * 2 * PITCH, chan), BF),
            ((27 * width, 2 * peers * 128), F32),
            ((27 * width, 256), F32),
        ],
    )
    by_clip = lax.all_to_all(part.reshape((clips, steps * shape[0], shape[1])), "clip", 0, 0)
    (summed,) = call(
        clip_kernel,
        "clip_sum",
        4,
        [((steps * shape[0], shape[1]), BF)],
        (by_clip,),
        [],
    )
    after = move(tall, ("tm",), (-1,))
    by_step = lax.all_to_all(summed.reshape((steps,) + shape), "tm", 0, 0)
    total = clips * 2 * frames * steps * rows * peers * cols
    (kernel_grad,) = call(
        functools.partial(last_kernel, 1.0 / math.sqrt(total)),
        "kernel_grad_sum",
        4,
        [((width, span), F32)],
        (by_step,),
        [],
    )
    (input_grad,) = call(
        grad_kernel,
        "input_grad",
        8,
        [((frames, rows, cols, chan), F32)],
        (tall, after),
        [(w1.shape, BF)],
        far=(w1,),
        sems=1,
    )
    return (input_grad[None], kernel_grad.T)


def solution(mesh):
    return jax.shard_map(
        local,
        mesh=mesh,
        in_specs=(
            P("clip", "tm", "row", None, None),
            P("clip", "tm", "row", None, None),
            P(),
            P(),
            P("clip"),
        ),
        out_specs=(P("clip", "tm", "row", None, None), P(("clip", "tm"), "row")),
        check_vma=False,
    )
```

```python
import functools
import math

import jax
import jax.numpy as jnp
from jax import lax
from jax.experimental import pallas as pl
from jax.experimental.pallas import tpu as pltpu
from jax.sharding import PartitionSpec as P

BF = jnp.bfloat16
F32 = jnp.float32
EDGE = 16
PITCH = 64
MIB = 1024 * 1024


def route(sizes, steps):
    total = math.prod(sizes)
    pairs = []
    for source in range(total):
        index, rest = [], source
        for size in reversed(sizes):
            index.append(rest % size)
            rest //= size
        index = index[::-1]
        there = [a + b for a, b in zip(index, steps)]
        if all(0 <= a < size for a, size in zip(there, sizes)):
            target = 0
            for a, size in zip(there, sizes):
                target = target * size + a
            pairs.append((source, target))
    return pairs


def move(value, axes, steps):
    sizes = [lax.axis_size(axis) for axis in axes]
    return lax.ppermute(value, axes if len(axes) > 1 else axes[0], route(sizes, steps))


def transposed_dot(a, b):
    return lax.dot_general(a, b, (((1,), (1,)), ((), ())), preferred_element_type=F32)


def plain_dot(a, b):
    return jnp.dot(a, b, preferred_element_type=F32)


def column_shift(value, by, cols):
    cells, chan = value.shape
    moved = pltpu.roll(value, by % cells, 0).reshape(cells // cols, cols, chan)
    column = lax.broadcasted_iota(jnp.int32, moved.shape, 1)
    moved = jnp.where(column == (0 if by > 0 else cols - 1), 0.0, moved)
    return moved.reshape(cells, chan)


def conv(patch, weight, dot, first_shift, cols, row_taps=(0, 1, 2), frame_taps=(0, 1, 2)):
    total = None
    for k in (1, 0, 2):
        part = None
        for i in frame_taps:
            for j in row_taps:
                term = dot(patch(i, j), weight[i * 9 + j * 3 + k])
                part = term if part is None else part + term
        if k != 1:
            part = column_shift(part, first_shift if k == 0 else -first_shift, cols)
        total = part if total is None else total + part
    return total


def blocks_of(ref, starts, count):
    value = jnp.concatenate([ref[at : at + count] for at in starts], axis=0)
    return value.reshape(-1, value.shape[-1])


def start_copies(pairs, sem):
    copies = [pltpu.make_async_copy(a, b, sem.at[n]) for n, (a, b) in enumerate(pairs)]
    for copy in copies:
        copy.start()
    return copies


def band_kernel(lengths, x, g_far, xprev, gnext, band, top, bot, g, sem):
    frames = xprev.shape[0]
    copies = start_copies(((g_far, g), (x, band.at[0:frames])), sem)
    band[frames : 2 * frames] = xprev[...]
    limit = 2 * lengths[0] - 2 * frames * lax.axis_index("tm")
    copies[0].wait()
    for r in range(2):
        values = [g[f, r] for f in range(4)] + [gnext[f, r] for f in range(2)]
        field = [jnp.where(f < limit, v.astype(F32), 0.0) for f, v in enumerate(values)]
        for a in range(5):
            band[2 * frames + a, r] = (field[a] + field[a + 1]).astype(BF)
    copies[1].wait()
    top[...] = band[:, 0]
    bot[...] = band[:, 1]


def packed(width, span):
    return (width, span) == (24, 81)


def own_kernel(w_far, band, turned, part, w, xe, ps, sem):
    _, rows, cols, chan = band.shape
    frames = 2
    peers = turned.shape[0]
    width = chan // peers
    copies = start_copies([(w_far, w)], sem)
    none = jnp.zeros((cols, chan), BF)
    for f in range(2 * frames):
        slot = (f + frames) % (2 * frames) * 4
        xe[slot] = none
        xe[slot + 1 : slot + 3] = band[f]
        xe[slot + 3] = none
    ps[:, 0:EDGE, :] = jnp.zeros((10, EDGE, chan), F32)
    for a in range(5):
        for r in range(2):
            ps[a * 2 + r, EDGE : EDGE + cols, :] = band[4 + a, r].astype(F32)
    fields = [jnp.transpose(ps[2 * a : 2 * a + 2].reshape(2 * PITCH, chan)) for a in range(5)]
    for p in range(peers):
        mine = jnp.concatenate([v[p * width : (p + 1) * width] for v in fields], axis=0)
        turned[p] = mine.astype(BF)
    copies[0].wait()

    def patch(i, j):
        return blocks_of(xe, [(f + 2 - i) * 4 + j for f in range(2)], 2)

    part[...] = conv(patch, w, plain_dot, 1, cols)


def silu_kernel(turned, w, part, above, below, pay, own, sem):
    _, cols, chan = above.shape
    frames = 2
    cells = part.shape[0]
    half = cells // 2
    peers = pay.shape[0]
    copies = [pltpu.make_async_copy(turned, pay.at[:, cells + half :], sem.at[peers])]
    copies[0].start()

    def top_patch(i, j):
        frame = [above[(f + 2 - i + frames) % (2 * frames)] for f in range(2)]
        return jnp.concatenate(frame, axis=0)

    def bottom_patch(i, j):
        frame = [below[(f + 2 - i + frames) % (2 * frames)] for f in range(2)]
        return jnp.concatenate(frame, axis=0)

    top = conv(top_patch, w, plain_dot, 1, cols, (0,)).reshape(frames, 1, cols, chan)
    bottom = conv(bottom_patch, w, plain_dot, 1, cols, (2,)).reshape(frames, 1, cols, chan)
    hidden = part[...] + jnp.concatenate([top, bottom], axis=1).reshape(cells, chan)
    act = hidden / (1.0 + jnp.exp(-hidden))
    own[0:cells] = act[:, :128].astype(BF)
    own[cells:] = jnp.concatenate([act[:half, 128:], act[half:, 128:]], axis=1).astype(BF)
    for p in range(peers):
        copies.append(pltpu.make_async_copy(own, pay.at[p, 0 : cells + half], sem.at[p]))
        copies[-1].start()
    for copy in copies:
        copy.wait()


def hidden_grad_kernel(
    w1_far, w2_far, above, below, own, grad, top, bot, xe, pe, w1, w2, sem
):
    _, rows, cols, chan = own.shape
    frames = 2
    copies = start_copies([(w1_far, w1), (w2_far, w2)], sem)
    for f in range(2 * frames + 5):
        target, slot = (xe, (f + frames) % (2 * frames) * 4) if f < 4 else (pe, (f - 4) * 4)
        target[slot] = above[f]
        target[slot + 1 : slot + 3] = own[f]
        target[slot + 3] = below[f]
    for copy in copies:
        copy.wait()

    def patch(i, j):
        return blocks_of(xe, [(f + 2 - i) * 4 + j for f in range(2)], 2)

    def pair_patch(i, j):
        return blocks_of(pe, [(2 * t + i) * 4 + 2 - j for t in range(2)], 2)

    hidden = conv(patch, w1, plain_dot, 1, cols)
    pair = conv(pair_patch, w2, transposed_dot, -1, cols)
    sigma = 1.0 / (1.0 + jnp.exp(-hidden))
    value = (pair * sigma * (1.0 + hidden * (1.0 - sigma))).astype(BF)
    value = value.reshape(frames, rows, cols, chan)
    grad[...] = value
    top[...] = value[:, 0]
    bot[...] = value[:, 1]


def tall_kernel(grad, above, below, tall):
    tall[:, 0] = above[...]
    tall[:, 1:3] = grad[...]
    tall[:, 3] = below[...]


def second_kernel(span, got, out, field, left, prod):
    peers = got.shape[0]
    cells = field.shape[0] // peers // (4 * PITCH) * 192
    half = cells // 2
    chan = field.shape[1]
    width = chan // peers
    cols = 48
    blocks, _, lanes = out.shape
    field[...] = jnp.zeros(field.shape, BF)
    low_lane = lax.broadcasted_iota(jnp.int32, (width, 128), 1) < PITCH
    for q in range(peers):
        low = got[q, 0:cells, :]
        high = got[q, cells : cells + half, :].astype(F32)
        high = [high[:, 0:64].astype(BF), high[:, 64:128].astype(BF)]
        for t in range(2):
            for r in range(2):
                at = ((t * peers + q) * 2 + r) * PITCH + EDGE
                field[at : at + cols, 0:128] = low[(t * 2 + r) * cols : (t * 2 + r + 1) * cols]
                field[at : at + cols, 128:192] = high[t][r * cols : (r + 1) * cols]
    base = cells + half
    for a in range(5):
        plain = [
            got[q, base + a * width : base + (a + 1) * width, :].astype(F32) for q in range(peers)
        ]
        swapped = [pltpu.roll(v, PITCH, 1) for v in plain]
        zero = jnp.zeros((width, 128), F32)
        ring = [zero] + swapped + [zero]
        for q in range(peers):
            rows_of = [
                jnp.where(low_lane, ring[q + 1], ring[q + 2]),
                plain[q],
                jnp.where(low_lane, ring[q], ring[q + 1]),
            ]
            for j in range(3):
                for k in range(3):
                    value = rows_of[j]
                    if k != 1:
                        value = pltpu.roll(value, 127 if k == 0 else 1, 1)
                    for t in range(2):
                        i = a - 2 * t
                        if 0 <= i < 3:
                            tap = i * 9 + j * 3 + k
                            at = (t * peers + q) * 128
                            left[tap * width : (tap + 1) * width, at : at + 128] = value
    prod[:, 192:256] = jnp.zeros((prod.shape[0], 64), F32)
    for i in range(3):
        rows = slice(i * 9 * width, (i + 1) * 9 * width)
        prod[rows, 0:192] = jnp.dot(
            left[rows, :].astype(BF), field[...], preferred_element_type=F32
        )
    lane = lax.broadcasted_iota(jnp.int32, (width, 256), 1)
    for b in range(blocks):
        pieces = []
        done = 0
        while done < span:
            tap, start = divmod(b * span + done, chan)
            size = min(span - done, chan - start)
            pieces.append((tap, start, size, done))
            done += size
        for chunk in range(0, lanes, 128):
            value = None
            for tap, start, size, at in pieces:
                if at + size <= chunk or at >= chunk + 128:
                    continue
                shift = (at - chunk - start) % 256
                part = prod[tap * width : (tap + 1) * width, :]
                if shift:
                    part = pltpu.roll(part, shift, 1)
                part = part[:, :128]
                if value is None:
                    value = part
                else:
                    value = jnp.where(lane[:, :128] < at - chunk, value, part)
            if value is None:
                value = jnp.zeros((width, 128), F32)
            if packed(width, span):
                tail = value[16:24]
                tail = jnp.concatenate([pltpu.roll(tail, 81, 1), pltpu.roll(tail, 40, 1)], axis=0)
                value = jnp.where(lane[:16, :128] < span, value[:16], tail)
            out[b, :, chunk : chunk + 128] = value.astype(BF)


def clip_kernel(got, out):
    total = got[0].astype(F32)
    for p in range(1, got.shape[0]):
        total += got[p].astype(F32)
    out[...] = total.astype(BF)


def last_kernel(scale, got, out):
    width, span = out.shape
    total = got[0].astype(F32)
    for p in range(1, got.shape[0]):
        total += got[p].astype(F32)
    total = total * scale
    if packed(width, span):
        lane = lax.broadcasted_iota(jnp.int32, (8, 128), 1)
        tail = jnp.where(lane < 41, pltpu.roll(total[:8], 47, 1), pltpu.roll(total[8:], 88, 1))
        out[:16] = total[:, :span]
        out[16:] = tail[:, :span]
    else:
        out[...] = total[:, :span]


def frame_conv(frames, weight, tap):
    _, cols, chan = frames[0].shape

    def patch(i, j):
        return jnp.concatenate([f[2 - j : 4 - j] for f in frames], axis=0).reshape(-1, chan)

    return conv(patch, weight, transposed_dot, -1, cols, frame_taps=(tap,))


def own_grad_kernel(w_far, tall, part, w, sem):
    copies = start_copies([(w_far, w)], sem)
    half = part.shape[0] // 2
    copies[0].wait()
    both = frame_conv([tall[0], tall[1]], w, 0)
    part[0:half] = both[0:half] + frame_conv([tall[1]], w, 1)
    part[half:] = both[half:]


def grad_kernel(w, part, after, grad):
    half = part.shape[0] // 2
    shape = grad.shape[1:]
    both = part[...] + frame_conv([after[0], after[1]], w, 2)
    grad[0] = both[0:half].reshape(shape)
    grad[1] = (both[half:] + frame_conv([after[0]], w, 1)).reshape(shape)


def call(body, name, limit, shapes, args, scratch, far=(), scalars=(), sems=0, out_far=False):
    spaces = [pltpu.SMEM] * len(scalars) + [pltpu.HBM] * len(far) + [pltpu.VMEM] * len(args)
    far = [pltpu.with_memory_space_constraint(value, pltpu.HBM) for value in far]
    made = pltpu.HBM if out_far else jax.ShapeDtypeStruct
    outs = [made(shape, kind) for shape, kind in shapes]
    buffers = [pltpu.VMEM(shape, kind) for shape, kind in scratch]
    if sems:
        buffers.append(pltpu.SemaphoreType.DMA((sems,)))
    return pl.pallas_call(
        body,
        name=name,
        out_shape=outs,
        in_specs=[pl.BlockSpec(memory_space=space) for space in spaces],
        out_specs=[pl.BlockSpec(memory_space=pltpu.HBM if out_far else pltpu.VMEM)] * len(outs),
        scratch_shapes=buffers,
        compiler_params=pltpu.CompilerParams(vmem_limit_bytes=limit * MIB),
    )(*scalars, *far, *args)


def local(clip_input, out_grad, weight_one, weight_two, lengths):
    frames, rows, cols, chan = clip_input.shape[1:]
    cells = frames * rows * cols
    peers = lax.axis_size("row")
    clips = lax.axis_size("clip")
    steps = lax.axis_size("tm")
    width = chan // peers
    x = clip_input[0]
    g = out_grad[0]
    w1 = weight_one.reshape(27, chan, chan)
    w2 = weight_two.reshape(27, chan, chan)

    xprev = move(x, ("tm",), (1,))
    gnext = move(g[:frames], ("tm",), (-1,))
    held = 2 * frames + 5
    band, top, bot = call(
        band_kernel,
        "band",
        4,
        [((held, rows, cols, chan), BF)] + [((held, cols, chan), BF)] * 2,
        (xprev, gnext),
        [(g.shape, BF)],
        far=(x, g),
        scalars=(lengths,),
        sems=2,
    )
    above = move(bot, ("row",), (1,))
    below = move(top, ("row",), (-1,))
    turned, own_part, w1_near = call(
        own_kernel,
        "own_rows",
        8,
        [((peers, 5 * width, 128), BF), ((cells, chan), F32), (w1.shape, BF)],
        (band,),
        [((16, cols, chan), BF), ((10, PITCH, chan), F32)],
        far=(w1,),
        sems=1,
    )
    (pay,) = call(
        silu_kernel,
        "hidden_and_act",
        4,
        [((peers, cells + cells // 2 + 5 * width, 128), BF)],
        (turned, w1_near, own_part, above, below),
        [((cells + cells // 2, 128), BF)],
        sems=peers + 1,
        out_far=True,
    )
    got = lax.all_to_all(pay, "row", 0, 0)
    edge = (frames, cols, chan)
    grad, grad_top, grad_bot = call(
        hidden_grad_kernel,
        "hidden_grad",
        14,
        [((frames, rows, cols, chan), BF), (edge, BF), (edge, BF)],
        (above, below, band),
        [
            ((16, cols, chan), BF),
            ((20, cols, chan), BF),
            (w1.shape, BF),
            (w2.shape, BF),
        ],
        far=(w1, w2),
        sems=2,
    )
    above_grad = move(grad_bot, ("row",), (1,))
    below_grad = move(grad_top, ("row",), (-1,))
    (tall,) = call(
        tall_kernel,
        "tall_band",
        4,
        [((frames, rows + 2, cols, chan), BF)],
        (grad, above_grad, below_grad),
        [],
    )
    got, tall = lax.optimization_barrier((got, tall))

    blocks = clips * steps
    span = 27 * chan // blocks
    shape = (16, 128) if packed(width, span) else (width, (span + 127) // 128 * 128)
    (part,) = call(
        functools.partial(second_kernel, span),
        "kernel_grad_part",
        13,
        [((blocks,) + shape, BF)],
        (got,),
        [
            ((2 * peers * 2 * PITCH, chan), BF),
            ((27 * width, 2 * peers * 128), F32),
            ((27 * width, 256), F32),
        ],
    )
    by_clip = lax.all_to_all(part.reshape((clips, steps * shape[0], shape[1])), "clip", 0, 0)
    (summed,) = call(
        clip_kernel,
        "clip_sum",
        4,
        [((steps * shape[0], shape[1]), BF)],
        (by_clip,),
        [],
    )
    after = move(tall, ("tm",), (-1,))
    by_step = lax.all_to_all(summed.reshape((steps,) + shape), "tm", 0, 0)
    total = clips * 2 * frames * steps * rows * peers * cols
    (kernel_grad,) = call(
        functools.partial(last_kernel, 1.0 / math.sqrt(total)),
        "kernel_grad_sum",
        4,
        [((width, span), F32)],
        (by_step,),
        [],
    )
    grad_part, w1_again = call(
        own_grad_kernel,
        "own_input_grad",
        5,
        [((cells, chan), F32), (w1.shape, BF)],
        (tall,),
        [],
        far=(w1,),
        sems=1,
    )
    (input_grad,) = call(
        grad_kernel,
        "input_grad",
        5,
        [((frames, rows, cols, chan), F32)],
        (w1_again, grad_part, after),
        [],
    )
    return (input_grad[None], kernel_grad.T)


def solution(mesh):
    return jax.shard_map(
        local,
        mesh=mesh,
        in_specs=(
            P("clip", "tm", "row", None, None),
            P("clip", "tm", "row", None, None),
            P(),
            P(),
            P("clip"),
        ),
        out_specs=(P("clip", "tm", "row", None, None), P(("clip", "tm"), "row")),
        check_vma=False,
    )
```

```python
import functools
import math

import jax
import jax.numpy as jnp
from jax import lax
from jax.experimental import pallas as pl
from jax.experimental.pallas import tpu as pltpu
from jax.sharding import PartitionSpec as P

BF = jnp.bfloat16
F32 = jnp.float32
EDGE = 16
PITCH = 64
MIB = 1024 * 1024


def route(sizes, steps):
    total = math.prod(sizes)
    pairs = []
    for source in range(total):
        index, rest = [], source
        for size in reversed(sizes):
            index.append(rest % size)
            rest //= size
        index = index[::-1]
        there = [a + b for a, b in zip(index, steps)]
        if all(0 <= a < size for a, size in zip(there, sizes)):
            target = 0
            for a, size in zip(there, sizes):
                target = target * size + a
            pairs.append((source, target))
    return pairs


def move(value, axes, steps):
    sizes = [lax.axis_size(axis) for axis in axes]
    return lax.ppermute(value, axes if len(axes) > 1 else axes[0], route(sizes, steps))


def transposed_dot(a, b):
    return lax.dot_general(a, b, (((1,), (1,)), ((), ())), preferred_element_type=F32)


def plain_dot(a, b):
    return jnp.dot(a, b, preferred_element_type=F32)


def column_shift(value, by, cols):
    cells, chan = value.shape
    moved = pltpu.roll(value, by % cells, 0).reshape(cells // cols, cols, chan)
    column = lax.broadcasted_iota(jnp.int32, moved.shape, 1)
    moved = jnp.where(column == (0 if by > 0 else cols - 1), 0.0, moved)
    return moved.reshape(cells, chan)


def conv(patch, weight, dot, first_shift, cols, row_taps=(0, 1, 2), frame_taps=(0, 1, 2)):
    total = None
    for k in (1, 0, 2):
        part = None
        for i in frame_taps:
            for j in row_taps:
                term = dot(patch(i, j), weight[i * 9 + j * 3 + k])
                part = term if part is None else part + term
        if k != 1:
            part = column_shift(part, first_shift if k == 0 else -first_shift, cols)
        total = part if total is None else total + part
    return total


def blocks_of(ref, starts, count):
    value = jnp.concatenate([ref[at : at + count] for at in starts], axis=0)
    return value.reshape(-1, value.shape[-1])


def start_copies(pairs, sem):
    copies = [pltpu.make_async_copy(a, b, sem.at[n]) for n, (a, b) in enumerate(pairs)]
    for copy in copies:
        copy.start()
    return copies


def band_kernel(lengths, x, g_far, xprev, gnext, band, top, bot, g, sem):
    frames = xprev.shape[0]
    copies = start_copies(((g_far, g), (x, band.at[0:frames])), sem)
    band[frames : 2 * frames] = xprev[...]
    limit = 2 * lengths[0] - 2 * frames * lax.axis_index("tm")
    copies[0].wait()
    for r in range(2):
        values = [g[f, r] for f in range(4)] + [gnext[f, r] for f in range(2)]
        field = [jnp.where(f < limit, v.astype(F32), 0.0) for f, v in enumerate(values)]
        for a in range(5):
            band[2 * frames + a, r] = (field[a] + field[a + 1]).astype(BF)
    copies[1].wait()
    top[...] = band[:, 0]
    bot[...] = band[:, 1]


def packed(width, span):
    return (width, span) == (24, 81)


def own_kernel(w_far, band, turned, part, w, xe, ps, sem):
    _, rows, cols, chan = band.shape
    frames = 2
    peers = turned.shape[0]
    width = chan // peers
    copies = start_copies([(w_far, w)], sem)
    none = jnp.zeros((cols, chan), BF)
    for f in range(2 * frames):
        slot = (f + frames) % (2 * frames) * 4
        xe[slot] = none
        xe[slot + 1 : slot + 3] = band[f]
        xe[slot + 3] = none
    ps[:, 0:EDGE, :] = jnp.zeros((10, EDGE, chan), F32)
    for a in range(5):
        for r in range(2):
            ps[a * 2 + r, EDGE : EDGE + cols, :] = band[4 + a, r].astype(F32)
    fields = [jnp.transpose(ps[2 * a : 2 * a + 2].reshape(2 * PITCH, chan)) for a in range(5)]
    for p in range(peers):
        mine = jnp.concatenate([v[p * width : (p + 1) * width] for v in fields], axis=0)
        turned[p] = mine.astype(BF)
    copies[0].wait()

    def patch(i, j):
        return blocks_of(xe, [(f + 2 - i) * 4 + j for f in range(2)], 2)

    part[...] = conv(patch, w, plain_dot, 1, cols)


def silu_kernel(turned, w, part, above, below, pay, own, sem):
    _, cols, chan = above.shape
    frames = 2
    cells = part.shape[0]
    half = cells // 2
    peers = pay.shape[0]
    copies = [pltpu.make_async_copy(turned, pay.at[:, cells + half :], sem.at[peers])]
    copies[0].start()

    def top_patch(i, j):
        frame = [above[(f + 2 - i + frames) % (2 * frames)] for f in range(2)]
        return jnp.concatenate(frame, axis=0)

    def bottom_patch(i, j):
        frame = [below[(f + 2 - i + frames) % (2 * frames)] for f in range(2)]
        return jnp.concatenate(frame, axis=0)

    top = conv(top_patch, w, plain_dot, 1, cols, (0,)).reshape(frames, 1, cols, chan)
    bottom = conv(bottom_patch, w, plain_dot, 1, cols, (2,)).reshape(frames, 1, cols, chan)
    hidden = part[...] + jnp.concatenate([top, bottom], axis=1).reshape(cells, chan)
    act = hidden / (1.0 + jnp.exp(-hidden))
    own[0:cells] = act[:, :128].astype(BF)
    own[cells:] = jnp.concatenate([act[:half, 128:], act[half:, 128:]], axis=1).astype(BF)
    for p in range(peers):
        copies.append(pltpu.make_async_copy(own, pay.at[p, 0 : cells + half], sem.at[p]))
        copies[-1].start()
    for copy in copies:
        copy.wait()


def hidden_grad_kernel(
    w1_far, w2_far, above, below, own, grad, top, bot, xe, pe, w1, w2, sem
):
    _, rows, cols, chan = own.shape
    frames = 2
    copies = start_copies([(w1_far, w1), (w2_far, w2)], sem)
    for f in range(2 * frames + 5):
        target, slot = (xe, (f + frames) % (2 * frames) * 4) if f < 4 else (pe, (f - 4) * 4)
        target[slot] = above[f]
        target[slot + 1 : slot + 3] = own[f]
        target[slot + 3] = below[f]
    for copy in copies:
        copy.wait()

    def patch(i, j):
        return blocks_of(xe, [(f + 2 - i) * 4 + j for f in range(2)], 2)

    def pair_patch(i, j):
        return blocks_of(pe, [(2 * t + i) * 4 + 2 - j for t in range(2)], 2)

    hidden = conv(patch, w1, plain_dot, 1, cols)
    pair = conv(pair_patch, w2, transposed_dot, -1, cols)
    sigma = 1.0 / (1.0 + jnp.exp(-hidden))
    value = (pair * sigma * (1.0 + hidden * (1.0 - sigma))).astype(BF)
    value = value.reshape(frames, rows, cols, chan)
    grad[...] = value
    top[...] = value[:, 0]
    bot[...] = value[:, 1]


def tall_kernel(grad, above, below, tall):
    tall[:, 0] = above[...]
    tall[:, 1:3] = grad[...]
    tall[:, 3] = below[...]


def second_kernel(span, got, out, field, left, prod):
    peers = got.shape[0]
    cells = field.shape[0] // peers // (4 * PITCH) * 192
    half = cells // 2
    chan = field.shape[1]
    width = chan // peers
    cols = 48
    blocks, _, lanes = out.shape
    field[...] = jnp.zeros(field.shape, BF)
    low_lane = lax.broadcasted_iota(jnp.int32, (width, 128), 1) < PITCH
    for q in range(peers):
        low = got[q, 0:cells, :]
        high = got[q, cells : cells + half, :].astype(F32)
        high = [high[:, 0:64].astype(BF), high[:, 64:128].astype(BF)]
        for t in range(2):
            for r in range(2):
                at = ((t * peers + q) * 2 + r) * PITCH + EDGE
                field[at : at + cols, 0:128] = low[(t * 2 + r) * cols : (t * 2 + r + 1) * cols]
                field[at : at + cols, 128:192] = high[t][r * cols : (r + 1) * cols]
    base = cells + half
    for a in range(5):
        plain = [
            got[q, base + a * width : base + (a + 1) * width, :].astype(F32) for q in range(peers)
        ]
        swapped = [pltpu.roll(v, PITCH, 1) for v in plain]
        zero = jnp.zeros((width, 128), F32)
        ring = [zero] + swapped + [zero]
        for q in range(peers):
            rows_of = [
                jnp.where(low_lane, ring[q + 1], ring[q + 2]),
                plain[q],
                jnp.where(low_lane, ring[q], ring[q + 1]),
            ]
            for j in range(3):
                for k in range(3):
                    value = rows_of[j]
                    if k != 1:
                        value = pltpu.roll(value, 127 if k == 0 else 1, 1)
                    for t in range(2):
                        i = a - 2 * t
                        if 0 <= i < 3:
                            tap = i * 9 + j * 3 + k
                            at = (t * peers + q) * 128
                            left[tap * width : (tap + 1) * width, at : at + 128] = value
    prod[:, 192:256] = jnp.zeros((prod.shape[0], 64), F32)
    for i in range(3):
        rows = slice(i * 9 * width, (i + 1) * 9 * width)
        prod[rows, 0:192] = jnp.dot(
            left[rows, :].astype(BF), field[...], preferred_element_type=F32
        )
    lane = lax.broadcasted_iota(jnp.int32, (width, 256), 1)
    for b in range(blocks):
        pieces = []
        done = 0
        while done < span:
            tap, start = divmod(b * span + done, chan)
            size = min(span - done, chan - start)
            pieces.append((tap, start, size, done))
            done += size
        for chunk in range(0, lanes, 128):
            value = None
            for tap, start, size, at in pieces:
                if at + size <= chunk or at >= chunk + 128:
                    continue
                shift = (at - chunk - start) % 256
                part = prod[tap * width : (tap + 1) * width, :]
                if shift:
                    part = pltpu.roll(part, shift, 1)
                part = part[:, :128]
                if value is None:
                    value = part
                else:
                    value = jnp.where(lane[:, :128] < at - chunk, value, part)
            if value is None:
                value = jnp.zeros((width, 128), F32)
            if packed(width, span):
                tail = value[16:24]
                tail = jnp.concatenate([pltpu.roll(tail, 81, 1), pltpu.roll(tail, 40, 1)], axis=0)
                value = jnp.where(lane[:16, :128] < span, value[:16], tail)
            out[b, :, chunk : chunk + 128] = value.astype(BF)


def clip_kernel(got, out):
    total = got[0].astype(F32)
    for p in range(1, got.shape[0]):
        total += got[p].astype(F32)
    out[...] = total.astype(BF)


def last_kernel(scale, got, out):
    width, span = out.shape
    total = got[0].astype(F32)
    for p in range(1, got.shape[0]):
        total += got[p].astype(F32)
    total = total * scale
    if packed(width, span):
        lane = lax.broadcasted_iota(jnp.int32, (8, 128), 1)
        tail = jnp.where(lane < 41, pltpu.roll(total[:8], 47, 1), pltpu.roll(total[8:], 88, 1))
        out[:16] = total[:, :span]
        out[16:] = tail[:, :span]
    else:
        out[...] = total[:, :span]


def frame_conv(frames, weight, tap):
    _, cols, chan = frames[0].shape

    def patch(i, j):
        return jnp.concatenate([f[2 - j : 4 - j] for f in frames], axis=0).reshape(-1, chan)

    return conv(patch, weight, transposed_dot, -1, cols, frame_taps=(tap,))


def own_grad_kernel(w_far, tall, part, w, sem):
    copies = start_copies([(w_far, w)], sem)
    half = part.shape[0] // 2
    copies[0].wait()
    both = frame_conv([tall[0], tall[1]], w, 0)
    part[0:half] = both[0:half] + frame_conv([tall[1]], w, 1)
    part[half:] = both[half:]


def grad_kernel(w, part, after, grad):
    half = part.shape[0] // 2
    shape = grad.shape[1:]
    both = part[...] + frame_conv([after[0], after[1]], w, 2)
    grad[0] = both[0:half].reshape(shape)
    grad[1] = (both[half:] + frame_conv([after[0]], w, 1)).reshape(shape)


def call(body, name, limit, shapes, args, scratch, far=(), scalars=(), sems=0, out_far=False):
    spaces = [pltpu.SMEM] * len(scalars) + [pltpu.HBM] * len(far) + [pltpu.VMEM] * len(args)
    far = [pltpu.with_memory_space_constraint(value, pltpu.HBM) for value in far]
    made = pltpu.HBM if out_far else jax.ShapeDtypeStruct
    outs = [made(shape, kind) for shape, kind in shapes]
    buffers = [pltpu.VMEM(shape, kind) for shape, kind in scratch]
    if sems:
        buffers.append(pltpu.SemaphoreType.DMA((sems,)))
    return pl.pallas_call(
        body,
        name=name,
        out_shape=outs,
        in_specs=[pl.BlockSpec(memory_space=space) for space in spaces],
        out_specs=[pl.BlockSpec(memory_space=pltpu.HBM if out_far else pltpu.VMEM)] * len(outs),
        scratch_shapes=buffers,
        compiler_params=pltpu.CompilerParams(vmem_limit_bytes=limit * MIB),
    )(*scalars, *far, *args)


def local(clip_input, out_grad, weight_one, weight_two, lengths):
    frames, rows, cols, chan = clip_input.shape[1:]
    cells = frames * rows * cols
    peers = lax.axis_size("row")
    clips = lax.axis_size("clip")
    steps = lax.axis_size("tm")
    width = chan // peers
    x = clip_input[0]
    g = out_grad[0]
    w1 = weight_one.reshape(27, chan, chan)
    w2 = weight_two.reshape(27, chan, chan)

    xprev = move(x, ("tm",), (1,))
    gnext = move(g[:frames], ("tm",), (-1,))
    held = 2 * frames + 5
    band, top, bot = call(
        band_kernel,
        "band",
        4,
        [((held, rows, cols, chan), BF)] + [((held, cols, chan), BF)] * 2,
        (xprev, gnext),
        [(g.shape, BF)],
        far=(x, g),
        scalars=(lengths,),
        sems=2,
    )
    above = move(bot, ("row",), (1,))
    below = move(top, ("row",), (-1,))
    turned, own_part, w1_near = call(
        own_kernel,
        "own_rows",
        8,
        [((peers, 5 * width, 128), BF), ((cells, chan), F32), (w1.shape, BF)],
        (band,),
        [((16, cols, chan), BF), ((10, PITCH, chan), F32)],
        far=(w1,),
        sems=1,
    )
    (pay,) = call(
        silu_kernel,
        "hidden_and_act",
        4,
        [((peers, cells + cells // 2 + 5 * width, 128), BF)],
        (turned, w1_near, own_part, above, below),
        [((cells + cells // 2, 128), BF)],
        sems=peers + 1,
        out_far=True,
    )
    got = lax.all_to_all(pay, "row", 0, 0)
    edge = (frames, cols, chan)
    grad, grad_top, grad_bot = call(
        hidden_grad_kernel,
        "hidden_grad",
        14,
        [((frames, rows, cols, chan), BF), (edge, BF), (edge, BF)],
        (above, below, band),
        [
            ((16, cols, chan), BF),
            ((20, cols, chan), BF),
            (w1.shape, BF),
            (w2.shape, BF),
        ],
        far=(w1, w2),
        sems=2,
    )
    above_grad = move(grad_bot, ("row",), (1,))
    below_grad = move(grad_top, ("row",), (-1,))
    blocks = clips * steps
    span = 27 * chan // blocks
    shape = (16, 128) if packed(width, span) else (width, (span + 127) // 128 * 128)
    (part,) = call(
        functools.partial(second_kernel, span),
        "kernel_grad_part",
        13,
        [((blocks,) + shape, BF)],
        (got,),
        [
            ((2 * peers * 2 * PITCH, chan), BF),
            ((27 * width, 2 * peers * 128), F32),
            ((27 * width, 256), F32),
        ],
    )
    part, above_grad, below_grad = lax.optimization_barrier((part, above_grad, below_grad))
    (tall,) = call(
        tall_kernel,
        "tall_band",
        4,
        [((frames, rows + 2, cols, chan), BF)],
        (grad, above_grad, below_grad),
        [],
    )
    by_clip = lax.all_to_all(part.reshape((clips, steps * shape[0], shape[1])), "clip", 0, 0)
    (summed,) = call(
        clip_kernel,
        "clip_sum",
        4,
        [((steps * shape[0], shape[1]), BF)],
        (by_clip,),
        [],
    )
    after = move(tall, ("tm",), (-1,))
    by_step = lax.all_to_all(summed.reshape((steps,) + shape), "tm", 0, 0)
    total = clips * 2 * frames * steps * rows * peers * cols
    (kernel_grad,) = call(
        functools.partial(last_kernel, 1.0 / math.sqrt(total)),
        "kernel_grad_sum",
        4,
        [((width, span), F32)],
        (by_step,),
        [],
    )
    grad_part, w1_again = call(
        own_grad_kernel,
        "own_input_grad",
        5,
        [((cells, chan), F32), (w1.shape, BF)],
        (tall,),
        [],
        far=(w1,),
        sems=1,
    )
    (input_grad,) = call(
        grad_kernel,
        "input_grad",
        5,
        [((frames, rows, cols, chan), F32)],
        (w1_again, grad_part, after),
        [],
    )
    return (input_grad[None], kernel_grad.T)


def solution(mesh):
    return jax.shard_map(
        local,
        mesh=mesh,
        in_specs=(
            P("clip", "tm", "row", None, None),
            P("clip", "tm", "row", None, None),
            P(),
            P(),
            P("clip"),
        ),
        out_specs=(P("clip", "tm", "row", None, None), P(("clip", "tm"), "row")),
        check_vma=False,
    )
```
